128 devices in a mesh: blk: 16 (over x_lo, z, core), rep: 8 (over x_hi, y).
Axes of the slice: x: 4 (x_hi: 2, x_lo: 2; x = x_hi * 2 + x_lo), y: 4, z: 4, core: 2. Of those that a mesh axis runs over, the one named last changes fastest.
Arguments:
- features: bfloat16 [32768, 512], P(('blk', 'rep')), may hold values from -6 to 6
- weight: bfloat16 [512, 512], replicated, may hold values from -0.25 to 0.25
- layer_bias: float32 [512], replicated, may hold values from -4 to 4
- tile_values: bfloat16 [16, 8, 32, 8, 128, 128], P('blk', 'rep'), may hold values from -0.21875 to 0.21875
- tile_target: int32 [16, 8, 32, 8], P('blk', 'rep'), may hold values from 0 to 15, as said below
- tile_counts: int32 [16, 8, 32], P('blk', 'rep'), may hold values from 1 to 8, as said below
- cotangent: bfloat16 [32768, 512], P(('blk', 'rep')), may hold values from -6 to 6
Outputs:
- output: bfloat16 [32768, 512], P(('blk', 'rep'))
- grad_features: bfloat16 [32768, 512], P(('blk', 'rep'))
- grad_weight: float32 [512, 512], replicated
- grad_bias: float32 [512], replicated
The draws below stay inside these ranges and needn't reach their ends.
Inputs may be any that keep to these rules, and one draw needn't show every extreme that they name: `tile_target`: within one source row tile of one list the 8 targets are distinct row tiles of the destination block. `tile_counts`: slots at or past the count are empty; every device's list has a source row tile with all 8 slots used.
All inputs are finite; a program needn't handle non-finite values.
Results may differ from the reference program's by a relative error of at most 0.008.
Values may be sent and summed in bfloat16 or wider, within the bound.
No kernel may reach another device: no remote copies, remote signals or barrier semaphores. Data moves between devices by JAX's collectives and lax.ppermute only.
A program may use at most 128 MiB of HBM per device.

```python
import math
import jax
import jax.numpy as jnp
from jax import lax

F = 512
TILE = 128
SLOTS = 8
ROWS_DEV = 256
DEST_TILES = 16
SRC_GROUPS = 32
NODES = 32768
N_BLK = 16
N_REP = 8


def draw_tile_target(key, part):
    total_lists = N_BLK * N_REP * SRC_GROUPS
    subkeys = jax.random.split(jax.random.fold_in(key, 11), total_lists)
    picked = jax.vmap(lambda subkey: jax.random.permutation(subkey, DEST_TILES)[:SLOTS])(subkeys)
    return picked.reshape(N_BLK, N_REP, SRC_GROUPS, SLOTS).astype(jnp.int32)


def draw_tile_counts(key, part):
    base_key = jax.random.fold_in(key, 23)
    first_key, second_key, third_key = jax.random.split(base_key, 3)
    device_load = jnp.left_shift(jnp.ones((N_BLK, N_REP, 1), jnp.int32), jax.random.randint(first_key, (N_BLK, N_REP, 1), 0, 4))
    spread = jnp.maximum(device_load * SLOTS // 8, 1)
    random_draw = jax.random.randint(second_key, (N_BLK, N_REP, SRC_GROUPS), 0, 1048576)
    counts = 1 + random_draw % spread
    full_group = jax.random.randint(third_key, (N_BLK, N_REP, 1), 0, SRC_GROUPS)
    positions = jnp.arange(SRC_GROUPS, dtype=jnp.int32)[None, None, :]
    counts = jnp.where(positions == full_group, SLOTS, counts)
    return jnp.minimum(counts, SLOTS).astype(jnp.int32)


def block_levels(own_key, dims, pieces, least, largest):
    level = 1.0
    for axis_at, parts in pieces:
        draws = jax.random.uniform(jax.random.fold_in(jax.random.fold_in(own_key, 6), axis_at), (parts,), jnp.float32, least / len(pieces), largest / len(pieces))
        level = level * jnp.repeat(jnp.exp(draws), dims[axis_at] // parts).reshape((-1,) + (1,) * (len(dims) - 1 - axis_at))
    return level


def normal_values(rng, shape, width, most, shards=(), kind=jnp.bfloat16):
    factor_of = block_levels(rng, shape, shards, -0.22, 0.18) if shards else 1.0
    entries = jax.random.normal(rng, shape, jnp.float32) * width * factor_of
    return jnp.minimum(jnp.maximum(entries, -most), most).astype(kind)


def setup_inputs(seed: int = 0) -> dict:
    streams_of = jax.random.split(jax.random.key(seed), 8)
    return {
        "features": normal_values(streams_of[0], (NODES, F), 1.0, 6.0, ((0, 128),)),
        "weight": normal_values(streams_of[1], (F, F), F ** -0.5, 0.25),
        "layer_bias": normal_values(streams_of[2], (F,), 1.0, 4.0, (), jnp.float32),
        "tile_values": normal_values(streams_of[3], (N_BLK, N_REP, SRC_GROUPS, SLOTS, TILE, TILE), (1.0 / (0.3 * TILE * SLOTS * N_BLK) ** 0.5), 0.21875, ((0, 16), (1, 8))),
        "tile_target": draw_tile_target(jax.random.fold_in(streams_of[7], 71), 0),
        "tile_counts": draw_tile_counts(jax.random.fold_in(streams_of[7], 71), 0),
        "cotangent": normal_values(streams_of[6], (NODES, F), 1.0, 6.0, ((0, 128),)),
    }


def swish_parts(summed, layer_bias, cotangent):
    shifted = summed + layer_bias[None, :]
    logistic = jax.nn.sigmoid(shifted)
    output = (shifted * logistic).astype(jnp.bfloat16)
    derivative = logistic * (1.0 + shifted * (1.0 - logistic))
    grad_summed = (cotangent.astype(jnp.float32) * derivative).astype(jnp.bfloat16)
    return (output, grad_summed)

def reference(features, weight, layer_bias, tile_values, tile_target, tile_counts, cotangent):
    tile_rows = ROWS_DEV // TILE
    projected = jnp.dot(features, weight, preferred_element_type=jnp.float32).astype(jnp.bfloat16)
    proj_tiles = projected.reshape(N_BLK, N_REP, tile_rows, TILE, F)
    slot_ids = jnp.arange(SLOTS, dtype=jnp.int32)
    active = slot_ids[None, None, None, :] < tile_counts[:, :, :, None]

    def masked_tiles(block_id, rep_id):
        return jnp.where(active[block_id, rep_id][:, :, None, None], tile_values[block_id, rep_id].astype(jnp.float32), jnp.zeros((), jnp.float32))

    def forward_block(block_id):

        def rep_step(running, rep_id):
            sources = lax.dynamic_index_in_dim(proj_tiles, rep_id, 1, keepdims=False)
            sources = sources.reshape(SRC_GROUPS, TILE, F).astype(jnp.float32)
            products = jnp.einsum('gsij,gjf->gsif', masked_tiles(block_id, rep_id), sources)
            targets = tile_target[block_id, rep_id].reshape(-1)
            running = running.at[targets].add(products.reshape(SRC_GROUPS * SLOTS, TILE, F))
            return (running, None)
        running, unused = lax.scan(rep_step, jnp.zeros((DEST_TILES, TILE, F), jnp.float32), jnp.arange(N_REP, dtype=jnp.int32))
        return running
    summed = lax.map(forward_block, jnp.arange(N_BLK, dtype=jnp.int32)).reshape(NODES, F)
    output, grad_summed = swish_parts(summed, layer_bias, cotangent)
    grad_tiles = grad_summed.reshape(N_BLK, DEST_TILES, TILE, F)

    def back_step(running, flat_id):
        block_id = flat_id // N_REP
        rep_id = flat_id % N_REP
        block_grads = lax.dynamic_index_in_dim(grad_tiles, block_id, 0, keepdims=False)
        gathered = block_grads[tile_target[block_id, rep_id]].astype(jnp.float32)
        terms = jnp.einsum('gsij,gsif->gjf', masked_tiles(block_id, rep_id), gathered)
        running = running.at[rep_id].add(terms)
        return (running, None)
    grad_rows, unused = lax.scan(back_step, jnp.zeros((N_REP, SRC_GROUPS, TILE, F), jnp.float32), jnp.arange(N_BLK * N_REP, dtype=jnp.int32))
    grad_rows = grad_rows.reshape(N_REP, N_BLK, tile_rows, TILE, F).transpose(1, 0, 2, 3, 4).reshape(NODES, F)
    grad_projected = grad_rows.astype(jnp.bfloat16)
    grad_features = jnp.dot(grad_projected, weight.T, preferred_element_type=jnp.float32).astype(jnp.bfloat16)
    norm_scale = 1.0 / math.sqrt(NODES)
    grad_weight = jnp.dot(features.T, grad_projected, preferred_element_type=jnp.float32) * norm_scale
    grad_bias = lax.optimization_barrier(jnp.sum(grad_summed.astype(jnp.float32), axis=0)) * norm_scale
    return (output, grad_features, grad_weight, grad_bias)
```

```python
import itertools
import math

import jax
import jax.numpy as jnp
import numpy as np
from jax import lax
from jax.experimental import pallas as pl
from jax.experimental.pallas import tpu as pltpu
from jax.sharding import Mesh, PartitionSpec as P

SIZES = {"xl": 2, "z": 4, "core": 2, "xh": 2, "y": 4}
BLK = ("xl", "z", "core")
REP = ("xh", "y")
CHIP = ("xl", "z")
ALL = BLK + REP
VMEM = 60 << 20


def send_by(value, axes, offsets):
    sizes = [SIZES[a] for a in axes]
    pairs = []
    for at in itertools.product(*[range(n) for n in sizes]):
        to = [(i + o) % n for i, o, n in zip(at, offsets, sizes)]
        pairs.append((int(np.ravel_multi_index(at, sizes)), int(np.ravel_multi_index(to, sizes))))
    return lax.ppermute(value, axes, pairs)


def all_offsets(axes):
    return list(itertools.product(*[range(SIZES[a]) for a in axes]))


def neighbours(axes, sign):
    found = []
    for offsets in all_offsets(axes):
        flat = jnp.int32(0)
        for axis, offset in zip(axes, offsets):
            n = SIZES[axis]
            flat = flat * n + (lax.axis_index(axis) + (n + sign * offset)) % n
        found.append(flat)
    return jnp.stack(found).astype(jnp.int32)


def forward_kernel(source_ref, slot_ref, count_ref, place_ref, x_ref, v_ref, out_ref, acc_ref):
    step = pl.program_id(0)
    tile = v_ref.shape[-1]
    slots = v_ref.shape[1]

    @pl.when(step == 0)
    def _():
        acc_ref[...] = jnp.zeros_like(acc_ref)

    for t in range(2):
        group = source_ref[step] * 2 + t
        count = count_ref[group]
        for s in range(0, slots, 2):

            @pl.when(s < count)
            def _():
                rows = x_ref[0, pl.ds(t * tile, tile), :]
                tiles = v_ref[t, pl.ds(s, 2)].reshape(2 * tile, tile)
                product = jnp.dot(tiles, rows, preferred_element_type=jnp.float32)
                for k in range(2):
                    acc_ref[slot_ref[group * slots + s + k]] += product[k * tile : (k + 1) * tile]

    @pl.when(step == pl.num_programs(0) - 1)
    def _():
        for i in range(out_ref.shape[0]):
            for t in range(2):
                out_ref[i, pl.ds(t * tile, tile), :] = acc_ref[place_ref[i] * 2 + t].astype(out_ref.dtype)


def aggregate(sources, slots, counts, places, gathered, values):
    steps, rows, width = gathered.shape
    groups, slot_total, tile, _ = values.shape
    parts = places.shape[0]
    return pl.pallas_call(
        forward_kernel,
        out_shape=jax.ShapeDtypeStruct((parts, rows, width), jnp.bfloat16),
        grid_spec=pltpu.PrefetchScalarGridSpec(
            num_scalar_prefetch=4,
            grid=(steps,),
            in_specs=[
                pl.BlockSpec((1, rows, width), lambda i, *_: (i, 0, 0)),
                pl.BlockSpec((2, slot_total, tile, tile), lambda i, source, *_: (source[i], 0, 0, 0)),
            ],
            out_specs=pl.BlockSpec((parts, rows, width), lambda i, *_: (0, 0, 0)),
            scratch_shapes=[pltpu.VMEM((parts * 2 + 1, tile, width), jnp.float32)],
        ),
        compiler_params=pltpu.CompilerParams(vmem_limit_bytes=VMEM),
    )(sources, slots, counts, places, gathered, values)


def backward_kernel(source_ref, slot_ref, count_ref, g_ref, v_ref, out_ref, acc_ref, table_ref):
    step = pl.program_id(0)
    tile = v_ref.shape[-1]
    slots = v_ref.shape[1]

    @pl.when(step == 0)
    def _():
        last = table_ref.shape[0] - 1
        table_ref[last] = jnp.zeros_like(table_ref[last])
        for i in range(last):
            table_ref[i] = g_ref[i]

    for t in range(2):
        group = source_ref[step] * 2 + t
        count = count_ref[group]
        for s in range(0, slots, 2):

            @pl.when(s < count)
            def _():
                tiles = v_ref[t, pl.ds(s, 2)].reshape(2 * tile, tile)
                rows = jnp.concatenate(
                    [table_ref[slot_ref[group * slots + s]], table_ref[slot_ref[group * slots + s + 1]]], axis=0
                )
                product = lax.dot_general(
                    tiles, rows, (((0,), (0,)), ((), ())), preferred_element_type=jnp.float32
                )
                if s == 0:
                    acc_ref[...] = product
                else:
                    acc_ref[...] += product

        out_ref[0, pl.ds(t * tile, tile), :] = acc_ref[...].astype(out_ref.dtype)


def spread(sources, slots, counts, tiles, values):
    total, tile, width = tiles.shape
    steps = sources.shape[0]
    slot_total = values.shape[1]
    return pl.pallas_call(
        backward_kernel,
        out_shape=jax.ShapeDtypeStruct((steps, 2 * tile, width), jnp.bfloat16),
        grid_spec=pltpu.PrefetchScalarGridSpec(
            num_scalar_prefetch=3,
            grid=(steps,),
            in_specs=[
                pl.BlockSpec((total, tile, width), lambda i, *_: (0, 0, 0)),
                pl.BlockSpec((2, slot_total, tile, tile), lambda i, source, *_: (source[i], 0, 0, 0)),
            ],
            out_specs=pl.BlockSpec((1, 2 * tile, width), lambda i, *_: (i, 0, 0)),
            scratch_shapes=[
                pltpu.VMEM((tile, width), jnp.float32),
                pltpu.VMEM((total + 1, tile, width), jnp.bfloat16),
            ],
        ),
        compiler_params=pltpu.CompilerParams(vmem_limit_bytes=VMEM),
    )(sources, slots, counts, tiles, values)


def middle_kernel(*refs):
    parts = refs[:-8]
    weight_ref, bias_ref, cotangent_ref, out_ref, back_ref, weight_part_ref, bias_part_ref, _ = refs[-8:]
    f32 = jnp.float32
    total = parts[0][...].astype(f32)
    for part in parts[1:]:
        total += part[...].astype(f32)
    rows = total.astype(jnp.bfloat16)
    shifted = jnp.dot(rows, weight_ref[...], preferred_element_type=f32) + bias_ref[...]
    logistic = jax.nn.sigmoid(shifted)
    out_ref[...] = (shifted * logistic).astype(jnp.bfloat16)
    derivative = logistic * (1.0 + shifted * (1.0 - logistic))
    grad = (cotangent_ref[...].astype(f32) * derivative).astype(jnp.bfloat16)
    back_ref[...] = lax.dot_general(
        grad, weight_ref[...], (((1,), (1,)), ((), ())), preferred_element_type=f32
    ).astype(jnp.bfloat16)
    weight_part_ref[...] = lax.dot_general(rows, grad, (((0,), (0,)), ((), ())), preferred_element_type=f32)
    bias_part_ref[...] = jnp.sum(grad.astype(f32), axis=0, keepdims=True)


def middle(parts, weight, layer_bias, cotangent):
    rows, width = cotangent.shape
    return pl.pallas_call(
        middle_kernel,
        out_shape=(
            jax.ShapeDtypeStruct((rows, width), jnp.bfloat16),
            jax.ShapeDtypeStruct((rows, width), jnp.bfloat16),
            jax.ShapeDtypeStruct((width, width), jnp.float32),
            jax.ShapeDtypeStruct((1, width), jnp.float32),
        ),
        scratch_shapes=[pltpu.VMEM((8, 128), jnp.float32)],
        compiler_params=pltpu.CompilerParams(vmem_limit_bytes=VMEM),
    )(*parts, weight, layer_bias[None, :], cotangent)


def body(features, weight, layer_bias, tile_values, tile_target, tile_counts, cotangent):
    local_rows, width = features.shape
    values = tile_values[0, 0]
    targets = tile_target[0, 0]
    counts = tile_counts[0, 0]
    groups, slot_total = targets.shape
    rep_total = math.prod(SIZES[a] for a in REP)
    tile = values.shape[-1]
    assert local_rows == 2 * tile
    dest_tiles = 2 * rep_total

    active = lax.broadcasted_iota(jnp.int32, targets.shape, 1) < counts[:, None]
    slots = jnp.where(active, targets, dest_tiles).reshape(-1)
    owner = targets // 2
    xh, y = SIZES["xh"], SIZES["y"]
    from_part = ((lax.axis_index("xh") + xh - owner // y) % xh) * y + (lax.axis_index("y") + y - owner % y) % y
    back_slots = jnp.where(active, from_part * 2 + targets % 2, dest_tiles).reshape(-1)

    chips = all_offsets(CHIP)
    parts = all_offsets(REP)

    own = jnp.stack([features] + [send_by(features, CHIP, o) for o in chips[1:]])
    gathered = jnp.concatenate([own, send_by(own, ("core",), (1,))])
    chip_at = neighbours(CHIP, -1)
    core = lax.axis_index("core")
    arrived = jnp.concatenate([chip_at * 2 + core, chip_at * 2 + 1 - core])
    partial = aggregate(arrived, slots, counts, neighbours(REP, 1), gathered, values)

    received = [partial[0]] + [send_by(partial[i], REP, o) for i, o in enumerate(parts) if i]
    output, back, weight_part, bias_part = middle(received, weight, layer_bias, cotangent)

    blocks = jnp.stack([back] + [send_by(back, REP, o) for o in parts[1:]])
    chip_to = neighbours(CHIP, 1)
    leaving = jnp.concatenate([chip_to * 2 + 1 - core, chip_to * 2 + core])
    terms = spread(leaving, back_slots, counts, blocks.reshape(dest_tiles, tile, width), values)
    terms = terms.reshape(2, len(chips), local_rows, width)
    crossed = send_by(terms[0], ("core",), (1,))
    merged = (terms[1].astype(jnp.float32) + crossed.astype(jnp.float32)).astype(jnp.bfloat16)
    total = merged[0].astype(jnp.float32)
    for i, o in enumerate(chips):
        if i:
            total += send_by(merged[i], CHIP, o).astype(jnp.float32)
    grad_features = total.astype(jnp.bfloat16)

    device_total = math.prod(SIZES.values())
    flat = jnp.concatenate([weight_part, jnp.pad(bias_part, ((0, device_total - 1), (0, 0)))])
    pieces = lax.all_to_all(flat.reshape(device_total, -1, width), ALL, 0, 0, tiled=True)
    piece = jnp.sum(pieces, axis=0)
    whole = lax.all_to_all(
        jnp.broadcast_to(piece[None], (device_total, *piece.shape)), ALL, 0, 0, tiled=True
    ).reshape(flat.shape)
    norm_scale = 1.0 / math.sqrt(local_rows * device_total)
    whole = whole * norm_scale
    return (output, grad_features, whole[:width], whole[width])


def solution(mesh):
    fine = Mesh(np.asarray(mesh.devices).reshape(tuple(SIZES.values())), tuple(SIZES))
    placed = (
        P(ALL, None),
        P(),
        P(),
        P(BLK, REP, None, None, None, None),
        P(BLK, REP, None, None),
        P(BLK, REP, None),
        P(ALL, None),
    )
    return jax.shard_map(
        body,
        mesh=fine,
        in_specs=placed,
        out_specs=(P(ALL, None), P(ALL, None), P(), P()),
        check_vma=False,
    )
```

```python
import itertools
import math

import jax
import jax.numpy as jnp
import numpy as np
from jax import lax
from jax.experimental import pallas as pl
from jax.experimental.pallas import tpu as pltpu
from jax.sharding import Mesh, PartitionSpec as P

SIZES = {"xl": 2, "z": 4, "core": 2, "xh": 2, "y": 4}
BLK = ("xl", "z", "core")
REP = ("xh", "y")
CHIP = ("xl", "z")
ALL = BLK + REP
VMEM = 60 << 20


def send_by(value, axes, offsets):
    sizes = [SIZES[a] for a in axes]
    pairs = []
    for at in itertools.product(*[range(n) for n in sizes]):
        to = [(i + o) % n for i, o, n in zip(at, offsets, sizes)]
        pairs.append((int(np.ravel_multi_index(at, sizes)), int(np.ravel_multi_index(to, sizes))))
    return lax.ppermute(value, axes, pairs)


def all_offsets(axes):
    return list(itertools.product(*[range(SIZES[a]) for a in axes]))


EXTRA = 16
VARIANTS = (1, 2, 3, 4, 6, 8)


def cost(flops, transferred):
    return pl.CostEstimate(flops=flops, transcendentals=0, bytes_accessed=transferred)


def start_all(pairs, sems):
    for i, (source, target) in enumerate(pairs):
        pltpu.make_async_copy(source, target, sems.at[i]).start()


def forward_kernel(shards, earlier, *refs):
    source_ref, slot_ref, count_ref, place_ref, v_ref = refs[:5]
    x_refs = refs[5 : 5 + shards]
    refs = refs[5 + shards :]
    if earlier:
        before_ref, out_refs, refs = refs[0], refs[1:9], refs[9:]
        acc_ref, x_buf, v_buf, x_sem, v_sem, before_buf, before_sem = refs
        pltpu.make_async_copy(before_ref, before_buf, before_sem).start()
    else:
        out_ref, acc_ref, x_buf, v_buf, x_sem, v_sem = refs
    slots, tile = v_ref.shape[1:3]
    for i in range(shards):
        pltpu.make_async_copy(v_ref.at[pl.ds(source_ref[i] * 2, 2)], v_buf.at[i], v_sem.at[i]).start()
        pltpu.make_async_copy(x_refs[i], x_buf.at[i], x_sem.at[i]).start()
    acc_ref[...] = jnp.zeros_like(acc_ref)

    def group_step(i, t):
        group = source_ref[i] * 2 + t
        count = count_ref[group]
        low = 0
        for n in VARIANTS:

            @pl.when((count > low) & (count <= n))
            def _():
                rows = x_buf[i, pl.ds(pl.multiple_of(t * tile, tile), tile), :]
                tiles = v_buf[i, t, pl.ds(0, n)].reshape(n * tile, tile)
                product = jnp.dot(tiles, rows, preferred_element_type=jnp.float32)
                for k in range(n):
                    acc_ref[slot_ref[group * slots + k]] += product[k * tile : (k + 1) * tile]

            low = n

    def shard_step(i, carry):
        pltpu.make_async_copy(v_ref.at[pl.ds(0, 2)], v_buf.at[i], v_sem.at[i]).wait()
        pltpu.make_async_copy(x_refs[0], x_buf.at[i], x_sem.at[i]).wait()

        def inner(t, carry):
            group_step(i, t)
            return carry

        return lax.fori_loop(0, 2, inner, carry)

    lax.fori_loop(0, shards, shard_step, 0)
    if earlier:
        pltpu.make_async_copy(before_ref, before_buf, before_sem).wait()
        for i, out_ref in enumerate(out_refs):
            for t in range(2):
                at = place_ref[i] * 2 + t
                out_ref[pl.ds(t * tile, tile), :] = (acc_ref[at] + before_buf[at]).astype(out_ref.dtype)
    else:
        out_ref[...] = acc_ref[pl.ds(0, out_ref.shape[0])]


def aggregate(sources, slots, counts, places, gathered, values, before=None):
    shards = len(gathered)
    rows, width = gathered[0].shape
    _, slot_total, tile, _ = values.shape
    parts = places.shape[0]
    anywhere = pl.BlockSpec(memory_space=pl.ANY)
    scratch = [
        pltpu.VMEM((parts * 2 + 1, tile, width), jnp.float32),
        pltpu.VMEM((shards, rows, width), jnp.bfloat16),
        pltpu.VMEM((shards, 2, slot_total, tile, tile), jnp.bfloat16),
        pltpu.SemaphoreType.DMA((shards,)),
        pltpu.SemaphoreType.DMA((shards,)),
    ]
    whole = jax.ShapeDtypeStruct((parts * 2, tile, width), jnp.float32)
    if before is None:
        out_shape, extra = whole, []
    else:
        out_shape = (jax.ShapeDtypeStruct((rows, width), jnp.bfloat16),) * parts
        extra = [before]
        scratch += [pltpu.VMEM(whole.shape, whole.dtype), pltpu.SemaphoreType.DMA(())]
    inside = pl.BlockSpec(memory_space=pltpu.VMEM)
    return pl.pallas_call(
        lambda *refs: forward_kernel(shards, before is not None, *refs),
        out_shape=out_shape,
        grid_spec=pltpu.PrefetchScalarGridSpec(
            num_scalar_prefetch=4,
            grid=(),
            in_specs=[anywhere] * (1 + shards + len(extra)),
            out_specs=inside if before is None else (inside,) * parts,
            scratch_shapes=scratch,
        ),
        compiler_params=pltpu.CompilerParams(vmem_limit_bytes=VMEM),
        cost_estimate=cost(4 << 30, 12 << 20),
        name="aggregate",
    )(sources, slots, counts, places, values, *gathered, *extra)


def backward_kernel(shards, parts, crossing, with_weight, *refs):
    source_ref, slot_ref, count_ref, v_ref = refs[:4]
    m_refs, refs = refs[4 : 4 + parts], refs[4 + parts :]
    if crossing:
        crossed_ref, mine_ref, other_ref = refs[:3]
        out_refs, refs = refs[3 : 3 + shards], refs[3 + shards :]
    else:
        out_ref, refs = refs[0], refs[1:]
        if with_weight:
            sum_ref, refs = refs[0], refs[1:]
    table_ref, v_buf, m_sem, v_sem = refs[:4]
    refs = refs[4:]
    slots, tile = v_ref.shape[1:3]
    rows = 2 * tile
    for i in range(parts):
        pltpu.make_async_copy(m_refs[i].at[pl.ds(0, rows)], table_ref.at[pl.ds(i * rows, rows)], m_sem.at[i]).start()
    for i in range(shards):
        pltpu.make_async_copy(v_ref.at[pl.ds(source_ref[i] * 2, 2)], v_buf.at[i], v_sem.at[i]).start()
    if crossing:
        term_ref, cross_buf, cross_sem = refs
        pltpu.make_async_copy(crossed_ref, cross_buf, cross_sem).start()
    elif with_weight:
        w_buf, w_sem = refs
        more = w_buf.shape[1]
        for i in range(parts):
            pltpu.make_async_copy(m_refs[i].at[pl.ds(rows, more)], w_buf.at[i], w_sem.at[i]).start()
    blank = table_ref.at[pl.ds(parts * rows, tile)]
    blank[...] = jnp.zeros_like(blank)
    for i in range(parts):
        pltpu.make_async_copy(m_refs[i].at[pl.ds(0, rows)], table_ref.at[pl.ds(i * rows, rows)], m_sem.at[i]).wait()
    if crossing:
        pltpu.make_async_copy(crossed_ref, cross_buf, cross_sem).wait()

    def group_step(i, t):
        group = source_ref[i] * 2 + t
        count = count_ref[group]
        for n in range(2, slots + 1, 2):

            @pl.when((count > n - 2) & (count <= n))
            def _():
                tiles = v_buf[i, t, pl.ds(0, n)].reshape(n * tile, tile)
                found = jnp.concatenate(
                    [
                        table_ref[pl.ds(pl.multiple_of(slot_ref[group * slots + k] * tile, tile), tile), :]
                        for k in range(n)
                    ],
                    axis=0,
                )
                product = lax.dot_general(tiles, found, (((0,), (0,)), ((), ())), preferred_element_type=jnp.float32)
                at = pl.ds(pl.multiple_of(t * tile, tile), tile)
                if crossing:
                    term_ref[i, at, :] = (product + cross_buf[i, at, :].astype(jnp.float32)).astype(jnp.bfloat16)
                else:
                    out_ref[i, at, :] = product.astype(jnp.bfloat16)

    def shard_step(i, carry):
        pltpu.make_async_copy(v_ref.at[pl.ds(0, 2)], v_buf.at[i], v_sem.at[i]).wait()

        def inner(t, carry):
            group_step(i, t)
            return carry

        return lax.fori_loop(0, 2, inner, carry)

    lax.fori_loop(0, shards, shard_step, 0)
    if crossing:
        both = mine_ref[...] + other_ref[...]
        share = both.shape[0] - EXTRA
        tail = split_rows(both[share : share + 1])
        for i in range(shards):
            out_refs[i][pl.ds(0, rows), :] = term_ref[i]
            out_refs[i][pl.ds(rows, share), :] = both[:share].astype(jnp.bfloat16)
            out_refs[i][pl.ds(rows + share, EXTRA), :] = tail
    elif with_weight:
        total = None
        for i in range(parts):
            pltpu.make_async_copy(m_refs[i].at[pl.ds(rows, more)], w_buf.at[i], w_sem.at[i]).wait()
            term = w_buf[i].astype(jnp.float32)
            total = term if total is None else total + term
        share = more - EXTRA
        sum_ref[pl.ds(0, share), :] = total[:share]
        bias = total[share : share + 1] + total[share + 1 : share + 2]
        sum_ref[pl.ds(share, EXTRA), :] = jnp.broadcast_to(bias, (EXTRA, bias.shape[1]))


def split_rows(row):
    high = row.astype(jnp.bfloat16)
    low = (row - high.astype(jnp.float32)).astype(jnp.bfloat16)
    line = lax.broadcasted_iota(jnp.int32, (EXTRA, row.shape[1]), 0)
    spread_high = jnp.broadcast_to(high.astype(jnp.float32), line.shape)
    spread_low = jnp.broadcast_to(low.astype(jnp.float32), line.shape)
    return jnp.where(line == 0, spread_high, jnp.where(line == 1, spread_low, 0.0)).astype(jnp.bfloat16)


def spread(sources, slots, counts, messages, values, crossed=None, sums=None, with_weight=False):
    parts = len(messages)
    shards = sources.shape[0]
    height, width = messages[0].shape
    slot_total, tile = values.shape[1:3]
    rows = 2 * tile
    anywhere = pl.BlockSpec(memory_space=pl.ANY)
    inside = pl.BlockSpec(memory_space=pltpu.VMEM)
    scratch = [
        pltpu.VMEM((parts * rows + tile, width), jnp.bfloat16),
        pltpu.VMEM((shards, 2, slot_total, tile, tile), jnp.bfloat16),
        pltpu.SemaphoreType.DMA((parts,)),
        pltpu.SemaphoreType.DMA((shards,)),
    ]
    crossing = crossed is not None
    in_specs = [anywhere] * (1 + parts)
    operands = []
    if crossing:
        operands = [crossed, *sums]
        in_specs += [anywhere, inside, inside]
        out_shape = (jax.ShapeDtypeStruct((height, width), jnp.bfloat16),) * shards
        out_specs = (inside,) * shards
        scratch += [
            pltpu.VMEM((shards, rows, width), jnp.bfloat16),
            pltpu.VMEM((shards, rows, width), jnp.bfloat16),
            pltpu.SemaphoreType.DMA(()),
        ]
    else:
        out_shape = (jax.ShapeDtypeStruct((shards, rows, width), jnp.bfloat16),)
        if with_weight:
            more = height - rows
            out_shape += (jax.ShapeDtypeStruct((more, width), jnp.float32),)
            scratch += [pltpu.VMEM((parts, more, width), jnp.bfloat16), pltpu.SemaphoreType.DMA((parts,))]
        out_specs = (inside,) * len(out_shape)
    return pl.pallas_call(
        lambda *refs: backward_kernel(shards, parts, crossing, with_weight, *refs),
        out_shape=out_shape,
        grid_spec=pltpu.PrefetchScalarGridSpec(
            num_scalar_prefetch=3, grid=(), in_specs=in_specs, out_specs=out_specs, scratch_shapes=scratch
        ),
        compiler_params=pltpu.CompilerParams(vmem_limit_bytes=VMEM),
        cost_estimate=cost(2 << 30, 8 << 20),
        name="spread",
    )(sources, slots, counts, values, *messages, *operands)


def middle_kernel(place_ref, *refs):
    parts = place_ref.shape[0]
    part_refs, refs = refs[:parts], refs[parts:]
    weight_ref, bias_ref, cotangent_ref, out_ref = refs[:4]
    message_refs, part_ref = refs[4 : 4 + parts], refs[4 + parts]
    f32 = jnp.float32
    total = part_refs[0][...].astype(f32)
    for part in part_refs[1:]:
        total += part[...].astype(f32)
    rows = total.astype(jnp.bfloat16)
    shifted = jnp.dot(rows, weight_ref[...], preferred_element_type=f32) + bias_ref[...]
    logistic = jax.nn.sigmoid(shifted)
    out_ref[...] = (shifted * logistic).astype(jnp.bfloat16)
    derivative = logistic * (1.0 + shifted * (1.0 - logistic))
    grad = (cotangent_ref[...].astype(f32) * derivative).astype(jnp.bfloat16)
    back = lax.dot_general(
        grad, weight_ref[...], (((1,), (1,)), ((), ())), preferred_element_type=f32
    ).astype(jnp.bfloat16)
    part_ref[...] = lax.dot_general(rows, grad, (((0,), (0,)), ((), ())), preferred_element_type=f32)
    tail = split_rows(jnp.sum(grad.astype(f32), axis=0, keepdims=True))
    share = part_ref.shape[0] // parts
    high = back.shape[0]
    for i, message_ref in enumerate(message_refs):
        message_ref[pl.ds(0, high), :] = back
        at = pl.multiple_of(place_ref[i] * share, share)
        message_ref[pl.ds(high, share), :] = part_ref[pl.ds(at, share), :].astype(jnp.bfloat16)
        message_ref[pl.ds(high + share, EXTRA), :] = tail


def middle(places, sums, weight, layer_bias, cotangent):
    rows, width = cotangent.shape
    parts = len(sums)
    inside = pl.BlockSpec(memory_space=pltpu.VMEM)
    message = jax.ShapeDtypeStruct((rows + width // parts + EXTRA, width), jnp.bfloat16)
    return pl.pallas_call(
        middle_kernel,
        out_shape=(jax.ShapeDtypeStruct((rows, width), jnp.bfloat16),) + (message,) * parts,
        grid_spec=pltpu.PrefetchScalarGridSpec(
            num_scalar_prefetch=1,
            grid=(),
            in_specs=[inside] * (parts + 3),
            out_specs=(inside,) * (parts + 1),
            scratch_shapes=[pltpu.VMEM((width, width), jnp.float32)],
        ),
        compiler_params=pltpu.CompilerParams(vmem_limit_bytes=VMEM),
        cost_estimate=cost(1 << 30, 8 << 20),
        name="middle",
    )(places, *sums, weight, layer_bias[None, :], cotangent)


def finish_kernel(rows, scale, *refs):
    messages, (grad_ref, part_ref, bias_ref) = refs[:-3], refs[-3:]
    f32 = jnp.float32
    total = messages[0][...].astype(f32)
    for message in messages[1:]:
        total += message[...].astype(f32)
    share = part_ref.shape[0]
    grad_ref[...] = total[:rows].astype(jnp.bfloat16)
    part_ref[...] = total[rows : rows + share].astype(jnp.bfloat16)
    last = rows + share
    bias_ref[...] = (total[last : last + 1] + total[last + 1 : last + 2]) * scale


def finish(messages, rows, scale):
    height, width = messages[0].shape
    return pl.pallas_call(
        lambda *refs: finish_kernel(rows, scale, *refs),
        out_shape=(
            jax.ShapeDtypeStruct((rows, width), jnp.bfloat16),
            jax.ShapeDtypeStruct((height - rows - EXTRA, width), jnp.bfloat16),
            jax.ShapeDtypeStruct((1, width), jnp.float32),
        ),
        compiler_params=pltpu.CompilerParams(vmem_limit_bytes=VMEM),
        name="finish",
    )(*messages)


def place_kernel(scale, place_ref, *refs):
    share = refs[0].shape[0]
    for i, piece in enumerate(refs[:-1]):
        at = pl.multiple_of(place_ref[i] * share, share)
        refs[-1][pl.ds(at, share), :] = piece[...].astype(jnp.float32) * scale


def place(places, pieces, scale):
    share, width = pieces[0].shape
    inside = pl.BlockSpec(memory_space=pltpu.VMEM)
    return pl.pallas_call(
        lambda *refs: place_kernel(scale, *refs),
        out_shape=jax.ShapeDtypeStruct((share * len(pieces), width), jnp.float32),
        grid_spec=pltpu.PrefetchScalarGridSpec(
            num_scalar_prefetch=1, grid=(), in_specs=[inside] * len(pieces), out_specs=inside
        ),
        compiler_params=pltpu.CompilerParams(vmem_limit_bytes=VMEM),
        name="place",
    )(places, *pieces)


CHIP_HALVES = (((0, 0), (0, 1), (0, 3), (1, 0)), ((0, 2), (1, 1), (1, 3), (1, 2)))


def at_offset(axes, offsets, sign):
    flat = jnp.int32(0)
    for axis, offset in zip(axes, offsets):
        n = SIZES[axis]
        flat = flat * n + (lax.axis_index(axis) + (n + sign * offset)) % n
    return flat


def listed(values):
    line = lax.iota(jnp.int32, len(values))
    found = jnp.zeros_like(line)
    for i, value in enumerate(values):
        found = jnp.where(line == i, value, found)
    return found


def body(features, weight, layer_bias, tile_values, tile_target, tile_counts, cotangent):
    local_rows, width = features.shape
    values = tile_values[0, 0]
    targets = tile_target[0, 0]
    counts = tile_counts[0, 0]
    tile = values.shape[-1]
    slot_total = values.shape[1]
    assert local_rows == 2 * tile and slot_total == VARIANTS[-1]
    parts = all_offsets(REP)
    dest_tiles = 2 * len(parts)

    active = lax.broadcasted_iota(jnp.int32, targets.shape, 1) < counts[:, None]
    slots = jnp.where(active, targets, dest_tiles).reshape(-1)
    owner = targets // 2
    xh, y = SIZES["xh"], SIZES["y"]
    from_part = ((lax.axis_index("xh") + xh - owner // y) % xh) * y + (lax.axis_index("y") + y - owner % y) % y
    back_slots = jnp.where(active, from_part * 2 + targets % 2, dest_tiles).reshape(-1)
    core = lax.axis_index("core")
    part_to = listed([at_offset(REP, o, 1) for o in parts])
    part_from = listed([at_offset(REP, o, -1) for o in parts])

    partial = None
    for half in CHIP_HALVES:
        own = [send_by(features, CHIP, o) if any(o) else features for o in half]
        crossed = [send_by(x, ("core",), (1,)) for x in own]
        at = [at_offset(CHIP, o, -1) * 2 for o in half]
        sources = listed([c + core for c in at] + [c + 1 - core for c in at])
        partial = aggregate(sources, slots, counts, part_to, own + crossed, values, partial)

    received = [send_by(partial[i], REP, o) if any(o) else partial[i] for i, o in enumerate(parts)]
    output, *messages = middle(part_to, received, weight, layer_bias, cotangent)
    messages = [send_by(messages[i], REP, o) if any(o) else messages[i] for i, o in enumerate(parts)]

    halves = CHIP_HALVES[::-1]
    to_chip = [[at_offset(CHIP, o, 1) * 2 for o in half] for half in halves]
    across, sums = [], None
    for i in range(2):
        sources = listed([c + 1 - core for c in to_chip[i]])
        found = spread(sources, back_slots, counts, messages, values, with_weight=i == 0)
        across.append(send_by(found[0], ("core",), (1,)))
        if i == 0:
            sums = (found[1], send_by(found[1], ("core",), (1,)))
    last = []
    for i in range(2):
        sources = listed([c + core for c in to_chip[i]])
        merged = spread(sources, back_slots, counts, messages, values, across[i], sums)
        last += [send_by(m, CHIP, o) if any(o) else m for m, o in zip(merged, halves[i])]
    norm_scale = 1.0 / math.sqrt(local_rows * math.prod(SIZES.values()))
    grad_features, piece, grad_bias = finish(last, local_rows, norm_scale)
    pieces = [send_by(piece, REP, o) if any(o) else piece for o in parts]
    grad_weight = place(part_from, pieces, norm_scale)
    return (output, grad_features, grad_weight, grad_bias[0])


def solution(mesh):
    fine = Mesh(np.asarray(mesh.devices).reshape(tuple(SIZES.values())), tuple(SIZES))
    placed = (
        P(ALL, None),
        P(),
        P(),
        P(BLK, REP, None, None, None, None),
        P(BLK, REP, None, None),
        P(BLK, REP, None),
        P(ALL, None),
    )
    return jax.shard_map(
        body,
        mesh=fine,
        in_specs=placed,
        out_specs=(P(ALL, None), P(ALL, None), P(), P()),
        check_vma=False,
    )
```

```python
import itertools
import math

import jax
import jax.numpy as jnp
import numpy as np
from jax import lax
from jax.experimental import pallas as pl
from jax.experimental.pallas import tpu as pltpu
from jax.sharding import Mesh, PartitionSpec as P

SIZES = {"xl": 2, "z": 4, "core": 2, "xh": 2, "y": 4}
BLK = ("xl", "z", "core")
REP = ("xh", "y")
CHIP = ("xl", "z")
ALL = BLK + REP
VMEM = 60 << 20


def send_by(value, axes, offsets):
    sizes = [SIZES[a] for a in axes]
    pairs = []
    for at in itertools.product(*[range(n) for n in sizes]):
        to = [(i + o) % n for i, o, n in zip(at, offsets, sizes)]
        pairs.append((int(np.ravel_multi_index(at, sizes)), int(np.ravel_multi_index(to, sizes))))
    return lax.ppermute(value, axes, pairs)


def exchange(value, axis, mask):
    return lax.ppermute(value, axis, [(i, i ^ mask) for i in range(SIZES[axis])])


def all_offsets(axes):
    return list(itertools.product(*[range(SIZES[a]) for a in axes]))


EXTRA = 16
VARIANTS = (1, 2, 3, 4, 6, 8)


def cost(flops, transferred):
    return pl.CostEstimate(flops=flops, transcendentals=0, bytes_accessed=transferred)


def of_class(count, action):
    low = 0
    for n in VARIANTS:

        @pl.when((count > low) & (count <= n))
        def _():
            action(n)

        low = n


def tiles_copy(v_ref, v_buf, sem, group, to, n):
    return pltpu.make_async_copy(v_ref.at[group, pl.ds(0, n)], v_buf.at[to, pl.ds(0, n)], sem.at[to])


def start_tiles(source_ref, count_ref, v_ref, v_buf, sem):
    def step(k, carry):
        group = source_ref[k // 2] * 2 + k % 2
        of_class(count_ref[group], lambda n: tiles_copy(v_ref, v_buf, sem, group, k, n).start())
        return carry

    lax.fori_loop(0, v_buf.shape[0], step, 0)


def forward_kernel(shards, source_ref, slot_ref, count_ref, place_ref, v_ref, *refs):
    x_refs, refs = refs[:shards], refs[shards:]
    acc_ref, x_buf, v_buf, x_sem, v_sem = refs[-5:]
    out_refs = refs[:-5]
    slots, tile = v_ref.shape[1:3]
    for i in range(shards):
        pltpu.make_async_copy(x_refs[i], x_buf.at[i], x_sem.at[i]).start()
    start_tiles(source_ref, count_ref, v_ref, v_buf, v_sem)
    acc_ref[...] = jnp.zeros_like(acc_ref)

    def group_step(k, carry):
        group = source_ref[k // 2] * 2 + k % 2

        @pl.when(k % 2 == 0)
        def _():
            pltpu.make_async_copy(x_refs[0], x_buf.at[k // 2], x_sem.at[k // 2]).wait()

        def work(n):
            tiles_copy(v_ref, v_buf, v_sem, group, k, n).wait()
            rows = x_buf[k // 2, pl.ds(pl.multiple_of(k % 2 * tile, tile), tile), :]
            tiles = v_buf[k, pl.ds(0, n)].reshape(n * tile, tile)
            product = jnp.dot(tiles, rows, preferred_element_type=jnp.float32)
            for m in range(n):
                acc_ref[slot_ref[group * slots + m]] += product[m * tile : (m + 1) * tile]

        of_class(count_ref[group], work)
        return carry

    lax.fori_loop(0, 2 * shards, group_step, 0)
    for i, out_ref in enumerate(out_refs):
        for t in range(2):
            out_ref[pl.ds(t * tile, tile), :] = acc_ref[place_ref[i] * 2 + t].astype(out_ref.dtype)


def aggregate(sources, slots, counts, places, gathered, values):
    shards = len(gathered)
    rows, width = gathered[0].shape
    _, slot_total, tile, _ = values.shape
    parts = places.shape[0]
    anywhere = pl.BlockSpec(memory_space=pl.ANY)
    inside = pl.BlockSpec(memory_space=pltpu.VMEM)
    return pl.pallas_call(
        lambda *refs: forward_kernel(shards, *refs),
        out_shape=(jax.ShapeDtypeStruct((rows, width), jnp.bfloat16),) * parts,
        grid_spec=pltpu.PrefetchScalarGridSpec(
            num_scalar_prefetch=4,
            grid=(),
            in_specs=[anywhere] * (1 + shards),
            out_specs=(inside,) * parts,
            scratch_shapes=[
                pltpu.VMEM((parts * 2 + 1, tile, width), jnp.float32),
                pltpu.VMEM((shards, rows, width), jnp.bfloat16),
                pltpu.VMEM((shards * 2, slot_total, tile, tile), jnp.bfloat16),
                pltpu.SemaphoreType.DMA((shards,)),
                pltpu.SemaphoreType.DMA((shards * 2,)),
            ],
        ),
        compiler_params=pltpu.CompilerParams(vmem_limit_bytes=VMEM),
        cost_estimate=cost(8 << 30, 16 << 20),
        name="aggregate",
    )(sources, slots, counts, places, values, *gathered)


def backward_kernel(shards, parts, crossing, with_weight, *refs):
    source_ref, slot_ref, count_ref, v_ref = refs[:4]
    m_refs, refs = refs[4 : 4 + parts], refs[4 + parts :]
    if crossing:
        crossed_refs, refs = refs[:crossing], refs[crossing:]
        out_refs, refs = refs[:shards], refs[shards:]
    else:
        out_ref, refs = refs[0], refs[1:]
        if with_weight:
            sum_ref, refs = refs[0], refs[1:]
    table_ref, v_buf, m_sem, v_sem = refs[:4]
    refs = refs[4:]
    slots, tile = v_ref.shape[1:3]
    rows = 2 * tile
    for i in range(parts):
        pltpu.make_async_copy(m_refs[i].at[pl.ds(0, rows)], table_ref.at[pl.ds(i * rows, rows)], m_sem.at[i]).start()
    start_tiles(source_ref, count_ref, v_ref, v_buf, v_sem)
    if crossing:
        term_ref, cross_buf, cross_sem = refs
        each = shards // crossing
        for i in range(crossing):
            pltpu.make_async_copy(crossed_refs[i], cross_buf.at[pl.ds(i * each, each)], cross_sem.at[i]).start()
    elif with_weight:
        w_buf, w_sem = refs
        more = w_buf.shape[1]
        for i in range(parts):
            pltpu.make_async_copy(m_refs[i].at[pl.ds(rows, more)], w_buf.at[i], w_sem.at[i]).start()
    blank = table_ref.at[pl.ds(parts * rows, tile)]
    blank[...] = jnp.zeros_like(blank)
    for i in range(parts):
        pltpu.make_async_copy(m_refs[i].at[pl.ds(0, rows)], table_ref.at[pl.ds(i * rows, rows)], m_sem.at[i]).wait()
    if crossing:
        for i in range(crossing):
            pltpu.make_async_copy(crossed_refs[i], cross_buf.at[pl.ds(i * each, each)], cross_sem.at[i]).wait()

    def group_step(k, carry):
        group = source_ref[k // 2] * 2 + k % 2
        i = k // 2
        at = pl.ds(pl.multiple_of(k % 2 * tile, tile), tile)

        def work(n):
            tiles_copy(v_ref, v_buf, v_sem, group, k, n).wait()
            tiles = v_buf[k, pl.ds(0, n)].reshape(n * tile, tile)
            found = [
                table_ref[pl.ds(pl.multiple_of(slot_ref[group * slots + m] * tile, tile), tile), :] for m in range(n)
            ]
            found = jnp.concatenate(found, axis=0) if n > 1 else found[0]
            product = lax.dot_general(tiles, found, (((0,), (0,)), ((), ())), preferred_element_type=jnp.float32)
            if crossing:
                term_ref[i, at, :] = (product + cross_buf[i, at, :].astype(jnp.float32)).astype(jnp.bfloat16)
            else:
                out_ref[i, at, :] = product.astype(jnp.bfloat16)

        of_class(count_ref[group], work)
        return carry

    lax.fori_loop(0, 2 * shards, group_step, 0)
    if crossing:
        for i in range(shards):
            out_refs[i][...] = term_ref[i]
    elif with_weight:
        total = None
        for i in range(parts):
            pltpu.make_async_copy(m_refs[i].at[pl.ds(rows, more)], w_buf.at[i], w_sem.at[i]).wait()
            term = w_buf[i].astype(jnp.float32)
            total = term if total is None else total + term
        share = more - EXTRA
        sum_ref[pl.ds(0, share), :] = total[:share]
        bias = total[share : share + 1] + total[share + 1 : share + 2]
        sum_ref[pl.ds(share, sum_ref.shape[0] - share), :] = jnp.broadcast_to(
            bias, (sum_ref.shape[0] - share, bias.shape[1])
        )


def split_rows(row):
    high = row.astype(jnp.bfloat16)
    low = (row - high.astype(jnp.float32)).astype(jnp.bfloat16)
    line = lax.broadcasted_iota(jnp.int32, (EXTRA, row.shape[1]), 0)
    spread_high = jnp.broadcast_to(high.astype(jnp.float32), line.shape)
    spread_low = jnp.broadcast_to(low.astype(jnp.float32), line.shape)
    return jnp.where(line == 0, spread_high, jnp.where(line == 1, spread_low, 0.0)).astype(jnp.bfloat16)


def spread(sources, slots, counts, messages, values, crossed=(), with_weight=False):
    parts = len(messages)
    shards = sources.shape[0]
    height, width = messages[0].shape
    slot_total, tile = values.shape[1:3]
    rows = 2 * tile
    anywhere = pl.BlockSpec(memory_space=pl.ANY)
    inside = pl.BlockSpec(memory_space=pltpu.VMEM)
    scratch = [
        pltpu.VMEM((parts * rows + tile, width), jnp.bfloat16),
        pltpu.VMEM((shards * 2, slot_total, tile, tile), jnp.bfloat16),
        pltpu.SemaphoreType.DMA((parts,)),
        pltpu.SemaphoreType.DMA((shards * 2,)),
    ]
    if crossed:
        out_shape = (jax.ShapeDtypeStruct((rows, width), jnp.bfloat16),) * shards
        scratch += [
            pltpu.VMEM((shards, rows, width), jnp.bfloat16),
            pltpu.VMEM((shards, rows, width), jnp.bfloat16),
            pltpu.SemaphoreType.DMA((len(crossed),)),
        ]
    else:
        out_shape = (jax.ShapeDtypeStruct((shards, rows, width), jnp.bfloat16),)
        if with_weight:
            more = height - rows
            out_shape += (jax.ShapeDtypeStruct((more - EXTRA + 8, width), jnp.float32),)
            scratch += [pltpu.VMEM((parts, more, width), jnp.bfloat16), pltpu.SemaphoreType.DMA((parts,))]
    return pl.pallas_call(
        lambda *refs: backward_kernel(shards, parts, len(crossed), with_weight, *refs),
        out_shape=out_shape,
        grid_spec=pltpu.PrefetchScalarGridSpec(
            num_scalar_prefetch=3,
            grid=(),
            in_specs=[anywhere] * (1 + parts + len(crossed)),
            out_specs=(inside,) * len(out_shape),
            scratch_shapes=scratch,
        ),
        compiler_params=pltpu.CompilerParams(vmem_limit_bytes=VMEM),
        cost_estimate=cost(shards << 29, shards << 20),
        name="spread",
    )(sources, slots, counts, values, *messages, *crossed)


def middle_kernel(place_ref, *refs):
    parts = place_ref.shape[0]
    part_refs, refs = refs[:parts], refs[parts:]
    weight_ref, bias_ref, cotangent_ref, out_ref = refs[:4]
    message_refs, part_ref = refs[4 : 4 + parts], refs[4 + parts]
    f32 = jnp.float32
    total = part_refs[0][...].astype(f32)
    for part in part_refs[1:]:
        total += part[...].astype(f32)
    rows = total.astype(jnp.bfloat16)
    shifted = jnp.dot(rows, weight_ref[...], preferred_element_type=f32) + bias_ref[...]
    logistic = jax.nn.sigmoid(shifted)
    out_ref[...] = (shifted * logistic).astype(jnp.bfloat16)
    derivative = logistic * (1.0 + shifted * (1.0 - logistic))
    grad = (cotangent_ref[...].astype(f32) * derivative).astype(jnp.bfloat16)
    back = lax.dot_general(
        grad, weight_ref[...], (((1,), (1,)), ((), ())), preferred_element_type=f32
    ).astype(jnp.bfloat16)
    part_ref[...] = lax.dot_general(rows, grad, (((0,), (0,)), ((), ())), preferred_element_type=f32)
    tail = split_rows(jnp.sum(grad.astype(f32), axis=0, keepdims=True))
    share = part_ref.shape[0] // parts
    high = back.shape[0]
    for i, message_ref in enumerate(message_refs):
        message_ref[pl.ds(0, high), :] = back
        at = pl.multiple_of(place_ref[i] * share, share)
        message_ref[pl.ds(high, share), :] = part_ref[pl.ds(at, share), :].astype(jnp.bfloat16)
        message_ref[pl.ds(high + share, EXTRA), :] = tail


def middle(places, sums, weight, layer_bias, cotangent):
    rows, width = cotangent.shape
    parts = len(sums)
    inside = pl.BlockSpec(memory_space=pltpu.VMEM)
    message = jax.ShapeDtypeStruct((rows + width // parts + EXTRA, width), jnp.bfloat16)
    return pl.pallas_call(
        middle_kernel,
        out_shape=(jax.ShapeDtypeStruct((rows, width), jnp.bfloat16),) + (message,) * parts,
        grid_spec=pltpu.PrefetchScalarGridSpec(
            num_scalar_prefetch=1,
            grid=(),
            in_specs=[inside] * (parts + 3),
            out_specs=(inside,) * (parts + 1),
            scratch_shapes=[pltpu.VMEM((width, width), jnp.float32)],
        ),
        compiler_params=pltpu.CompilerParams(vmem_limit_bytes=VMEM),
        cost_estimate=cost(1 << 30, 8 << 20),
        name="middle",
    )(places, *sums, weight, layer_bias[None, :], cotangent)


def place_kernel(scale, share, place_ref, *refs):
    for i, piece in enumerate(refs[:-1]):
        for k in range(piece.shape[0] // share):
            at = pl.multiple_of(place_ref[2 * i + k] * share, share)
            refs[-1][pl.ds(at, share), :] = piece[pl.ds(k * share, share), :].astype(jnp.float32) * scale


def place(places, pieces, share, scale):
    width = pieces[0].shape[1]
    inside = pl.BlockSpec(memory_space=pltpu.VMEM)
    return pl.pallas_call(
        lambda *refs: place_kernel(scale, share, *refs),
        out_shape=jax.ShapeDtypeStruct((share * places.shape[0], width), jnp.float32),
        grid_spec=pltpu.PrefetchScalarGridSpec(
            num_scalar_prefetch=1, grid=(), in_specs=[inside] * len(pieces), out_specs=inside
        ),
        compiler_params=pltpu.CompilerParams(vmem_limit_bytes=VMEM),
        name="place",
    )(places, *pieces)


CHIP_HALVES = (((0, 0), (0, 1), (0, 3), (1, 0)), ((0, 2), (1, 1), (1, 3), (1, 2)))


def at_offset(axes, offsets, sign):
    flat = jnp.int32(0)
    for axis, offset in zip(axes, offsets):
        n = SIZES[axis]
        flat = flat * n + (lax.axis_index(axis) + (n + sign * offset)) % n
    return flat


def listed(values):
    line = lax.iota(jnp.int32, len(values))
    found = jnp.zeros_like(line)
    for i, value in enumerate(values):
        found = jnp.where(line == i, value, found)
    return found


def body(features, weight, layer_bias, tile_values, tile_target, tile_counts, cotangent):
    local_rows, width = features.shape
    values = tile_values[0, 0]
    targets = tile_target[0, 0]
    counts = tile_counts[0, 0]
    tile = values.shape[-1]
    slot_total = values.shape[1]
    assert local_rows == 2 * tile and slot_total == VARIANTS[-1]
    parts = all_offsets(REP)
    dest_tiles = 2 * len(parts)

    active = lax.broadcasted_iota(jnp.int32, targets.shape, 1) < counts[:, None]
    slots = jnp.where(active, targets, dest_tiles).reshape(-1)
    owner = targets // 2
    xh, y = SIZES["xh"], SIZES["y"]
    from_part = ((lax.axis_index("xh") + xh - owner // y) % xh) * y + (lax.axis_index("y") + y - owner % y) % y
    back_slots = jnp.where(active, from_part * 2 + targets % 2, dest_tiles).reshape(-1)
    core = lax.axis_index("core")
    part_to = listed([at_offset(REP, o, 1) for o in parts])

    chips = CHIP_HALVES[0] + CHIP_HALVES[1]
    own = [send_by(features, CHIP, o) if any(o) else features for o in chips]
    crossed = [send_by(x, ("core",), (1,)) for x in own]
    at = [at_offset(CHIP, o, -1) * 2 for o in chips]
    sources = listed([c + core for c in at] + [c + 1 - core for c in at])
    partial = aggregate(sources, slots, counts, part_to, own + crossed, values)

    received = [send_by(partial[i], REP, o) if any(o) else partial[i] for i, o in enumerate(parts)]
    output, *messages = middle(part_to, received, weight, layer_bias, cotangent)
    messages = [send_by(messages[i], REP, o) if any(o) else messages[i] for i, o in enumerate(parts)]

    halves = CHIP_HALVES[::-1]
    to_chip = [[at_offset(CHIP, o, 1) * 2 for o in half] for half in halves]
    across = []
    for i in range(2):
        sources = listed([c + 1 - core for c in to_chip[i]])
        found = spread(sources, back_slots, counts, messages, values, with_weight=i == 0)
        across.append(send_by(found[0], ("core",), (1,)))
        if i == 0:
            share_sum = found[1]
    sources = listed([c + core for c in to_chip[0] + to_chip[1]])
    merged = spread(sources, back_slots, counts, messages, values, across)
    total = None
    for piece, o in zip(merged, halves[0] + halves[1]):
        piece = (send_by(piece, CHIP, o) if any(o) else piece).astype(jnp.float32)
        total = piece if total is None else total + piece
    grad_features = total.astype(jnp.bfloat16)

    share_sum = share_sum + send_by(share_sum, ("core",), (1,))
    share_sum = share_sum + send_by(share_sum, ("xl",), (1,))
    share_sum = share_sum + exchange(share_sum, "z", 1)
    share_sum = share_sum + exchange(share_sum, "z", 2)
    norm_scale = 1.0 / math.sqrt(local_rows * math.prod(SIZES.values()))
    share = width // len(parts)
    grad_bias = share_sum[share] * norm_scale
    piece = share_sum[:share].astype(jnp.bfloat16)
    pair = jnp.concatenate([piece, send_by(piece, ("xh",), (1,))])
    pieces = [send_by(pair, ("y",), (o,)) if o else pair for o in range(y)]
    at = [at_offset(REP, (k, o), -1) for o in range(y) for k in range(xh)]
    grad_weight = place(listed(at), pieces, share, norm_scale)
    return (output, grad_features, grad_weight, grad_bias)


def solution(mesh):
    fine = Mesh(np.asarray(mesh.devices).reshape(tuple(SIZES.values())), tuple(SIZES))
    placed = (
        P(ALL, None),
        P(),
        P(),
        P(BLK, REP, None, None, None, None),
        P(BLK, REP, None, None),
        P(BLK, REP, None),
        P(ALL, None),
    )
    return jax.shard_map(
        body,
        mesh=fine,
        in_specs=placed,
        out_specs=(P(ALL, None), P(ALL, None), P(), P()),
        check_vma=False,
    )
```

```python
import itertools
import math

import jax
import jax.numpy as jnp
import numpy as np
from jax import lax
from jax.experimental import pallas as pl
from jax.experimental.pallas import tpu as pltpu
from jax.sharding import Mesh, PartitionSpec as P

SIZES = {"xl": 2, "z": 4, "core": 2, "xh": 2, "y": 4}
BLK = ("xl", "z", "core")
REP = ("xh", "y")
CHIP = ("xl", "z")
ALL = BLK + REP
VMEM = 60 << 20


def send_by(value, axes, offsets):
    sizes = [SIZES[a] for a in axes]
    pairs = []
    for at in itertools.product(*[range(n) for n in sizes]):
        to = [(i + o) % n for i, o, n in zip(at, offsets, sizes)]
        pairs.append((int(np.ravel_multi_index(at, sizes)), int(np.ravel_multi_index(to, sizes))))
    return lax.ppermute(value, axes, pairs)


def exchange(value, axis, mask):
    return lax.ppermute(value, axis, [(i, i ^ mask) for i in range(SIZES[axis])])


def all_offsets(axes):
    return list(itertools.product(*[range(SIZES[a]) for a in axes]))


EXTRA = 16
VARIANTS = (1, 2, 3, 4, 6, 8)


def cost(flops, transferred):
    return pl.CostEstimate(flops=flops, transcendentals=0, bytes_accessed=transferred)


class Window:
    def __init__(self, ref, base, length):
        self.ref, self.base, self.shape = ref, base, (length,)

    def __getitem__(self, i):
        return self.ref[self.base + i]


def of_class(count, action):
    low = 0
    for n in VARIANTS:

        @pl.when((count > low) & (count <= n))
        def _():
            action(n)

        low = n


def tiles_copy(v_ref, v_buf, sem, group, to, n):
    return pltpu.make_async_copy(v_ref.at[group, pl.ds(0, n)], v_buf.at[to, pl.ds(0, n)], sem.at[to])


def start_tiles(source_ref, count_ref, v_ref, v_buf, sem):
    def step(k, carry):
        group = source_ref[k // 2] * 2 + k % 2
        of_class(count_ref[group], lambda n: tiles_copy(v_ref, v_buf, sem, group, k, n).start())
        return carry

    lax.fori_loop(0, v_buf.shape[0], step, 0)


def forward_kernel(shards, at_source, at_place, index_ref, target_ref, count_ref, v_ref, *refs):
    source_ref = Window(index_ref, at_source, shards)
    place_ref = Window(index_ref, at_place, len(refs) - 5 - shards)
    x_refs, refs = refs[:shards], refs[shards:]
    acc_ref, x_buf, v_buf, x_sem, v_sem = refs[-5:]
    out_refs = refs[:-5]
    tile = v_ref.shape[-1]
    dummy = acc_ref.shape[0] - 1
    for i in range(shards):
        pltpu.make_async_copy(x_refs[i], x_buf.at[i], x_sem.at[i]).start()
    start_tiles(source_ref, count_ref, v_ref, v_buf, v_sem)
    acc_ref[...] = jnp.zeros_like(acc_ref)

    def group_step(k, carry):
        group = source_ref[k // 2] * 2 + k % 2

        @pl.when(k % 2 == 0)
        def _():
            pltpu.make_async_copy(x_refs[0], x_buf.at[k // 2], x_sem.at[k // 2]).wait()

        def work(n):
            tiles_copy(v_ref, v_buf, v_sem, group, k, n).wait()
            rows = x_buf[k // 2, pl.ds(pl.multiple_of(k % 2 * tile, tile), tile), :]
            tiles = v_buf[k, pl.ds(0, n)].reshape(n * tile, tile)
            product = jnp.dot(tiles, rows, preferred_element_type=jnp.float32)
            for m in range(n):
                to = jnp.where(m < count_ref[group], target_ref[group, m], dummy)
                acc_ref[to] += product[m * tile : (m + 1) * tile]

        of_class(count_ref[group], work)
        return carry

    lax.fori_loop(0, 2 * shards, group_step, 0)
    for i, out_ref in enumerate(out_refs):
        for t in range(2):
            out_ref[pl.ds(t * tile, tile), :] = acc_ref[place_ref[i] * 2 + t].astype(out_ref.dtype)


def aggregate(at_source, at_place, parts, index, targets, counts, gathered, values):
    shards = len(gathered)
    rows, width = gathered[0].shape
    _, slot_total, tile, _ = values.shape
    anywhere = pl.BlockSpec(memory_space=pl.ANY)
    inside = pl.BlockSpec(memory_space=pltpu.VMEM)
    return pl.pallas_call(
        lambda *refs: forward_kernel(shards, at_source, at_place, *refs),
        out_shape=(jax.ShapeDtypeStruct((rows, width), jnp.bfloat16),) * parts,
        grid_spec=pltpu.PrefetchScalarGridSpec(
            num_scalar_prefetch=3,
            grid=(),
            in_specs=[anywhere] * (1 + shards),
            out_specs=(inside,) * parts,
            scratch_shapes=[
                pltpu.VMEM((parts * 2 + 1, tile, width), jnp.float32),
                pltpu.VMEM((shards, rows, width), jnp.bfloat16),
                pltpu.VMEM((shards * 2, slot_total, tile, tile), jnp.bfloat16),
                pltpu.SemaphoreType.DMA((shards,)),
                pltpu.SemaphoreType.DMA((shards * 2,)),
            ],
        ),
        compiler_params=pltpu.CompilerParams(vmem_limit_bytes=VMEM),
        cost_estimate=cost(8 << 30, 16 << 20),
        name="aggregate",
    )(index, targets, counts, values, *gathered)


def backward_kernel(shards, parts, at_source, at_turn, crossing, *refs):
    index_ref, target_ref, count_ref, v_ref = refs[:4]
    source_ref = Window(index_ref, at_source, shards)
    m_refs, refs = refs[4 : 4 + parts], refs[4 + parts :]
    if crossing:
        crossed_refs, refs = refs[:crossing], refs[crossing:]
        out_refs, refs = refs[:shards], refs[shards:]
    else:
        out_ref, refs = refs[0], refs[1:]
    table_ref, v_buf, m_sem, v_sem = refs[:4]
    refs = refs[4:]
    tile = v_ref.shape[-1]
    rows = 2 * tile
    for i in range(parts):
        pltpu.make_async_copy(m_refs[i].at[pl.ds(0, rows)], table_ref.at[pl.ds(i * rows, rows)], m_sem.at[i]).start()
    start_tiles(source_ref, count_ref, v_ref, v_buf, v_sem)
    if crossing:
        term_ref, cross_buf, cross_sem = refs
        each = shards // crossing
        for i in range(crossing):
            pltpu.make_async_copy(crossed_refs[i], cross_buf.at[pl.ds(i * each, each)], cross_sem.at[i]).start()
    blank = table_ref.at[pl.ds(parts * rows, tile)]
    blank[...] = jnp.zeros_like(blank)
    for i in range(parts):
        pltpu.make_async_copy(m_refs[i].at[pl.ds(0, rows)], table_ref.at[pl.ds(i * rows, rows)], m_sem.at[i]).wait()
    if crossing:
        for i in range(crossing):
            pltpu.make_async_copy(crossed_refs[i], cross_buf.at[pl.ds(i * each, each)], cross_sem.at[i]).wait()

    def group_step(k, carry):
        group = source_ref[k // 2] * 2 + k % 2
        i = k // 2
        at = pl.ds(pl.multiple_of(k % 2 * tile, tile), tile)

        def work(n):
            tiles_copy(v_ref, v_buf, v_sem, group, k, n).wait()
            tiles = v_buf[k, pl.ds(0, n)].reshape(n * tile, tile)
            found = []
            for m in range(n):
                target = target_ref[group, m]
                held = index_ref[at_turn + target // 2] * 2 + target % 2
                held = jnp.where(m < count_ref[group], held, 2 * parts)
                found.append(table_ref[pl.ds(pl.multiple_of(held * tile, tile), tile), :])
            found = jnp.concatenate(found, axis=0) if n > 1 else found[0]
            product = lax.dot_general(tiles, found, (((0,), (0,)), ((), ())), preferred_element_type=jnp.float32)
            if crossing:
                term_ref[i, at, :] = (product + cross_buf[i, at, :].astype(jnp.float32)).astype(jnp.bfloat16)
            else:
                out_ref[i, at, :] = product.astype(jnp.bfloat16)

        of_class(count_ref[group], work)
        return carry

    lax.fori_loop(0, 2 * shards, group_step, 0)
    if crossing:
        for i in range(shards):
            out_refs[i][...] = term_ref[i]


def share_kernel(*refs):
    m_refs, (sum_ref, w_buf, w_sem) = refs[:-3], refs[-3:]
    more = w_buf.shape[1]
    copies = [
        pltpu.make_async_copy(m_ref.at[pl.ds(m_ref.shape[0] - more, more)], w_buf.at[i], w_sem.at[i])
        for i, m_ref in enumerate(m_refs)
    ]
    for copy in copies:
        copy.start()
    total = None
    for i, copy in enumerate(copies):
        copy.wait()
        term = w_buf[i].astype(jnp.float32)
        total = term if total is None else total + term
    share = more - EXTRA
    sum_ref[pl.ds(0, share), :] = total[:share]
    bias = total[share : share + 1] + total[share + 1 : share + 2]
    rest = sum_ref.shape[0] - share
    sum_ref[pl.ds(share, rest), :] = jnp.broadcast_to(bias, (rest, bias.shape[1]))


def add_shares(messages, share):
    width = messages[0].shape[1]
    return pl.pallas_call(
        share_kernel,
        out_shape=jax.ShapeDtypeStruct((share + 8, width), jnp.float32),
        in_specs=[pl.BlockSpec(memory_space=pl.ANY)] * len(messages),
        out_specs=pl.BlockSpec(memory_space=pltpu.VMEM),
        scratch_shapes=[
            pltpu.VMEM((len(messages), share + EXTRA, width), jnp.bfloat16),
            pltpu.SemaphoreType.DMA((len(messages),)),
        ],
        compiler_params=pltpu.CompilerParams(vmem_limit_bytes=VMEM),
        cost_estimate=cost(1 << 20, 1 << 20),
        name="add_shares",
    )(*messages)


def split_rows(row):
    high = row.astype(jnp.bfloat16)
    low = (row - high.astype(jnp.float32)).astype(jnp.bfloat16)
    line = lax.broadcasted_iota(jnp.int32, (EXTRA, row.shape[1]), 0)
    spread_high = jnp.broadcast_to(high.astype(jnp.float32), line.shape)
    spread_low = jnp.broadcast_to(low.astype(jnp.float32), line.shape)
    return jnp.where(line == 0, spread_high, jnp.where(line == 1, spread_low, 0.0)).astype(jnp.bfloat16)


def spread(shards, at_source, at_turn, index, targets, counts, messages, values, crossed=()):
    parts = len(messages)
    width = messages[0].shape[1]
    slot_total, tile = values.shape[1:3]
    rows = 2 * tile
    anywhere = pl.BlockSpec(memory_space=pl.ANY)
    inside = pl.BlockSpec(memory_space=pltpu.VMEM)
    scratch = [
        pltpu.VMEM((parts * rows + tile, width), jnp.bfloat16),
        pltpu.VMEM((shards * 2, slot_total, tile, tile), jnp.bfloat16),
        pltpu.SemaphoreType.DMA((parts,)),
        pltpu.SemaphoreType.DMA((shards * 2,)),
    ]
    if crossed:
        out_shape = (jax.ShapeDtypeStruct((rows, width), jnp.bfloat16),) * shards
        scratch += [
            pltpu.VMEM((shards, rows, width), jnp.bfloat16),
            pltpu.VMEM((shards, rows, width), jnp.bfloat16),
            pltpu.SemaphoreType.DMA((len(crossed),)),
        ]
    else:
        out_shape = (jax.ShapeDtypeStruct((shards, rows, width), jnp.bfloat16),)
    return pl.pallas_call(
        lambda *refs: backward_kernel(
            shards, parts, at_source, at_turn, len(crossed), *refs
        ),
        out_shape=out_shape,
        grid_spec=pltpu.PrefetchScalarGridSpec(
            num_scalar_prefetch=3,
            grid=(),
            in_specs=[anywhere] * (1 + parts + len(crossed)),
            out_specs=(inside,) * len(out_shape),
            scratch_shapes=scratch,
        ),
        compiler_params=pltpu.CompilerParams(vmem_limit_bytes=VMEM),
        cost_estimate=cost(shards << 29, shards << 20),
        name="spread",
    )(index, targets, counts, values, *messages, *crossed)


def middle_kernel(parts, at_place, index_ref, *refs):
    place_ref = Window(index_ref, at_place, parts)
    part_refs, refs = refs[:parts], refs[parts:]
    weight_ref, bias_ref, cotangent_ref, out_ref = refs[:4]
    message_refs, part_ref = refs[4 : 4 + parts], refs[4 + parts]
    f32 = jnp.float32
    total = part_refs[0][...].astype(f32)
    for part in part_refs[1:]:
        total += part[...].astype(f32)
    rows = total.astype(jnp.bfloat16)
    shifted = jnp.dot(rows, weight_ref[...], preferred_element_type=f32) + bias_ref[...]
    logistic = jax.nn.sigmoid(shifted)
    out_ref[...] = (shifted * logistic).astype(jnp.bfloat16)
    derivative = logistic * (1.0 + shifted * (1.0 - logistic))
    grad = (cotangent_ref[...].astype(f32) * derivative).astype(jnp.bfloat16)
    back = lax.dot_general(
        grad, weight_ref[...], (((1,), (1,)), ((), ())), preferred_element_type=f32
    ).astype(jnp.bfloat16)
    part_ref[...] = lax.dot_general(rows, grad, (((0,), (0,)), ((), ())), preferred_element_type=f32)
    tail = split_rows(jnp.sum(grad.astype(f32), axis=0, keepdims=True))
    share = part_ref.shape[0] // parts
    high = back.shape[0]
    for i, message_ref in enumerate(message_refs):
        message_ref[pl.ds(0, high), :] = back
        at = pl.multiple_of(place_ref[i] * share, share)
        message_ref[pl.ds(high, share), :] = part_ref[pl.ds(at, share), :].astype(jnp.bfloat16)
        message_ref[pl.ds(high + share, EXTRA), :] = tail


def middle(at_place, index, sums, weight, layer_bias, cotangent):
    rows, width = cotangent.shape
    parts = len(sums)
    inside = pl.BlockSpec(memory_space=pltpu.VMEM)
    message = jax.ShapeDtypeStruct((rows + width // parts + EXTRA, width), jnp.bfloat16)
    return pl.pallas_call(
        lambda *refs: middle_kernel(parts, at_place, *refs),
        out_shape=(jax.ShapeDtypeStruct((rows, width), jnp.bfloat16),) + (message,) * parts,
        grid_spec=pltpu.PrefetchScalarGridSpec(
            num_scalar_prefetch=1,
            grid=(),
            in_specs=[inside] * (parts + 3),
            out_specs=(inside,) * (parts + 1),
            scratch_shapes=[pltpu.VMEM((width, width), jnp.float32)],
        ),
        compiler_params=pltpu.CompilerParams(vmem_limit_bytes=VMEM),
        cost_estimate=cost(1 << 30, 8 << 20),
        name="middle",
    )(index, *sums, weight, layer_bias[None, :], cotangent)


def place_kernel(scale, share, at_place, index_ref, *refs):
    place_ref = Window(index_ref, at_place, refs[-1].shape[0] // share)
    for i, piece in enumerate(refs[:-1]):
        for k in range(piece.shape[0] // share):
            at = pl.multiple_of(place_ref[2 * i + k] * share, share)
            refs[-1][pl.ds(at, share), :] = piece[pl.ds(k * share, share), :].astype(jnp.float32) * scale


def place(at_place, count, index, pieces, share, scale):
    width = pieces[0].shape[1]
    inside = pl.BlockSpec(memory_space=pltpu.VMEM)
    return pl.pallas_call(
        lambda *refs: place_kernel(scale, share, at_place, *refs),
        out_shape=jax.ShapeDtypeStruct((share * count, width), jnp.float32),
        grid_spec=pltpu.PrefetchScalarGridSpec(
            num_scalar_prefetch=1, grid=(), in_specs=[inside] * len(pieces), out_specs=inside
        ),
        compiler_params=pltpu.CompilerParams(vmem_limit_bytes=VMEM),
        name="place",
    )(index, *pieces)


CHIP_HALVES = (((0, 0), (0, 1), (0, 3), (1, 0)), ((0, 2), (1, 1), (1, 3), (1, 2)))


def lists_of_numbers(halves, chips, parts):
    table, begin = [], {}
    for place in itertools.product(*[range(n) for n in SIZES.values()]):
        at = dict(zip(SIZES, place))

        def number(axes, offsets, sign):
            flat = 0
            for axis, offset in zip(axes, offsets):
                flat = flat * SIZES[axis] + (at[axis] + sign * offset) % SIZES[axis]
            return flat

        core = at["core"]
        come = [number(CHIP, o, -1) * 2 for o in chips]
        go = [number(CHIP, o, 1) * 2 for o in halves[0] + halves[1]]
        lists = {
            "come": [c + core for c in come] + [c + 1 - core for c in come],
            "to": [number(REP, o, 1) for o in parts],
            "cross": [c + 1 - core for c in go],
            "stay": [c + core for c in go],
            "turn": [(at["xh"] - o[0]) % SIZES["xh"] * SIZES["y"] + (at["y"] - o[1]) % SIZES["y"] for o in parts],
            "piece": [number(REP, (k, o), -1) for o in range(SIZES["y"]) for k in range(SIZES["xh"])],
        }
        row = []
        for name, numbers in lists.items():
            begin[name] = len(row)
            row += numbers
        table.append(row)
    return np.asarray(table, np.int32), begin


def body(features, weight, layer_bias, tile_values, tile_target, tile_counts, cotangent):
    local_rows, width = features.shape
    values = tile_values[0, 0]
    targets = tile_target[0, 0]
    counts = tile_counts[0, 0]
    tile = values.shape[-1]
    slot_total = values.shape[1]
    assert local_rows == 2 * tile and slot_total == VARIANTS[-1]
    parts = all_offsets(REP)
    halves = CHIP_HALVES[::-1]
    chips = CHIP_HALVES[0] + CHIP_HALVES[1]
    y = SIZES["y"]
    table, begin = lists_of_numbers(halves, chips, parts)
    index = lax.dynamic_slice_in_dim(jnp.asarray(table), lax.axis_index(ALL), 1)[0]

    own = [send_by(features, CHIP, o) if any(o) else features for o in chips]
    crossed = [send_by(x, ("core",), (1,)) for x in own]
    partial = aggregate(begin["come"], begin["to"], len(parts), index, targets, counts, own + crossed, values)

    received = [send_by(partial[i], REP, o) if any(o) else partial[i] for i, o in enumerate(parts)]
    output, *messages = middle(begin["to"], index, received, weight, layer_bias, cotangent)
    messages = [send_by(messages[i], REP, o) if any(o) else messages[i] for i, o in enumerate(parts)]

    share = width // len(parts)
    share_sum = add_shares(messages, share)
    steps = (("xl", 1), ("z", 1), ("z", 2))
    across, each = [], len(halves[0])
    for i, step in enumerate(steps):
        index, share_sum = lax.optimization_barrier((index, share_sum))
        arriving = exchange(share_sum, *step)
        if i < 2:
            found = spread(each, begin["cross"] + each * i, begin["turn"], index, targets, counts, messages, values)
            across.append(send_by(found[0], ("core",), (1,)))
        else:
            found = spread(
                2 * each, begin["stay"], begin["turn"], index, targets, counts, messages, values, across
            )
        _, share_sum, arriving = lax.optimization_barrier((found, share_sum, arriving))
        share_sum = share_sum + arriving
    merged = found
    total = None
    for piece, o in zip(merged, halves[0] + halves[1]):
        piece = (send_by(piece, CHIP, o) if any(o) else piece).astype(jnp.float32)
        total = piece if total is None else total + piece
    grad_features = total.astype(jnp.bfloat16)

    share_sum = share_sum + exchange(share_sum, "core", 1)
    norm_scale = 1.0 / math.sqrt(local_rows * math.prod(SIZES.values()))
    grad_bias = share_sum[share] * norm_scale
    piece = share_sum[:share].astype(jnp.bfloat16)
    pair = jnp.concatenate([piece, send_by(piece, ("xh",), (1,))])
    pieces = [send_by(pair, ("y",), (o,)) if o else pair for o in range(y)]
    grad_weight = place(begin["piece"], len(parts), index, pieces, share, norm_scale)
    return (output, grad_features, grad_weight, grad_bias)


def solution(mesh):
    fine = Mesh(np.asarray(mesh.devices).reshape(tuple(SIZES.values())), tuple(SIZES))
    placed = (
        P(ALL, None),
        P(),
        P(),
        P(BLK, REP, None, None, None, None),
        P(BLK, REP, None, None),
        P(BLK, REP, None),
        P(ALL, None),
    )
    return jax.shard_map(
        body,
        mesh=fine,
        in_specs=placed,
        out_specs=(P(ALL, None), P(ALL, None), P(), P()),
        check_vma=False,
    )
```

```python
import itertools
import math

import jax
import jax.numpy as jnp
import numpy as np
from jax import lax
from jax.experimental import pallas as pl
from jax.experimental.pallas import tpu as pltpu
from jax.sharding import Mesh, PartitionSpec as P

SIZES = {"xl": 2, "z": 4, "core": 2, "xh": 2, "y": 4}
BLK = ("xl", "z", "core")
REP = ("xh", "y")
CHIP = ("xl", "z")
ALL = BLK + REP
VMEM = 26 << 20


def send_by(value, axes, offsets):
    sizes = [SIZES[a] for a in axes]
    pairs = []
    for at in itertools.product(*[range(n) for n in sizes]):
        to = [(i + o) % n for i, o, n in zip(at, offsets, sizes)]
        pairs.append((int(np.ravel_multi_index(at, sizes)), int(np.ravel_multi_index(to, sizes))))
    return lax.ppermute(value, axes, pairs)


def exchange(value, axis, mask):
    return lax.ppermute(value, axis, [(i, i ^ mask) for i in range(SIZES[axis])])


def all_offsets(axes):
    return list(itertools.product(*[range(SIZES[a]) for a in axes]))


EXTRA = 16
VARIANTS = (1, 2, 3, 4, 6, 8)


def cost(flops, transferred):
    return pl.CostEstimate(flops=flops, transcendentals=0, bytes_accessed=transferred)


class Window:
    def __init__(self, ref, base, length):
        self.ref, self.base, self.shape = ref, base, (length,)

    def __getitem__(self, i):
        return self.ref[self.base + i]


def of_class(count, action):
    low = 0
    for n in VARIANTS:

        @pl.when((count > low) & (count <= n))
        def _():
            action(n)

        low = n


def tiles_copy(v_ref, v_buf, sem, group, to, n):
    return pltpu.make_async_copy(v_ref.at[group, pl.ds(0, n)], v_buf.at[to, pl.ds(0, n)], sem.at[to])


def start_tiles(source_ref, count_ref, v_ref, v_buf, sem):
    def step(k, carry):
        group = source_ref[k // 2] * 2 + k % 2
        of_class(count_ref[group], lambda n: tiles_copy(v_ref, v_buf, sem, group, k, n).start())
        return carry

    lax.fori_loop(0, v_buf.shape[0], step, 0)


def forward_kernel(shards, at_source, at_place, index_ref, target_ref, count_ref, v_ref, *refs):
    source_ref = Window(index_ref, at_source, shards)
    place_ref = Window(index_ref, at_place, len(refs) - 5 - shards)
    x_refs, refs = refs[:shards], refs[shards:]
    acc_ref, x_buf, v_buf, x_sem, v_sem = refs[-5:]
    out_refs = refs[:-5]
    tile = v_ref.shape[-1]
    dummy = acc_ref.shape[0] - 1
    for i in range(shards):
        pltpu.make_async_copy(x_refs[i], x_buf.at[i], x_sem.at[i]).start()
    start_tiles(source_ref, count_ref, v_ref, v_buf, v_sem)
    acc_ref[...] = jnp.zeros_like(acc_ref)

    def group_step(k, carry):
        group = source_ref[k // 2] * 2 + k % 2

        @pl.when(k % 2 == 0)
        def _():
            pltpu.make_async_copy(x_refs[0], x_buf.at[k // 2], x_sem.at[k // 2]).wait()

        def work(n):
            tiles_copy(v_ref, v_buf, v_sem, group, k, n).wait()
            rows = x_buf[k // 2, pl.ds(pl.multiple_of(k % 2 * tile, tile), tile), :]
            tiles = v_buf[k, pl.ds(0, n)].reshape(n * tile, tile)
            product = jnp.dot(tiles, rows, preferred_element_type=jnp.float32)
            for m in range(n):
                to = jnp.where(m < count_ref[group], target_ref[m, group], dummy)
                acc_ref[to] += product[m * tile : (m + 1) * tile]

        of_class(count_ref[group], work)
        return carry

    lax.fori_loop(0, 2 * shards, group_step, 0)
    for i, out_ref in enumerate(out_refs):
        for t in range(2):
            out_ref[pl.ds(t * tile, tile), :] = acc_ref[place_ref[i] * 2 + t].astype(out_ref.dtype)


def aggregate(at_source, at_place, parts, index, targets, counts, gathered, values):
    shards = len(gathered)
    rows, width = gathered[0].shape
    _, slot_total, tile, _ = values.shape
    anywhere = pl.BlockSpec(memory_space=pl.ANY)
    inside = pl.BlockSpec(memory_space=pltpu.VMEM)
    return pl.pallas_call(
        lambda *refs: forward_kernel(shards, at_source, at_place, *refs),
        out_shape=(jax.ShapeDtypeStruct((rows, width), jnp.bfloat16),) * parts,
        grid_spec=pltpu.PrefetchScalarGridSpec(
            num_scalar_prefetch=3,
            grid=(),
            in_specs=[anywhere] * (1 + shards),
            out_specs=(inside,) * parts,
            scratch_shapes=[
                pltpu.VMEM((parts * 2 + 1, tile, width), jnp.float32),
                pltpu.VMEM((shards, rows, width), jnp.bfloat16),
                pltpu.VMEM((shards * 2, slot_total, tile, tile), jnp.bfloat16),
                pltpu.SemaphoreType.DMA((shards,)),
                pltpu.SemaphoreType.DMA((shards * 2,)),
            ],
        ),
        compiler_params=pltpu.CompilerParams(vmem_limit_bytes=VMEM),
        cost_estimate=cost(8 << 30, 16 << 20),
        name="aggregate",
    )(index, targets, counts, values, *gathered)


def backward_kernel(shards, parts, at_source, at_turn, crossing, *refs):
    index_ref, target_ref, count_ref, v_ref = refs[:4]
    source_ref = Window(index_ref, at_source, shards)
    m_refs, refs = refs[4 : 4 + parts], refs[4 + parts :]
    if crossing:
        crossed_refs, refs = refs[:crossing], refs[crossing:]
        out_refs, refs = refs[:shards], refs[shards:]
    else:
        out_ref, refs = refs[0], refs[1:]
    table_ref, v_buf, m_sem, v_sem = refs[:4]
    refs = refs[4:]
    tile = v_ref.shape[-1]
    rows = 2 * tile
    for i in range(parts):
        pltpu.make_async_copy(m_refs[i].at[pl.ds(0, rows)], table_ref.at[pl.ds(i * rows, rows)], m_sem.at[i]).start()
    start_tiles(source_ref, count_ref, v_ref, v_buf, v_sem)
    if crossing:
        term_ref, cross_buf, cross_sem = refs
        each = shards // crossing
        for i in range(crossing):
            pltpu.make_async_copy(crossed_refs[i], cross_buf.at[pl.ds(i * each, each)], cross_sem.at[i]).start()
    blank = table_ref.at[pl.ds(parts * rows, tile)]
    blank[...] = jnp.zeros_like(blank)
    for i in range(parts):
        pltpu.make_async_copy(m_refs[i].at[pl.ds(0, rows)], table_ref.at[pl.ds(i * rows, rows)], m_sem.at[i]).wait()
    if crossing:
        for i in range(crossing):
            pltpu.make_async_copy(crossed_refs[i], cross_buf.at[pl.ds(i * each, each)], cross_sem.at[i]).wait()

    def group_step(k, carry):
        group = source_ref[k // 2] * 2 + k % 2
        i = k // 2
        at = pl.ds(pl.multiple_of(k % 2 * tile, tile), tile)

        def work(n):
            tiles_copy(v_ref, v_buf, v_sem, group, k, n).wait()
            tiles = v_buf[k, pl.ds(0, n)].reshape(n * tile, tile)
            found = []
            for m in range(n):
                target = target_ref[m, group]
                held = index_ref[at_turn + target // 2] * 2 + target % 2
                held = jnp.where(m < count_ref[group], held, 2 * parts)
                found.append(table_ref[pl.ds(pl.multiple_of(held * tile, tile), tile), :])
            found = jnp.concatenate(found, axis=0) if n > 1 else found[0]
            product = lax.dot_general(tiles, found, (((0,), (0,)), ((), ())), preferred_element_type=jnp.float32)
            if crossing:
                term_ref[i, at, :] = (product + cross_buf[i, at, :].astype(jnp.float32)).astype(jnp.bfloat16)
            else:
                out_ref[i, at, :] = product.astype(jnp.bfloat16)

        of_class(count_ref[group], work)
        return carry

    lax.fori_loop(0, 2 * shards, group_step, 0)
    if crossing:
        for i in range(shards):
            out_refs[i][...] = term_ref[i]


def share_kernel(*refs):
    m_refs, (sum_ref, w_buf, w_sem) = refs[:-3], refs[-3:]
    more = w_buf.shape[1]
    copies = [
        pltpu.make_async_copy(m_ref.at[pl.ds(m_ref.shape[0] - more, more)], w_buf.at[i], w_sem.at[i])
        for i, m_ref in enumerate(m_refs)
    ]
    for copy in copies:
        copy.start()
    total = None
    for i, copy in enumerate(copies):
        copy.wait()
        term = w_buf[i].astype(jnp.float32)
        total = term if total is None else total + term
    share = more - EXTRA
    sum_ref[pl.ds(0, share), :] = total[:share]
    bias = total[share : share + 1] + total[share + 1 : share + 2]
    rest = sum_ref.shape[0] - share
    sum_ref[pl.ds(share, rest), :] = jnp.broadcast_to(bias, (rest, bias.shape[1]))


def add_shares(messages, share):
    width = messages[0].shape[1]
    return pl.pallas_call(
        share_kernel,
        out_shape=jax.ShapeDtypeStruct((share + 8, width), jnp.float32),
        in_specs=[pl.BlockSpec(memory_space=pl.ANY)] * len(messages),
        out_specs=pl.BlockSpec(memory_space=pltpu.VMEM),
        scratch_shapes=[
            pltpu.VMEM((len(messages), share + EXTRA, width), jnp.bfloat16),
            pltpu.SemaphoreType.DMA((len(messages),)),
        ],
        compiler_params=pltpu.CompilerParams(vmem_limit_bytes=VMEM),
        cost_estimate=cost(1 << 20, 1 << 20),
        name="add_shares",
    )(*messages)


def split_rows(row):
    high = row.astype(jnp.bfloat16)
    low = (row - high.astype(jnp.float32)).astype(jnp.bfloat16)
    line = lax.broadcasted_iota(jnp.int32, (EXTRA, row.shape[1]), 0)
    spread_high = jnp.broadcast_to(high.astype(jnp.float32), line.shape)
    spread_low = jnp.broadcast_to(low.astype(jnp.float32), line.shape)
    return jnp.where(line == 0, spread_high, jnp.where(line == 1, spread_low, 0.0)).astype(jnp.bfloat16)


def spread(shards, at_source, at_turn, index, targets, counts, messages, values, crossed=()):
    parts = len(messages)
    width = messages[0].shape[1]
    slot_total, tile = values.shape[1:3]
    rows = 2 * tile
    anywhere = pl.BlockSpec(memory_space=pl.ANY)
    inside = pl.BlockSpec(memory_space=pltpu.VMEM)
    scratch = [
        pltpu.VMEM((parts * rows + tile, width), jnp.bfloat16),
        pltpu.VMEM((shards * 2, slot_total, tile, tile), jnp.bfloat16),
        pltpu.SemaphoreType.DMA((parts,)),
        pltpu.SemaphoreType.DMA((shards * 2,)),
    ]
    if crossed:
        out_shape = (jax.ShapeDtypeStruct((rows, width), jnp.bfloat16),) * shards
        scratch += [
            pltpu.VMEM((shards, rows, width), jnp.bfloat16),
            pltpu.VMEM((shards, rows, width), jnp.bfloat16),
            pltpu.SemaphoreType.DMA((len(crossed),)),
        ]
    else:
        out_shape = (jax.ShapeDtypeStruct((shards, rows, width), jnp.bfloat16),)
    return pl.pallas_call(
        lambda *refs: backward_kernel(
            shards, parts, at_source, at_turn, len(crossed), *refs
        ),
        out_shape=out_shape,
        grid_spec=pltpu.PrefetchScalarGridSpec(
            num_scalar_prefetch=3,
            grid=(),
            in_specs=[anywhere] * (1 + parts + len(crossed)),
            out_specs=(inside,) * len(out_shape),
            scratch_shapes=scratch,
        ),
        compiler_params=pltpu.CompilerParams(vmem_limit_bytes=VMEM),
        cost_estimate=cost(shards << 32, shards << 20),
        name="spread",
    )(index, targets, counts, values, *messages, *crossed)


def middle_kernel(parts, at_place, index_ref, *refs):
    place_ref = Window(index_ref, at_place, parts)
    part_refs, refs = refs[:parts], refs[parts:]
    weight_ref, bias_ref, cotangent_ref, out_ref = refs[:4]
    message_refs, part_ref = refs[4 : 4 + parts], refs[4 + parts]
    f32 = jnp.float32
    total = part_refs[0][...].astype(f32)
    for part in part_refs[1:]:
        total += part[...].astype(f32)
    rows = total.astype(jnp.bfloat16)
    shifted = jnp.dot(rows, weight_ref[...], preferred_element_type=f32) + bias_ref[...]
    logistic = jax.nn.sigmoid(shifted)
    out_ref[...] = (shifted * logistic).astype(jnp.bfloat16)
    derivative = logistic * (1.0 + shifted * (1.0 - logistic))
    grad = (cotangent_ref[...].astype(f32) * derivative).astype(jnp.bfloat16)
    back = lax.dot_general(
        grad, weight_ref[...], (((1,), (1,)), ((), ())), preferred_element_type=f32
    ).astype(jnp.bfloat16)
    part_ref[...] = lax.dot_general(rows, grad, (((0,), (0,)), ((), ())), preferred_element_type=f32)
    tail = split_rows(jnp.sum(grad.astype(f32), axis=0, keepdims=True))
    share = part_ref.shape[0] // parts
    high = back.shape[0]
    for i, message_ref in enumerate(message_refs):
        message_ref[pl.ds(0, high), :] = back
        at = pl.multiple_of(place_ref[i] * share, share)
        message_ref[pl.ds(high, share), :] = part_ref[pl.ds(at, share), :].astype(jnp.bfloat16)
        message_ref[pl.ds(high + share, EXTRA), :] = tail


def middle(at_place, index, sums, weight, layer_bias, cotangent):
    rows, width = cotangent.shape
    parts = len(sums)
    inside = pl.BlockSpec(memory_space=pltpu.VMEM)
    message = jax.ShapeDtypeStruct((rows + width // parts + EXTRA, width), jnp.bfloat16)
    return pl.pallas_call(
        lambda *refs: middle_kernel(parts, at_place, *refs),
        out_shape=(jax.ShapeDtypeStruct((rows, width), jnp.bfloat16),) + (message,) * parts,
        grid_spec=pltpu.PrefetchScalarGridSpec(
            num_scalar_prefetch=1,
            grid=(),
            in_specs=[inside] * (parts + 3),
            out_specs=(inside,) * (parts + 1),
            scratch_shapes=[pltpu.VMEM((width, width), jnp.float32)],
        ),
        compiler_params=pltpu.CompilerParams(vmem_limit_bytes=VMEM),
        cost_estimate=cost(1 << 30, 8 << 20),
        name="middle",
    )(index, *sums, weight, layer_bias[None, :], cotangent)


def place_kernel(scale, share, at_place, index_ref, *refs):
    place_ref = Window(index_ref, at_place, refs[-1].shape[0] // share)
    for i, piece in enumerate(refs[:-1]):
        for k in range(piece.shape[0] // share):
            at = pl.multiple_of(place_ref[2 * i + k] * share, share)
            refs[-1][pl.ds(at, share), :] = piece[pl.ds(k * share, share), :].astype(jnp.float32) * scale


def place(at_place, count, index, pieces, share, scale):
    width = pieces[0].shape[1]
    inside = pl.BlockSpec(memory_space=pltpu.VMEM)
    return pl.pallas_call(
        lambda *refs: place_kernel(scale, share, at_place, *refs),
        out_shape=jax.ShapeDtypeStruct((share * count, width), jnp.float32),
        grid_spec=pltpu.PrefetchScalarGridSpec(
            num_scalar_prefetch=1, grid=(), in_specs=[inside] * len(pieces), out_specs=inside
        ),
        compiler_params=pltpu.CompilerParams(vmem_limit_bytes=VMEM),
        name="place",
    )(index, *pieces)


CHIP_HALVES = (((0, 0), (0, 1), (0, 3), (1, 0)), ((0, 2), (1, 1), (1, 3), (1, 2)))


def lists_of_numbers(halves, chips, parts):
    table, begin = [], {}
    for place in itertools.product(*[range(n) for n in SIZES.values()]):
        at = dict(zip(SIZES, place))

        def number(axes, offsets, sign):
            flat = 0
            for axis, offset in zip(axes, offsets):
                flat = flat * SIZES[axis] + (at[axis] + sign * offset) % SIZES[axis]
            return flat

        core = at["core"]
        come = [number(CHIP, o, -1) * 2 for o in chips]
        go = [number(CHIP, o, 1) * 2 for o in halves[0] + halves[1]]
        lists = {
            "come": [c + core for c in come] + [c + 1 - core for c in come],
            "to": [number(REP, o, 1) for o in parts],
            "cross": [c + 1 - core for c in go],
            "stay": [c + core for c in go],
            "turn": [(at["xh"] - o[0]) % SIZES["xh"] * SIZES["y"] + (at["y"] - o[1]) % SIZES["y"] for o in parts],
            "piece": [number(REP, (k, o), -1) for o in range(SIZES["y"]) for k in range(SIZES["xh"])],
        }
        row = []
        for name, numbers in lists.items():
            begin[name] = len(row)
            row += numbers
        table.append(row)
    return np.asarray(table, np.int32), begin


def body(features, weight, layer_bias, tile_values, tile_target, tile_counts, cotangent):
    local_rows, width = features.shape
    values = tile_values[0, 0]
    targets = tile_target[0, 0].T
    counts = tile_counts[0, 0]
    tile = values.shape[-1]
    slot_total = values.shape[1]
    assert local_rows == 2 * tile and slot_total == VARIANTS[-1]
    parts = all_offsets(REP)
    halves = CHIP_HALVES[::-1]
    chips = CHIP_HALVES[0] + CHIP_HALVES[1]
    y = SIZES["y"]
    table, begin = lists_of_numbers(halves, chips, parts)
    index = lax.dynamic_slice_in_dim(jnp.asarray(table), lax.axis_index(ALL), 1)[0]

    own = [send_by(features, CHIP, o) if any(o) else features for o in chips]
    index, own[1] = lax.optimization_barrier((index, own[1]))
    crossed = [send_by(x, ("core",), (1,)) for x in own]
    partial = aggregate(begin["come"], begin["to"], len(parts), index, targets, counts, own + crossed, values)

    received = [send_by(partial[i], REP, o) if any(o) else partial[i] for i, o in enumerate(parts)]
    output, *messages = middle(begin["to"], index, received, weight, layer_bias, cotangent)
    messages = [send_by(messages[i], REP, o) if any(o) else messages[i] for i, o in enumerate(parts)]

    share = width // len(parts)
    share_sum = add_shares(messages, share)
    each = len(halves[0])
    across, merged = [], []
    for i, step in enumerate((("xl", 1), ("z", 1), ("z", 2), ("xh", 1))):
        index, share_sum = lax.optimization_barrier((index, share_sum))
        arriving = exchange(share_sum, *step)
        k = i % 2
        if i < 2:
            found = spread(each, begin["cross"] + each * k, begin["turn"], index, targets, counts, messages, values)
            across.append(send_by(found[0], ("core",), (1,)))
        else:
            found = spread(
                each, begin["stay"] + each * k, begin["turn"], index, targets, counts, messages, values, across[k : k + 1]
            )
            merged += found
        _, share_sum, arriving = lax.optimization_barrier((found, share_sum, arriving))
        if i < 3:
            share_sum = share_sum + arriving
        if i == 2:
            share_sum = share_sum + exchange(share_sum, "core", 1)
    total = None
    for piece, o in zip(merged, halves[0] + halves[1]):
        piece = (send_by(piece, CHIP, o) if any(o) else piece).astype(jnp.float32)
        total = piece if total is None else total + piece
    grad_features = total.astype(jnp.bfloat16)

    norm_scale = 1.0 / math.sqrt(local_rows * math.prod(SIZES.values()))
    grad_bias = share_sum[share] * norm_scale
    pair = jnp.concatenate([share_sum[:share], arriving[:share]]).astype(jnp.bfloat16)
    pieces = [send_by(pair, ("y",), (o,)) if o else pair for o in range(y)]
    grad_weight = place(begin["piece"], len(parts), index, pieces, share, norm_scale)
    return (output, grad_features, grad_weight, grad_bias)


def solution(mesh):
    fine = Mesh(np.asarray(mesh.devices).reshape(tuple(SIZES.values())), tuple(SIZES))
    placed = (
        P(ALL, None),
        P(),
        P(),
        P(BLK, REP, None, None, None, None),
        P(BLK, REP, None, None),
        P(BLK, REP, None),
        P(ALL, None),
    )
    return jax.shard_map(
        body,
        mesh=fine,
        in_specs=placed,
        out_specs=(P(ALL, None), P(ALL, None), P(), P()),
        check_vma=False,
    )
```

```python
import itertools
import math

import jax
import jax.numpy as jnp
import numpy as np
from jax import lax
from jax.experimental import pallas as pl
from jax.experimental.pallas import tpu as pltpu
from jax.sharding import Mesh, PartitionSpec as P

SIZES = {"xl": 2, "z": 4, "core": 2, "xh": 2, "y": 4}
BLK = ("xl", "z", "core")
REP = ("xh", "y")
CHIP = ("xl", "z")
ALL = BLK + REP
VMEM = 26 << 20


def send_by(value, axes, offsets):
    sizes = [SIZES[a] for a in axes]
    pairs = []
    for at in itertools.product(*[range(n) for n in sizes]):
        to = [(i + o) % n for i, o, n in zip(at, offsets, sizes)]
        pairs.append((int(np.ravel_multi_index(at, sizes)), int(np.ravel_multi_index(to, sizes))))
    return lax.ppermute(value, axes, pairs)


def exchange(value, axis, mask):
    return lax.ppermute(value, axis, [(i, i ^ mask) for i in range(SIZES[axis])])


def all_offsets(axes):
    return list(itertools.product(*[range(SIZES[a]) for a in axes]))


EXTRA = 16
VARIANTS = (1, 2, 3, 4, 6, 8)


def cost(flops, transferred):
    return pl.CostEstimate(flops=flops, transcendentals=0, bytes_accessed=transferred)


class Window:
    def __init__(self, ref, base, length):
        self.ref, self.base, self.shape = ref, base, (length,)

    def __getitem__(self, i):
        return self.ref[self.base + i]


def of_class(count, action):
    low = 0
    for n in VARIANTS:

        @pl.when((count > low) & (count <= n))
        def _():
            action(n)

        low = n


def fetch_kernel(index_ref, v_ref, out_ref, again_ref, sem):
    parts = sem.shape[0]
    each = v_ref.shape[0] // parts
    copies = [
        pltpu.make_async_copy(v_ref.at[pl.ds(i * each, each)], out_ref.at[pl.ds(i * each, each)], sem.at[i])
        for i in range(parts)
    ]
    for copy in copies:
        copy.start()
    for copy in copies:
        copy.wait()
    for i in range(index_ref.shape[0]):
        again_ref[i] = index_ref[i]


def fetch(values, index):
    return pl.pallas_call(
        fetch_kernel,
        out_shape=(pltpu.VMEM(values.shape, values.dtype), jax.ShapeDtypeStruct(index.shape, index.dtype)),
        in_specs=[pl.BlockSpec(memory_space=pltpu.SMEM), pl.BlockSpec(memory_space=pl.ANY)],
        out_specs=(pl.BlockSpec(memory_space=pltpu.VMEM), pl.BlockSpec(memory_space=pltpu.SMEM)),
        scratch_shapes=[pltpu.SemaphoreType.DMA((8,))],
        compiler_params=pltpu.CompilerParams(vmem_limit_bytes=VMEM),
        cost_estimate=cost(0, 16 << 20),
        name="fetch",
    )(index, pltpu.with_memory_space_constraint(values, pltpu.HBM))


def forward_kernel(shards, at_source, at_place, index_ref, target_ref, count_ref, v_ref, *refs):
    source_ref = Window(index_ref, at_source, shards)
    place_ref = Window(index_ref, at_place, len(refs) - 2 - shards)
    x_refs, refs = refs[:shards], refs[shards:]
    acc_ref, x_buf = refs[-2:]
    out_refs = refs[:-2]
    tile = v_ref.shape[-1]
    dummy = acc_ref.shape[0] - 1
    for i in range(shards):
        x_buf[i] = x_refs[i][...]
    acc_ref[...] = jnp.zeros_like(acc_ref)

    def group_step(k, carry):
        group = source_ref[k // 2] * 2 + k % 2

        def work(n):
            rows = x_buf[k // 2, pl.ds(pl.multiple_of(k % 2 * tile, tile), tile), :]
            tiles = v_ref[group, pl.ds(0, n)].reshape(n * tile, tile)
            product = jnp.dot(tiles, rows, preferred_element_type=jnp.float32)
            for m in range(n):
                to = jnp.where(m < count_ref[group], target_ref[m, group], dummy)
                acc_ref[to] += product[m * tile : (m + 1) * tile]

        of_class(count_ref[group], work)
        return carry

    lax.fori_loop(0, 2 * shards, group_step, 0)
    for i, out_ref in enumerate(out_refs):
        for t in range(2):
            out_ref[pl.ds(t * tile, tile), :] = acc_ref[place_ref[i] * 2 + t].astype(out_ref.dtype)


def aggregate(at_source, at_place, parts, index, targets, counts, gathered, values):
    shards = len(gathered)
    rows, width = gathered[0].shape
    tile = values.shape[-1]
    inside = pl.BlockSpec(memory_space=pltpu.VMEM)
    return pl.pallas_call(
        lambda *refs: forward_kernel(shards, at_source, at_place, *refs),
        out_shape=(jax.ShapeDtypeStruct((rows, width), jnp.bfloat16),) * parts,
        grid_spec=pltpu.PrefetchScalarGridSpec(
            num_scalar_prefetch=3,
            grid=(),
            in_specs=[inside] * (1 + shards),
            out_specs=(inside,) * parts,
            scratch_shapes=[
                pltpu.VMEM((parts * 2 + 1, tile, width), jnp.float32),
                pltpu.VMEM((shards, rows, width), jnp.bfloat16),
            ],
        ),
        compiler_params=pltpu.CompilerParams(vmem_limit_bytes=VMEM),
        cost_estimate=cost(8 << 30, 16 << 20),
        name="aggregate",
    )(index, targets, counts, pltpu.with_memory_space_constraint(values, pltpu.VMEM), *gathered)


def backward_kernel(shards, parts, at_source, at_turn, crossing, *refs):
    index_ref, target_ref, count_ref, v_ref = refs[:4]
    source_ref = Window(index_ref, at_source, shards)
    m_refs, refs = refs[4 : 4 + parts], refs[4 + parts :]
    if crossing:
        crossed_refs, refs = refs[:crossing], refs[crossing:]
        out_refs, refs = refs[:shards], refs[shards:]
    else:
        out_ref, refs = refs[0], refs[1:]
    table_ref = refs[0]
    tile = v_ref.shape[-1]
    rows = 2 * tile
    for i in range(parts):
        table_ref[pl.ds(i * rows, rows), :] = m_refs[i][pl.ds(0, rows), :]
    blank = table_ref.at[pl.ds(parts * rows, tile)]
    blank[...] = jnp.zeros_like(blank)
    if crossing:
        term_ref = refs[1]

    def group_step(k, carry):
        group = source_ref[k // 2] * 2 + k % 2
        i = k // 2
        at = pl.ds(pl.multiple_of(k % 2 * tile, tile), tile)

        def work(n):
            tiles = v_ref[group, pl.ds(0, n)].reshape(n * tile, tile)
            found = []
            for m in range(n):
                target = target_ref[m, group]
                held = index_ref[at_turn + target // 2] * 2 + target % 2
                held = jnp.where(m < count_ref[group], held, 2 * parts)
                found.append(table_ref[pl.ds(pl.multiple_of(held * tile, tile), tile), :])
            found = jnp.concatenate(found, axis=0) if n > 1 else found[0]
            product = lax.dot_general(tiles, found, (((0,), (0,)), ((), ())), preferred_element_type=jnp.float32)
            if crossing:
                term_ref[i, at, :] = (product + crossed_refs[0][i, at, :].astype(jnp.float32)).astype(jnp.bfloat16)
            else:
                out_ref[i, at, :] = product.astype(jnp.bfloat16)

        of_class(count_ref[group], work)
        return carry

    lax.fori_loop(0, 2 * shards, group_step, 0)
    if crossing:
        for i in range(shards):
            out_refs[i][...] = term_ref[i]


def share_kernel(*refs):
    m_refs, sum_ref = refs[:-1], refs[-1]
    share = sum_ref.shape[0] - 8
    more = share + EXTRA
    total = None
    for m_ref in m_refs:
        term = m_ref[pl.ds(m_ref.shape[0] - more, more), :].astype(jnp.float32)
        total = term if total is None else total + term
    sum_ref[pl.ds(0, share), :] = total[:share]
    bias = total[share : share + 1] + total[share + 1 : share + 2]
    sum_ref[pl.ds(share, 8), :] = jnp.broadcast_to(bias, (8, bias.shape[1]))


def add_shares(messages, share):
    width = messages[0].shape[1]
    return pl.pallas_call(
        share_kernel,
        out_shape=jax.ShapeDtypeStruct((share + 8, width), jnp.float32),
        in_specs=[pl.BlockSpec(memory_space=pltpu.VMEM)] * len(messages),
        out_specs=pl.BlockSpec(memory_space=pltpu.VMEM),
        compiler_params=pltpu.CompilerParams(vmem_limit_bytes=VMEM),
        cost_estimate=cost(1 << 20, 1 << 20),
        name="add_shares",
    )(*messages)


def split_rows(row):
    high = row.astype(jnp.bfloat16)
    low = (row - high.astype(jnp.float32)).astype(jnp.bfloat16)
    line = lax.broadcasted_iota(jnp.int32, (EXTRA, row.shape[1]), 0)
    spread_high = jnp.broadcast_to(high.astype(jnp.float32), line.shape)
    spread_low = jnp.broadcast_to(low.astype(jnp.float32), line.shape)
    return jnp.where(line == 0, spread_high, jnp.where(line == 1, spread_low, 0.0)).astype(jnp.bfloat16)


def spread(shards, at_source, at_turn, index, targets, counts, messages, values, crossed=()):
    parts = len(messages)
    width = messages[0].shape[1]
    tile = values.shape[-1]
    rows = 2 * tile
    inside = pl.BlockSpec(memory_space=pltpu.VMEM)
    scratch = [pltpu.VMEM((parts * rows + tile, width), jnp.bfloat16)]
    if crossed:
        out_shape = (jax.ShapeDtypeStruct((rows, width), jnp.bfloat16),) * shards
        scratch.append(pltpu.VMEM((shards, rows, width), jnp.bfloat16))
    else:
        out_shape = (jax.ShapeDtypeStruct((shards, rows, width), jnp.bfloat16),)
    return pl.pallas_call(
        lambda *refs: backward_kernel(
            shards, parts, at_source, at_turn, len(crossed), *refs
        ),
        out_shape=out_shape,
        grid_spec=pltpu.PrefetchScalarGridSpec(
            num_scalar_prefetch=3,
            grid=(),
            in_specs=[inside] * (1 + parts + len(crossed)),
            out_specs=(inside,) * len(out_shape),
            scratch_shapes=scratch,
        ),
        compiler_params=pltpu.CompilerParams(vmem_limit_bytes=VMEM),
        cost_estimate=cost(shards << 32, shards << 20),
        name="spread",
    )(index, targets, counts, pltpu.with_memory_space_constraint(values, pltpu.VMEM), *messages, *crossed)


def middle_kernel(parts, at_place, index_ref, *refs):
    place_ref = Window(index_ref, at_place, parts)
    part_refs, refs = refs[:parts], refs[parts:]
    weight_ref, bias_ref, cotangent_ref, out_ref = refs[:4]
    message_refs, part_ref = refs[4 : 4 + parts], refs[4 + parts]
    f32 = jnp.float32
    total = part_refs[0][...].astype(f32)
    for part in part_refs[1:]:
        total += part[...].astype(f32)
    rows = total.astype(jnp.bfloat16)
    shifted = jnp.dot(rows, weight_ref[...], preferred_element_type=f32) + bias_ref[...]
    logistic = jax.nn.sigmoid(shifted)
    out_ref[...] = (shifted * logistic).astype(jnp.bfloat16)
    derivative = logistic * (1.0 + shifted * (1.0 - logistic))
    grad = (cotangent_ref[...].astype(f32) * derivative).astype(jnp.bfloat16)
    back = lax.dot_general(
        grad, weight_ref[...], (((1,), (1,)), ((), ())), preferred_element_type=f32
    ).astype(jnp.bfloat16)
    part_ref[...] = lax.dot_general(rows, grad, (((0,), (0,)), ((), ())), preferred_element_type=f32)
    tail = split_rows(jnp.sum(grad.astype(f32), axis=0, keepdims=True))
    share = part_ref.shape[0] // parts
    high = back.shape[0]
    for i, message_ref in enumerate(message_refs):
        message_ref[pl.ds(0, high), :] = back
        at = pl.multiple_of(place_ref[i] * share, share)
        message_ref[pl.ds(high, share), :] = part_ref[pl.ds(at, share), :].astype(jnp.bfloat16)
        message_ref[pl.ds(high + share, EXTRA), :] = tail


def middle(at_place, index, sums, weight, layer_bias, cotangent):
    rows, width = cotangent.shape
    parts = len(sums)
    inside = pl.BlockSpec(memory_space=pltpu.VMEM)
    message = jax.ShapeDtypeStruct((rows + width // parts + EXTRA, width), jnp.bfloat16)
    return pl.pallas_call(
        lambda *refs: middle_kernel(parts, at_place, *refs),
        out_shape=(jax.ShapeDtypeStruct((rows, width), jnp.bfloat16),) + (message,) * parts,
        grid_spec=pltpu.PrefetchScalarGridSpec(
            num_scalar_prefetch=1,
            grid=(),
            in_specs=[inside] * (parts + 3),
            out_specs=(inside,) * (parts + 1),
            scratch_shapes=[pltpu.VMEM((width, width), jnp.float32)],
        ),
        compiler_params=pltpu.CompilerParams(vmem_limit_bytes=VMEM),
        cost_estimate=cost(1 << 30, 8 << 20),
        name="middle",
    )(index, *sums, weight, layer_bias[None, :], cotangent)


def place_kernel(scale, share, at_place, index_ref, *refs):
    place_ref = Window(index_ref, at_place, refs[-1].shape[0] // share)
    for i, piece in enumerate(refs[:-1]):
        for k in range(piece.shape[0] // share):
            at = pl.multiple_of(place_ref[2 * i + k] * share, share)
            refs[-1][pl.ds(at, share), :] = piece[pl.ds(k * share, share), :].astype(jnp.float32) * scale


def place(at_place, count, index, pieces, share, scale):
    width = pieces[0].shape[1]
    inside = pl.BlockSpec(memory_space=pltpu.VMEM)
    return pl.pallas_call(
        lambda *refs: place_kernel(scale, share, at_place, *refs),
        out_shape=jax.ShapeDtypeStruct((share * count, width), jnp.float32),
        grid_spec=pltpu.PrefetchScalarGridSpec(
            num_scalar_prefetch=1, grid=(), in_specs=[inside] * len(pieces), out_specs=inside
        ),
        compiler_params=pltpu.CompilerParams(vmem_limit_bytes=VMEM),
        name="place",
    )(index, *pieces)


CHIP_HALVES = (((0, 0), (0, 1), (0, 3), (1, 0)), ((0, 2), (1, 1), (1, 3), (1, 2)))


def lists_of_numbers(halves, chips, parts):
    table, begin = [], {}
    for place in itertools.product(*[range(n) for n in SIZES.values()]):
        at = dict(zip(SIZES, place))

        def number(axes, offsets, sign):
            flat = 0
            for axis, offset in zip(axes, offsets):
                flat = flat * SIZES[axis] + (at[axis] + sign * offset) % SIZES[axis]
            return flat

        core = at["core"]
        come = [number(CHIP, o, -1) * 2 for o in chips]
        go = [number(CHIP, o, 1) * 2 for o in halves[0] + halves[1]]
        lists = {
            "come": [c + core for c in come] + [c + 1 - core for c in come],
            "to": [number(REP, o, 1) for o in parts],
            "cross": [c + 1 - core for c in go],
            "stay": [c + core for c in go],
            "turn": [(at["xh"] - o[0]) % SIZES["xh"] * SIZES["y"] + (at["y"] - o[1]) % SIZES["y"] for o in parts],
            "piece": [number(REP, (k, o), -1) for o in range(SIZES["y"]) for k in range(SIZES["xh"])],
        }
        row = []
        for name, numbers in lists.items():
            begin[name] = len(row)
            row += numbers
        table.append(row)
    return np.asarray(table, np.int32), begin


def body(features, weight, layer_bias, tile_values, tile_target, tile_counts, cotangent):
    local_rows, width = features.shape
    values = tile_values[0, 0]
    targets = tile_target[0, 0].T
    counts = tile_counts[0, 0]
    tile = values.shape[-1]
    slot_total = values.shape[1]
    assert local_rows == 2 * tile and slot_total == VARIANTS[-1]
    parts = all_offsets(REP)
    halves = CHIP_HALVES[::-1]
    chips = CHIP_HALVES[0] + CHIP_HALVES[1]
    y = SIZES["y"]
    table, begin = lists_of_numbers(halves, chips, parts)
    index = lax.dynamic_slice_in_dim(jnp.asarray(table), lax.axis_index(ALL), 1)[0]

    own = [send_by(features, CHIP, o) if any(o) else features for o in chips]
    values, index = fetch(values, index)
    index, own[1] = lax.optimization_barrier((index, own[1]))
    crossed = [send_by(x, ("core",), (1,)) for x in own]
    partial = aggregate(begin["come"], begin["to"], len(parts), index, targets, counts, own + crossed, values)

    received = [send_by(partial[i], REP, o) if any(o) else partial[i] for i, o in enumerate(parts)]
    output, *messages = middle(begin["to"], index, received, weight, layer_bias, cotangent)
    messages = [send_by(messages[i], REP, o) if any(o) else messages[i] for i, o in enumerate(parts)]

    share = width // len(parts)
    share_sum = add_shares(messages, share)
    each = len(halves[0])
    across, merged = [], []
    for i, step in enumerate((("xl", 1), ("z", 1), ("z", 2), ("xh", 1))):
        index, share_sum = lax.optimization_barrier((index, share_sum))
        arriving = exchange(share_sum, *step)
        k = i % 2
        if i < 2:
            found = spread(each, begin["cross"] + each * k, begin["turn"], index, targets, counts, messages, values)
            across.append(send_by(found[0], ("core",), (1,)))
        else:
            found = spread(
                each, begin["stay"] + each * k, begin["turn"], index, targets, counts, messages, values, across[k : k + 1]
            )
            merged += found
        _, share_sum, arriving = lax.optimization_barrier((found, share_sum, arriving))
        if i < 3:
            share_sum = share_sum + arriving
        if i == 2:
            share_sum = share_sum + exchange(share_sum, "core", 1)
    total = None
    for piece, o in zip(merged, halves[0] + halves[1]):
        piece = (send_by(piece, CHIP, o) if any(o) else piece).astype(jnp.float32)
        total = piece if total is None else total + piece
    grad_features = total.astype(jnp.bfloat16)

    norm_scale = 1.0 / math.sqrt(local_rows * math.prod(SIZES.values()))
    grad_bias = share_sum[share] * norm_scale
    pair = jnp.concatenate([share_sum[:share], arriving[:share]]).astype(jnp.bfloat16)
    pieces = [send_by(pair, ("y",), (o,)) if o else pair for o in range(y)]
    grad_weight = place(begin["piece"], len(parts), index, pieces, share, norm_scale)
    return (output, grad_features, grad_weight, grad_bias)


def solution(mesh):
    fine = Mesh(np.asarray(mesh.devices).reshape(tuple(SIZES.values())), tuple(SIZES))
    placed = (
        P(ALL, None),
        P(),
        P(),
        P(BLK, REP, None, None, None, None),
        P(BLK, REP, None, None),
        P(BLK, REP, None),
        P(ALL, None),
    )
    return jax.shard_map(
        body,
        mesh=fine,
        in_specs=placed,
        out_specs=(P(ALL, None), P(ALL, None), P(), P()),
        check_vma=False,
    )
```

```python
import itertools
import math

import jax
import jax.numpy as jnp
import numpy as np
from jax import lax
from jax.experimental import pallas as pl
from jax.experimental.pallas import tpu as pltpu
from jax.sharding import Mesh, PartitionSpec as P

SIZES = {"xl": 2, "z": 4, "core": 2, "xh": 2, "y": 4}
BLK = ("xl", "z", "core")
REP = ("xh", "y")
CHIP = ("xl", "z")
ALL = BLK + REP
VMEM = 26 << 20


def send_by(value, axes, offsets):
    sizes = [SIZES[a] for a in axes]
    pairs = []
    for at in itertools.product(*[range(n) for n in sizes]):
        to = [(i + o) % n for i, o, n in zip(at, offsets, sizes)]
        pairs.append((int(np.ravel_multi_index(at, sizes)), int(np.ravel_multi_index(to, sizes))))
    return lax.ppermute(value, axes, pairs)


def exchange(value, axis, mask):
    return lax.ppermute(value, axis, [(i, i ^ mask) for i in range(SIZES[axis])])


def all_offsets(axes):
    return list(itertools.product(*[range(SIZES[a]) for a in axes]))


EXTRA = 16
VARIANTS = (1, 2, 3, 4, 6, 8)


def cost(flops, transferred):
    return pl.CostEstimate(flops=flops, transcendentals=0, bytes_accessed=transferred)


class Window:
    def __init__(self, ref, base, length):
        self.ref, self.base, self.shape = ref, base, (length,)

    def __getitem__(self, i):
        return self.ref[self.base + i]


def of_class(count, action):
    low = 0
    for n in VARIANTS:

        @pl.when((count > low) & (count <= n))
        def _():
            action(n)

        low = n


def fetch_kernel(index_ref, v_ref, out_ref, again_ref, sem):
    parts = sem.shape[0]
    each = v_ref.shape[0] // parts
    copies = [
        pltpu.make_async_copy(v_ref.at[pl.ds(i * each, each)], out_ref.at[pl.ds(i * each, each)], sem.at[i])
        for i in range(parts)
    ]
    for copy in copies:
        copy.start()
    for copy in copies:
        copy.wait()
    for i in range(index_ref.shape[0]):
        again_ref[i] = index_ref[i]


def fetch(values, index):
    return pl.pallas_call(
        fetch_kernel,
        out_shape=(pltpu.VMEM(values.shape, values.dtype), jax.ShapeDtypeStruct(index.shape, index.dtype)),
        in_specs=[pl.BlockSpec(memory_space=pltpu.SMEM), pl.BlockSpec(memory_space=pl.ANY)],
        out_specs=(pl.BlockSpec(memory_space=pltpu.VMEM), pl.BlockSpec(memory_space=pltpu.SMEM)),
        scratch_shapes=[pltpu.SemaphoreType.DMA((8,))],
        compiler_params=pltpu.CompilerParams(vmem_limit_bytes=VMEM),
        cost_estimate=cost(0, 16 << 20),
        name="fetch",
    )(index, pltpu.with_memory_space_constraint(values, pltpu.HBM))


def forward_kernel(shards, at_source, at_place, index_ref, target_ref, count_ref, v_ref, *refs):
    source_ref = Window(index_ref, at_source, shards)
    place_ref = Window(index_ref, at_place, len(refs) - 2 - shards)
    x_refs, refs = refs[:shards], refs[shards:]
    acc_ref, x_buf = refs[-2:]
    out_refs = refs[:-2]
    tile = v_ref.shape[-1]
    dummy = acc_ref.shape[0] - 1
    for i in range(shards):
        x_buf[i] = x_refs[i][...]
    acc_ref[...] = jnp.zeros_like(acc_ref)

    def group_step(k, carry):
        group = source_ref[k // 2] * 2 + k % 2

        def work(n):
            rows = x_buf[k // 2, pl.ds(pl.multiple_of(k % 2 * tile, tile), tile), :]
            tiles = v_ref[group, pl.ds(0, n)].reshape(n * tile, tile)
            product = jnp.dot(tiles, rows, preferred_element_type=jnp.float32)
            for m in range(n):
                to = jnp.where(m < count_ref[group], target_ref[m, group], dummy)
                acc_ref[to] += product[m * tile : (m + 1) * tile]

        of_class(count_ref[group], work)
        return carry

    lax.fori_loop(0, 2 * shards, group_step, 0)
    for i, out_ref in enumerate(out_refs):
        for t in range(2):
            out_ref[pl.ds(t * tile, tile), :] = acc_ref[place_ref[i] * 2 + t].astype(out_ref.dtype)


def aggregate(at_source, at_place, parts, index, targets, counts, gathered, values):
    shards = len(gathered)
    rows, width = gathered[0].shape
    tile = values.shape[-1]
    inside = pl.BlockSpec(memory_space=pltpu.VMEM)
    return pl.pallas_call(
        lambda *refs: forward_kernel(shards, at_source, at_place, *refs),
        out_shape=(jax.ShapeDtypeStruct((rows, width), jnp.bfloat16),) * parts,
        grid_spec=pltpu.PrefetchScalarGridSpec(
            num_scalar_prefetch=3,
            grid=(),
            in_specs=[inside] * (1 + shards),
            out_specs=(inside,) * parts,
            scratch_shapes=[
                pltpu.VMEM((parts * 2 + 1, tile, width), jnp.float32),
                pltpu.VMEM((shards, rows, width), jnp.bfloat16),
            ],
        ),
        compiler_params=pltpu.CompilerParams(vmem_limit_bytes=VMEM),
        cost_estimate=cost(8 << 30, 16 << 20),
        name="aggregate",
    )(index, targets, counts, pltpu.with_memory_space_constraint(values, pltpu.VMEM), *gathered)


def backward_kernel(shards, parts, at_source, at_turn, crossing, *refs):
    index_ref, target_ref, count_ref, v_ref = refs[:4]
    source_ref = Window(index_ref, at_source, shards)
    m_refs, refs = refs[4 : 4 + parts], refs[4 + parts :]
    if crossing:
        crossed_refs, refs = refs[:crossing], refs[crossing:]
        out_refs, refs = refs[:shards], refs[shards:]
    else:
        out_ref, refs = refs[0], refs[1:]
    table_ref = refs[0]
    tile = v_ref.shape[-1]
    rows = 2 * tile
    for i in range(parts):
        table_ref[pl.ds(i * rows, rows), :] = m_refs[i][pl.ds(0, rows), :]
    blank = table_ref.at[pl.ds(parts * rows, tile)]
    blank[...] = jnp.zeros_like(blank)
    if crossing:
        term_ref = refs[1]

    def group_step(k, carry):
        group = source_ref[k // 2] * 2 + k % 2
        i = k // 2
        at = pl.ds(pl.multiple_of(k % 2 * tile, tile), tile)

        def work(n):
            tiles = v_ref[group, pl.ds(0, n)].reshape(n * tile, tile)
            found = []
            for m in range(n):
                target = target_ref[m, group]
                held = index_ref[at_turn + target // 2] * 2 + target % 2
                held = jnp.where(m < count_ref[group], held, 2 * parts)
                found.append(table_ref[pl.ds(pl.multiple_of(held * tile, tile), tile), :])
            found = jnp.concatenate(found, axis=0) if n > 1 else found[0]
            product = lax.dot_general(tiles, found, (((0,), (0,)), ((), ())), preferred_element_type=jnp.float32)
            if crossing:
                term_ref[i, at, :] = (product + crossed_refs[0][i, at, :].astype(jnp.float32)).astype(jnp.bfloat16)
            else:
                out_ref[i, at, :] = product.astype(jnp.bfloat16)

        of_class(count_ref[group], work)
        return carry

    lax.fori_loop(0, 2 * shards, group_step, 0)
    if crossing:
        for i in range(shards):
            out_refs[i][...] = term_ref[i]


def share_kernel(*refs):
    m_refs, sum_ref = refs[:-1], refs[-1]
    share = sum_ref.shape[0] - 8
    more = share + EXTRA
    total = None
    for m_ref in m_refs:
        term = m_ref[pl.ds(m_ref.shape[0] - more, more), :].astype(jnp.float32)
        total = term if total is None else total + term
    sum_ref[pl.ds(0, share), :] = total[:share]
    bias = total[share : share + 1] + total[share + 1 : share + 2]
    sum_ref[pl.ds(share, 8), :] = jnp.broadcast_to(bias, (8, bias.shape[1]))


def add_shares(messages, share):
    width = messages[0].shape[1]
    return pl.pallas_call(
        share_kernel,
        out_shape=jax.ShapeDtypeStruct((share + 8, width), jnp.float32),
        in_specs=[pl.BlockSpec(memory_space=pltpu.VMEM)] * len(messages),
        out_specs=pl.BlockSpec(memory_space=pltpu.VMEM),
        compiler_params=pltpu.CompilerParams(vmem_limit_bytes=VMEM),
        cost_estimate=cost(1 << 20, 1 << 20),
        name="add_shares",
    )(*messages)


def split_rows(row):
    high = row.astype(jnp.bfloat16)
    low = (row - high.astype(jnp.float32)).astype(jnp.bfloat16)
    line = lax.broadcasted_iota(jnp.int32, (EXTRA, row.shape[1]), 0)
    spread_high = jnp.broadcast_to(high.astype(jnp.float32), line.shape)
    spread_low = jnp.broadcast_to(low.astype(jnp.float32), line.shape)
    return jnp.where(line == 0, spread_high, jnp.where(line == 1, spread_low, 0.0)).astype(jnp.bfloat16)


def spread(shards, at_source, at_turn, index, targets, counts, messages, values, crossed=()):
    parts = len(messages)
    width = messages[0].shape[1]
    tile = values.shape[-1]
    rows = 2 * tile
    inside = pl.BlockSpec(memory_space=pltpu.VMEM)
    scratch = [pltpu.VMEM((parts * rows + tile, width), jnp.bfloat16)]
    if crossed:
        out_shape = (jax.ShapeDtypeStruct((rows, width), jnp.bfloat16),) * shards
        scratch.append(pltpu.VMEM((shards, rows, width), jnp.bfloat16))
    else:
        out_shape = (jax.ShapeDtypeStruct((shards, rows, width), jnp.bfloat16),)
    return pl.pallas_call(
        lambda *refs: backward_kernel(
            shards, parts, at_source, at_turn, len(crossed), *refs
        ),
        out_shape=out_shape,
        grid_spec=pltpu.PrefetchScalarGridSpec(
            num_scalar_prefetch=3,
            grid=(),
            in_specs=[inside] * (1 + parts + len(crossed)),
            out_specs=(inside,) * len(out_shape),
            scratch_shapes=scratch,
        ),
        compiler_params=pltpu.CompilerParams(vmem_limit_bytes=VMEM),
        cost_estimate=cost(shards << 32, shards << 20),
        name="spread",
    )(index, targets, counts, pltpu.with_memory_space_constraint(values, pltpu.VMEM), *messages, *crossed)


def middle_kernel(parts, at_place, index_ref, *refs):
    place_ref = Window(index_ref, at_place, parts)
    part_refs, refs = refs[:parts], refs[parts:]
    weight_ref, bias_ref, cotangent_ref, out_ref = refs[:4]
    message_refs, part_ref = refs[4 : 4 + parts], refs[4 + parts]
    f32 = jnp.float32
    total = part_refs[0][...].astype(f32)
    for part in part_refs[1:]:
        total += part[...].astype(f32)
    rows = total.astype(jnp.bfloat16)
    shifted = jnp.dot(rows, weight_ref[...], preferred_element_type=f32) + bias_ref[...]
    logistic = jax.nn.sigmoid(shifted)
    out_ref[...] = (shifted * logistic).astype(jnp.bfloat16)
    derivative = logistic * (1.0 + shifted * (1.0 - logistic))
    grad = (cotangent_ref[...].astype(f32) * derivative).astype(jnp.bfloat16)
    back = lax.dot_general(
        grad, weight_ref[...], (((1,), (1,)), ((), ())), preferred_element_type=f32
    ).astype(jnp.bfloat16)
    part_ref[...] = lax.dot_general(rows, grad, (((0,), (0,)), ((), ())), preferred_element_type=f32)
    tail = split_rows(jnp.sum(grad.astype(f32), axis=0, keepdims=True))
    share = part_ref.shape[0] // parts
    high = back.shape[0]
    for i, message_ref in enumerate(message_refs):
        message_ref[pl.ds(0, high), :] = back
        at = pl.multiple_of(place_ref[i] * share, share)
        message_ref[pl.ds(high, share), :] = part_ref[pl.ds(at, share), :].astype(jnp.bfloat16)
        message_ref[pl.ds(high + share, EXTRA), :] = tail


def middle(at_place, index, sums, weight, layer_bias, cotangent):
    rows, width = cotangent.shape
    parts = len(sums)
    inside = pl.BlockSpec(memory_space=pltpu.VMEM)
    message = jax.ShapeDtypeStruct((rows + width // parts + EXTRA, width), jnp.bfloat16)
    return pl.pallas_call(
        lambda *refs: middle_kernel(parts, at_place, *refs),
        out_shape=(jax.ShapeDtypeStruct((rows, width), jnp.bfloat16),) + (message,) * parts,
        grid_spec=pltpu.PrefetchScalarGridSpec(
            num_scalar_prefetch=1,
            grid=(),
            in_specs=[inside] * (parts + 3),
            out_specs=(inside,) * (parts + 1),
            scratch_shapes=[pltpu.VMEM((width, width), jnp.float32)],
        ),
        compiler_params=pltpu.CompilerParams(vmem_limit_bytes=VMEM),
        cost_estimate=cost(1 << 30, 8 << 20),
        name="middle",
    )(index, *sums, weight, layer_bias[None, :], cotangent)


def place_kernel(scale, share, at_place, index_ref, *refs):
    place_ref = Window(index_ref, at_place, refs[-1].shape[0] // share)
    for i, piece in enumerate(refs[:-1]):
        for k in range(piece.shape[0] // share):
            at = pl.multiple_of(place_ref[2 * i + k] * share, share)
            refs[-1][pl.ds(at, share), :] = piece[pl.ds(k * share, share), :].astype(jnp.float32) * scale


def place(at_place, count, index, pieces, share, scale):
    width = pieces[0].shape[1]
    inside = pl.BlockSpec(memory_space=pltpu.VMEM)
    return pl.pallas_call(
        lambda *refs: place_kernel(scale, share, at_place, *refs),
        out_shape=jax.ShapeDtypeStruct((share * count, width), jnp.float32),
        grid_spec=pltpu.PrefetchScalarGridSpec(
            num_scalar_prefetch=1, grid=(), in_specs=[inside] * len(pieces), out_specs=inside
        ),
        compiler_params=pltpu.CompilerParams(vmem_limit_bytes=VMEM),
        name="place",
    )(index, *pieces)


PARTS = ((0, 0), (0, 1), (0, 3), (1, 0), (1, 2), (0, 2), (1, 1), (1, 3))
CHIP_HALVES = (((0, 0), (0, 1), (0, 3), (1, 0)), ((0, 2), (1, 1), (1, 3), (1, 2)))


def lists_of_numbers(halves, chips, parts):
    table, begin = [], {}
    for place in itertools.product(*[range(n) for n in SIZES.values()]):
        at = dict(zip(SIZES, place))

        def number(axes, offsets, sign):
            flat = 0
            for axis, offset in zip(axes, offsets):
                flat = flat * SIZES[axis] + (at[axis] + sign * offset) % SIZES[axis]
            return flat

        core = at["core"]
        come = [number(CHIP, o, -1) * 2 for o in chips]
        go = [number(CHIP, o, 1) * 2 for o in halves[0] + halves[1]]
        lists = {
            "come": [c + core for c in come] + [c + 1 - core for c in come],
            "to": [number(REP, o, 1) for o in parts],
            "cross": [c + 1 - core for c in go],
            "stay": [c + core for c in go],
            "turn": [
                parts.index(((at["xh"] - h) % SIZES["xh"], (at["y"] - y) % SIZES["y"])) for h, y in all_offsets(REP)
            ],
            "piece": [number(REP, (k, o), -1) for o in range(SIZES["y"]) for k in range(SIZES["xh"])],
        }
        row = []
        for name, numbers in lists.items():
            begin[name] = len(row)
            row += numbers
        table.append(row)
    return np.asarray(table, np.int32), begin


def body(features, weight, layer_bias, tile_values, tile_target, tile_counts, cotangent):
    local_rows, width = features.shape
    values = tile_values[0, 0]
    targets = tile_target[0, 0].T
    counts = tile_counts[0, 0]
    tile = values.shape[-1]
    slot_total = values.shape[1]
    assert local_rows == 2 * tile and slot_total == VARIANTS[-1]
    parts = list(PARTS)
    halves = CHIP_HALVES[::-1]
    chips = CHIP_HALVES[0] + CHIP_HALVES[1]
    y = SIZES["y"]
    table, begin = lists_of_numbers(halves, chips, parts)
    index = lax.dynamic_slice_in_dim(jnp.asarray(table), lax.axis_index(ALL), 1)[0]

    own = [send_by(features, CHIP, o) if any(o) else features for o in chips]
    values, index = fetch(values, index)
    index, own[1] = lax.optimization_barrier((index, own[1]))
    crossed = [send_by(x, ("core",), (1,)) for x in own]
    partial = aggregate(begin["come"], begin["to"], len(parts), index, targets, counts, own + crossed, values)

    received = [send_by(partial[i], REP, o) if any(o) else partial[i] for i, o in enumerate(parts)]
    output, *messages = middle(begin["to"], index, received, weight, layer_bias, cotangent)
    messages = [send_by(messages[i], REP, o) if any(o) else messages[i] for i, o in enumerate(parts)]

    share = width // len(parts)
    share_sum = add_shares(messages, share)
    each = len(halves[0])
    across, merged = [], []
    for i, step in enumerate((("xl", 1), ("z", 1), ("z", 2), None)):
        if step:
            index, share_sum = lax.optimization_barrier((index, share_sum))
            arriving = exchange(share_sum, *step)
        k = i % 2
        if i < 2:
            found = spread(each, begin["cross"] + each * k, begin["turn"], index, targets, counts, messages, values)
            across.append(send_by(found[0], ("core",), (1,)))
        else:
            found = spread(
                each, begin["stay"] + each * k, begin["turn"], index, targets, counts, messages, values, across[k : k + 1]
            )
            merged += found
        if step:
            _, share_sum, arriving = lax.optimization_barrier((found, share_sum, arriving))
            share_sum = share_sum + arriving
    last = [send_by(piece, CHIP, o) if any(o) else piece for piece, o in zip(merged, halves[0] + halves[1])]
    _, share_sum = lax.optimization_barrier((found, share_sum))
    share_sum = share_sum + exchange(share_sum, "core", 1)
    arriving = exchange(share_sum, "xh", 1)
    arriving, last[5] = lax.optimization_barrier((arriving, last[5]))
    total = None
    for piece in last:
        piece = piece.astype(jnp.float32)
        total = piece if total is None else total + piece
    grad_features = total.astype(jnp.bfloat16)

    norm_scale = 1.0 / math.sqrt(local_rows * math.prod(SIZES.values()))
    grad_bias = share_sum[share] * norm_scale
    pair = jnp.concatenate([share_sum[:share], arriving[:share]]).astype(jnp.bfloat16)
    pieces = [send_by(pair, ("y",), (o,)) if o else pair for o in range(y)]
    grad_weight = place(begin["piece"], len(parts), index, pieces, share, norm_scale)
    return (output, grad_features, grad_weight, grad_bias)


def solution(mesh):
    fine = Mesh(np.asarray(mesh.devices).reshape(tuple(SIZES.values())), tuple(SIZES))
    placed = (
        P(ALL, None),
        P(),
        P(),
        P(BLK, REP, None, None, None, None),
        P(BLK, REP, None, None),
        P(BLK, REP, None),
        P(ALL, None),
    )
    return jax.shard_map(
        body,
        mesh=fine,
        in_specs=placed,
        out_specs=(P(ALL, None), P(ALL, None), P(), P()),
        check_vma=False,
    )
```

```python
import itertools
import math

import jax
import jax.numpy as jnp
import numpy as np
from jax import lax
from jax.experimental import pallas as pl
from jax.experimental.pallas import tpu as pltpu
from jax.sharding import Mesh, PartitionSpec as P

SIZES = {"xl": 2, "z": 4, "core": 2, "xh": 2, "y": 4}
BLK = ("xl", "z", "core")
REP = ("xh", "y")
CHIP = ("xl", "z")
ALL = BLK + REP
VMEM = 26 << 20


def send_by(value, axes, offsets):
    sizes = [SIZES[a] for a in axes]
    pairs = []
    for at in itertools.product(*[range(n) for n in sizes]):
        to = [(i + o) % n for i, o, n in zip(at, offsets, sizes)]
        pairs.append((int(np.ravel_multi_index(at, sizes)), int(np.ravel_multi_index(to, sizes))))
    return lax.ppermute(value, axes, pairs)


def exchange(value, axis, mask):
    return lax.ppermute(value, axis, [(i, i ^ mask) for i in range(SIZES[axis])])


def all_offsets(axes):
    return list(itertools.product(*[range(SIZES[a]) for a in axes]))


EXTRA = 8
VARIANTS = (1, 2, 3, 4, 6, 8)


def cost(flops, transferred):
    return pl.CostEstimate(flops=flops, transcendentals=0, bytes_accessed=transferred)


class Window:
    def __init__(self, ref, base, length):
        self.ref, self.base, self.shape = ref, base, (length,)

    def __getitem__(self, i):
        return self.ref[self.base + i]


def of_class(count, action):
    low = 0
    for n in VARIANTS:

        @pl.when((count > low) & (count <= n))
        def _():
            action(n)

        low = n


def fetch_kernel(index_ref, v_ref, out_ref, again_ref, sem):
    parts = sem.shape[0]
    each = v_ref.shape[0] // parts
    copies = [
        pltpu.make_async_copy(v_ref.at[pl.ds(i * each, each)], out_ref.at[pl.ds(i * each, each)], sem.at[i])
        for i in range(parts)
    ]
    for copy in copies:
        copy.start()
    for copy in copies:
        copy.wait()
    for i in range(index_ref.shape[0]):
        again_ref[i] = index_ref[i]


def fetch(values, index):
    return pl.pallas_call(
        fetch_kernel,
        out_shape=(pltpu.VMEM(values.shape, values.dtype), jax.ShapeDtypeStruct(index.shape, index.dtype)),
        in_specs=[pl.BlockSpec(memory_space=pltpu.SMEM), pl.BlockSpec(memory_space=pl.ANY)],
        out_specs=(pl.BlockSpec(memory_space=pltpu.VMEM), pl.BlockSpec(memory_space=pltpu.SMEM)),
        scratch_shapes=[pltpu.SemaphoreType.DMA((8,))],
        compiler_params=pltpu.CompilerParams(vmem_limit_bytes=VMEM),
        cost_estimate=cost(0, 16 << 20),
        name="fetch",
    )(index, pltpu.with_memory_space_constraint(values, pltpu.HBM))


def forward_kernel(shards, at_source, at_place, index_ref, target_ref, count_ref, v_ref, *refs):
    source_ref = Window(index_ref, at_source, shards)
    place_ref = Window(index_ref, at_place, len(refs) - 2 - shards)
    x_refs, refs = refs[:shards], refs[shards:]
    acc_ref, x_buf = refs[-2:]
    out_refs = refs[:-2]
    tile = v_ref.shape[-1]
    dummy = acc_ref.shape[0] - 1
    for i in range(shards):
        x_buf[i] = x_refs[i][...]
    acc_ref[...] = jnp.zeros_like(acc_ref)

    def group_step(k, carry):
        group = source_ref[k // 2] * 2 + k % 2

        def work(n):
            rows = x_buf[k // 2, pl.ds(pl.multiple_of(k % 2 * tile, tile), tile), :]
            tiles = v_ref[group, pl.ds(0, n)].reshape(n * tile, tile)
            product = jnp.dot(tiles, rows, preferred_element_type=jnp.float32)
            for m in range(n):
                to = jnp.where(m < count_ref[group], target_ref[m, group], dummy)
                acc_ref[to] += product[m * tile : (m + 1) * tile]

        of_class(count_ref[group], work)
        return carry

    lax.fori_loop(0, 2 * shards, group_step, 0)
    for i, out_ref in enumerate(out_refs):
        for t in range(2):
            out_ref[pl.ds(t * tile, tile), :] = acc_ref[place_ref[i] * 2 + t].astype(out_ref.dtype)


def aggregate(at_source, at_place, parts, index, targets, counts, gathered, values):
    shards = len(gathered)
    rows, width = gathered[0].shape
    tile = values.shape[-1]
    inside = pl.BlockSpec(memory_space=pltpu.VMEM)
    return pl.pallas_call(
        lambda *refs: forward_kernel(shards, at_source, at_place, *refs),
        out_shape=(jax.ShapeDtypeStruct((rows, width), jnp.bfloat16),) * parts,
        grid_spec=pltpu.PrefetchScalarGridSpec(
            num_scalar_prefetch=3,
            grid=(),
            in_specs=[inside] * (1 + shards),
            out_specs=(inside,) * parts,
            scratch_shapes=[
                pltpu.VMEM((parts * 2 + 1, tile, width), jnp.float32),
                pltpu.VMEM((shards, rows, width), jnp.bfloat16),
            ],
        ),
        compiler_params=pltpu.CompilerParams(vmem_limit_bytes=VMEM),
        cost_estimate=cost(8 << 30, 16 << 20),
        name="aggregate",
    )(index, targets, counts, pltpu.with_memory_space_constraint(values, pltpu.VMEM), *gathered)


def backward_kernel(shards, parts, at_source, at_turn, crossing, *refs):
    index_ref, target_ref, count_ref, v_ref = refs[:4]
    source_ref = Window(index_ref, at_source, shards)
    m_refs, refs = refs[4 : 4 + parts], refs[4 + parts :]
    if crossing:
        crossed_refs, refs = refs[:crossing], refs[crossing:]
        out_refs, refs = refs[:shards], refs[shards:]
    else:
        out_ref, refs = refs[0], refs[1:]
    table_ref = refs[0]
    tile = v_ref.shape[-1]
    rows = 2 * tile
    for i in range(parts):
        table_ref[pl.ds(i * rows, rows), :] = m_refs[i][pl.ds(0, rows), :]
    blank = table_ref.at[pl.ds(parts * rows, tile)]
    blank[...] = jnp.zeros_like(blank)
    if crossing:
        term_ref = refs[1]

    def group_step(k, carry):
        group = source_ref[k // 2] * 2 + k % 2
        i = k // 2
        at = pl.ds(pl.multiple_of(k % 2 * tile, tile), tile)

        def work(n):
            tiles = v_ref[group, pl.ds(0, n)].reshape(n * tile, tile)
            found = []
            for m in range(n):
                target = target_ref[m, group]
                held = index_ref[at_turn + target // 2] * 2 + target % 2
                held = jnp.where(m < count_ref[group], held, 2 * parts)
                found.append(table_ref[pl.ds(pl.multiple_of(held * tile, tile), tile), :])
            found = jnp.concatenate(found, axis=0) if n > 1 else found[0]
            product = lax.dot_general(tiles, found, (((0,), (0,)), ((), ())), preferred_element_type=jnp.float32)
            if crossing:
                term_ref[i, at, :] = (product + crossed_refs[0][i, at, :].astype(jnp.float32)).astype(jnp.bfloat16)
            else:
                out_ref[i, at, :] = product.astype(jnp.bfloat16)

        of_class(count_ref[group], work)
        return carry

    lax.fori_loop(0, 2 * shards, group_step, 0)
    if crossing:
        for i in range(shards):
            out_refs[i][...] = term_ref[i]


def share_kernel(*refs):
    m_refs, sum_ref = refs[:-1], refs[-1]
    share = sum_ref.shape[0] - 8
    more = share + EXTRA
    total = None
    for m_ref in m_refs:
        term = m_ref[pl.ds(m_ref.shape[0] - more, more), :].astype(jnp.float32)
        total = term if total is None else total + term
    sum_ref[pl.ds(0, share), :] = total[:share]
    bias = total[share : share + 1] + total[share + 1 : share + 2]
    sum_ref[pl.ds(share, 8), :] = jnp.broadcast_to(bias, (8, bias.shape[1]))


def add_shares(messages, share):
    width = messages[0].shape[1]
    return pl.pallas_call(
        share_kernel,
        out_shape=jax.ShapeDtypeStruct((share + 8, width), jnp.float32),
        in_specs=[pl.BlockSpec(memory_space=pltpu.VMEM)] * len(messages),
        out_specs=pl.BlockSpec(memory_space=pltpu.VMEM),
        compiler_params=pltpu.CompilerParams(vmem_limit_bytes=VMEM),
        cost_estimate=cost(1 << 20, 1 << 20),
        name="add_shares",
    )(*messages)


def split_rows(row):
    high = row.astype(jnp.bfloat16)
    low = (row - high.astype(jnp.float32)).astype(jnp.bfloat16)
    line = lax.broadcasted_iota(jnp.int32, (EXTRA, row.shape[1]), 0)
    spread_high = jnp.broadcast_to(high.astype(jnp.float32), line.shape)
    spread_low = jnp.broadcast_to(low.astype(jnp.float32), line.shape)
    return jnp.where(line == 0, spread_high, jnp.where(line == 1, spread_low, 0.0)).astype(jnp.bfloat16)


def spread(shards, at_source, at_turn, index, targets, counts, messages, values, crossed=()):
    parts = len(messages)
    width = messages[0].shape[1]
    tile = values.shape[-1]
    rows = 2 * tile
    inside = pl.BlockSpec(memory_space=pltpu.VMEM)
    scratch = [pltpu.VMEM((parts * rows + tile, width), jnp.bfloat16)]
    if crossed:
        out_shape = (jax.ShapeDtypeStruct((rows, width), jnp.bfloat16),) * shards
        scratch.append(pltpu.VMEM((shards, rows, width), jnp.bfloat16))
    else:
        out_shape = (jax.ShapeDtypeStruct((shards, rows, width), jnp.bfloat16),)
    return pl.pallas_call(
        lambda *refs: backward_kernel(
            shards, parts, at_source, at_turn, len(crossed), *refs
        ),
        out_shape=out_shape,
        grid_spec=pltpu.PrefetchScalarGridSpec(
            num_scalar_prefetch=3,
            grid=(),
            in_specs=[inside] * (1 + parts + len(crossed)),
            out_specs=(inside,) * len(out_shape),
            scratch_shapes=scratch,
        ),
        compiler_params=pltpu.CompilerParams(vmem_limit_bytes=VMEM),
        cost_estimate=cost(shards << 32, shards << 20),
        name="spread",
    )(index, targets, counts, pltpu.with_memory_space_constraint(values, pltpu.VMEM), *messages, *crossed)


def middle_kernel(parts, at_place, index_ref, *refs):
    place_ref = Window(index_ref, at_place, parts)
    part_refs, refs = refs[:parts], refs[parts:]
    weight_ref, bias_ref, cotangent_ref, out_ref = refs[:4]
    message_refs, part_ref = refs[4 : 4 + parts], refs[4 + parts]
    f32 = jnp.float32
    total = part_refs[0][...].astype(f32)
    for part in part_refs[1:]:
        total += part[...].astype(f32)
    rows = total.astype(jnp.bfloat16)
    shifted = jnp.dot(rows, weight_ref[...], preferred_element_type=f32) + bias_ref[...]
    logistic = jax.nn.sigmoid(shifted)
    out_ref[...] = (shifted * logistic).astype(jnp.bfloat16)
    derivative = logistic * (1.0 + shifted * (1.0 - logistic))
    grad = (cotangent_ref[...].astype(f32) * derivative).astype(jnp.bfloat16)
    back = lax.dot_general(
        grad, weight_ref[...], (((1,), (1,)), ((), ())), preferred_element_type=f32
    ).astype(jnp.bfloat16)
    part_ref[...] = lax.dot_general(rows, grad, (((0,), (0,)), ((), ())), preferred_element_type=f32)
    tail = split_rows(jnp.sum(grad.astype(f32), axis=0, keepdims=True))
    share = part_ref.shape[0] // parts
    high = back.shape[0]
    for i, message_ref in enumerate(message_refs):
        message_ref[pl.ds(0, high), :] = back
        at = pl.multiple_of(place_ref[i] * share, share)
        message_ref[pl.ds(high, share), :] = part_ref[pl.ds(at, share), :].astype(jnp.bfloat16)
        message_ref[pl.ds(high + share, EXTRA), :] = tail


def middle(at_place, index, sums, weight, layer_bias, cotangent):
    rows, width = cotangent.shape
    parts = len(sums)
    inside = pl.BlockSpec(memory_space=pltpu.VMEM)
    message = jax.ShapeDtypeStruct((rows + width // parts + EXTRA, width), jnp.bfloat16)
    return pl.pallas_call(
        lambda *refs: middle_kernel(parts, at_place, *refs),
        out_shape=(jax.ShapeDtypeStruct((rows, width), jnp.bfloat16),) + (message,) * parts,
        grid_spec=pltpu.PrefetchScalarGridSpec(
            num_scalar_prefetch=1,
            grid=(),
            in_specs=[inside] * (parts + 3),
            out_specs=(inside,) * (parts + 1),
            scratch_shapes=[pltpu.VMEM((width, width), jnp.float32)],
        ),
        compiler_params=pltpu.CompilerParams(vmem_limit_bytes=VMEM),
        cost_estimate=cost(1 << 30, 8 << 20),
        name="middle",
    )(index, *sums, weight, layer_bias[None, :], cotangent)


def place_kernel(scale, share, at_place, index_ref, *refs):
    place_ref = Window(index_ref, at_place, refs[-1].shape[0] // share)
    for i, piece in enumerate(refs[:-1]):
        for k in range(piece.shape[0] // share):
            at = pl.multiple_of(place_ref[2 * i + k] * share, share)
            refs[-1][pl.ds(at, share), :] = piece[pl.ds(k * share, share), :].astype(jnp.float32) * scale


def place(at_place, count, index, pieces, share, scale):
    width = pieces[0].shape[1]
    inside = pl.BlockSpec(memory_space=pltpu.VMEM)
    return pl.pallas_call(
        lambda *refs: place_kernel(scale, share, at_place, *refs),
        out_shape=jax.ShapeDtypeStruct((share * count, width), jnp.float32),
        grid_spec=pltpu.PrefetchScalarGridSpec(
            num_scalar_prefetch=1, grid=(), in_specs=[inside] * len(pieces), out_specs=inside
        ),
        compiler_params=pltpu.CompilerParams(vmem_limit_bytes=VMEM),
        name="place",
    )(index, *pieces)


PARTS = ((0, 0), (0, 1), (0, 3), (1, 0), (1, 2), (0, 2), (1, 1), (1, 3))
CHIP_HALVES = (((0, 0), (0, 1), (0, 3), (1, 0)), ((1, 2), (0, 2), (1, 1), (1, 3)))


def lists_of_numbers(halves, chips, parts):
    table, begin = [], {}
    for place in itertools.product(*[range(n) for n in SIZES.values()]):
        at = dict(zip(SIZES, place))

        def number(axes, offsets, sign):
            flat = 0
            for axis, offset in zip(axes, offsets):
                flat = flat * SIZES[axis] + (at[axis] + sign * offset) % SIZES[axis]
            return flat

        core = at["core"]
        come = [number(CHIP, o, -1) * 2 for o in chips]
        go = [number(CHIP, o, 1) * 2 for o in halves[0] + halves[1]]
        lists = {
            "come": [c + core for c in come] + [c + 1 - core for c in come],
            "to": [number(REP, o, 1) for o in parts],
            "cross": [c + 1 - core for c in go],
            "stay": [c + core for c in go],
            "turn": [
                parts.index(((at["xh"] - h) % SIZES["xh"], (at["y"] - y) % SIZES["y"])) for h, y in all_offsets(REP)
            ],
            "piece": [number(REP, (k, o), -1) for o in range(SIZES["y"]) for k in range(SIZES["xh"])],
        }
        row = []
        for name, numbers in lists.items():
            begin[name] = len(row)
            row += numbers
        table.append(row)
    return np.asarray(table, np.int32), begin


def body(features, weight, layer_bias, tile_values, tile_target, tile_counts, cotangent):
    local_rows, width = features.shape
    values = tile_values[0, 0]
    targets = tile_target[0, 0].T
    counts = tile_counts[0, 0]
    tile = values.shape[-1]
    slot_total = values.shape[1]
    assert local_rows == 2 * tile and slot_total == VARIANTS[-1]
    parts = list(PARTS)
    halves = CHIP_HALVES[::-1]
    chips = CHIP_HALVES[0] + CHIP_HALVES[1]
    y = SIZES["y"]
    table, begin = lists_of_numbers(halves, chips, parts)
    index = lax.dynamic_slice_in_dim(jnp.asarray(table), lax.axis_index(ALL), 1)[0]

    own = [send_by(features, CHIP, o) if any(o) else features for o in chips]
    values, index = fetch(values, index)
    index, own[1] = lax.optimization_barrier((index, own[1]))
    crossed = [send_by(x, ("core",), (1,)) for x in own]
    partial = aggregate(begin["come"], begin["to"], len(parts), index, targets, counts, own + crossed, values)

    received = [send_by(partial[i], REP, o) if any(o) else partial[i] for i, o in enumerate(parts)]
    output, *messages = middle(begin["to"], index, received, weight, layer_bias, cotangent)
    messages = [send_by(messages[i], REP, o) if any(o) else messages[i] for i, o in enumerate(parts)]

    share = width // len(parts)
    share_sum = add_shares(messages, share)
    each = len(halves[0])
    across, merged = [], []
    for i, step in enumerate((None, ("xl", 1), ("z", 1), ("z", 2))):
        if step:
            index, share_sum = lax.optimization_barrier((index, share_sum))
            arriving = exchange(share_sum, *step)
        k = i % 2
        if i < 2:
            found = spread(each, begin["cross"] + each * k, begin["turn"], index, targets, counts, messages, values)
            across.append(send_by(found[0], ("core",), (1,)))
        else:
            found = spread(
                each, begin["stay"] + each * k, begin["turn"], index, targets, counts, messages, values, across[k : k + 1]
            )
            merged += found
        if step:
            _, share_sum, arriving = lax.optimization_barrier((found, share_sum, arriving))
            share_sum = share_sum + arriving
    last = [send_by(piece, CHIP, o) if any(o) else piece for piece, o in zip(merged, halves[0] + halves[1])]
    _, share_sum = lax.optimization_barrier((found, share_sum))
    share_sum = share_sum + exchange(share_sum, "core", 1)
    arriving = exchange(share_sum, "xh", 1)
    arriving, last[5] = lax.optimization_barrier((arriving, last[5]))
    total = None
    for piece in last:
        piece = piece.astype(jnp.float32)
        total = piece if total is None else total + piece
    grad_features = total.astype(jnp.bfloat16)

    norm_scale = 1.0 / math.sqrt(local_rows * math.prod(SIZES.values()))
    grad_bias = share_sum[share] * norm_scale
    pair = jnp.concatenate([share_sum[:share], arriving[:share]]).astype(jnp.bfloat16)
    pieces = [send_by(pair, ("y",), (o,)) if o else pair for o in range(y)]
    grad_weight = place(begin["piece"], len(parts), index, pieces, share, norm_scale)
    return (output, grad_features, grad_weight, grad_bias)


def solution(mesh):
    fine = Mesh(np.asarray(mesh.devices).reshape(tuple(SIZES.values())), tuple(SIZES))
    placed = (
        P(ALL, None),
        P(),
        P(),
        P(BLK, REP, None, None, None, None),
        P(BLK, REP, None, None),
        P(BLK, REP, None),
        P(ALL, None),
    )
    return jax.shard_map(
        body,
        mesh=fine,
        in_specs=placed,
        out_specs=(P(ALL, None), P(ALL, None), P(), P()),
        check_vma=False,
    )
```

```python
import itertools
import math

import jax
import jax.numpy as jnp
import numpy as np
from jax import lax
from jax.experimental import pallas as pl
from jax.experimental.pallas import tpu as pltpu
from jax.sharding import Mesh, PartitionSpec as P

SIZES = {"xl": 2, "z": 4, "core": 2, "xh": 2, "y": 4}
BLK = ("xl", "z", "core")
REP = ("xh", "y")
CHIP = ("xl", "z")
ALL = BLK + REP
VMEM = 26 << 20


def send_by(value, axes, offsets):
    sizes = [SIZES[a] for a in axes]
    pairs = []
    for at in itertools.product(*[range(n) for n in sizes]):
        to = [(i + o) % n for i, o, n in zip(at, offsets, sizes)]
        pairs.append((int(np.ravel_multi_index(at, sizes)), int(np.ravel_multi_index(to, sizes))))
    return lax.ppermute(value, axes, pairs)


def exchange(value, axis, mask):
    return lax.ppermute(value, axis, [(i, i ^ mask) for i in range(SIZES[axis])])


def all_offsets(axes):
    return list(itertools.product(*[range(SIZES[a]) for a in axes]))


EXTRA = 8
VARIANTS = (1, 2, 3, 4, 6, 8)


def cost(flops, transferred):
    return pl.CostEstimate(flops=flops, transcendentals=0, bytes_accessed=transferred)


class Window:
    def __init__(self, ref, base, length):
        self.ref, self.base, self.shape = ref, base, (length,)

    def __getitem__(self, i):
        return self.ref[self.base + i]


def of_class(count, action):
    low = 0
    for n in VARIANTS:

        @pl.when((count > low) & (count <= n))
        def _():
            action(n)

        low = n


def fetch_kernel(index_ref, v_ref, out_ref, again_ref, sem):
    parts = sem.shape[0]
    each = v_ref.shape[0] // parts
    copies = [
        pltpu.make_async_copy(v_ref.at[pl.ds(i * each, each)], out_ref.at[pl.ds(i * each, each)], sem.at[i])
        for i in range(parts)
    ]
    for copy in copies:
        copy.start()
    for copy in copies:
        copy.wait()
    for i in range(index_ref.shape[0]):
        again_ref[i] = index_ref[i]


def fetch(values, index):
    return pl.pallas_call(
        fetch_kernel,
        out_shape=(pltpu.VMEM(values.shape, values.dtype), jax.ShapeDtypeStruct(index.shape, index.dtype)),
        in_specs=[pl.BlockSpec(memory_space=pltpu.SMEM), pl.BlockSpec(memory_space=pl.ANY)],
        out_specs=(pl.BlockSpec(memory_space=pltpu.VMEM), pl.BlockSpec(memory_space=pltpu.SMEM)),
        scratch_shapes=[pltpu.SemaphoreType.DMA((8,))],
        compiler_params=pltpu.CompilerParams(vmem_limit_bytes=VMEM),
        cost_estimate=cost(0, 16 << 20),
        name="fetch",
    )(index, pltpu.with_memory_space_constraint(values, pltpu.HBM))


def forward_kernel(shards, at_source, at_place, index_ref, target_ref, count_ref, v_ref, *refs):
    source_ref = Window(index_ref, at_source, shards)
    place_ref = Window(index_ref, at_place, len(refs) - 2 - shards)
    x_refs, refs = refs[:shards], refs[shards:]
    acc_ref, x_buf = refs[-2:]
    out_refs = refs[:-2]
    tile = v_ref.shape[-1]
    dummy = acc_ref.shape[0] - 1
    for i in range(shards):
        x_buf[i] = x_refs[i][...]
    acc_ref[...] = jnp.zeros_like(acc_ref)

    def group_step(k, carry):
        group = source_ref[k // 2] * 2 + k % 2

        def work(n):
            rows = x_buf[k // 2, pl.ds(pl.multiple_of(k % 2 * tile, tile), tile), :]
            tiles = v_ref[group, pl.ds(0, n)].reshape(n * tile, tile)
            product = jnp.dot(tiles, rows, preferred_element_type=jnp.float32)
            for m in range(n):
                to = jnp.where(m < count_ref[group], target_ref[m, group], dummy)
                acc_ref[to] += product[m * tile : (m + 1) * tile]

        of_class(count_ref[group], work)
        return carry

    lax.fori_loop(0, 2 * shards, group_step, 0)
    for i, out_ref in enumerate(out_refs):
        for t in range(2):
            out_ref[pl.ds(t * tile, tile), :] = acc_ref[place_ref[i] * 2 + t].astype(out_ref.dtype)


def aggregate(at_source, at_place, parts, index, targets, counts, gathered, values):
    shards = len(gathered)
    rows, width = gathered[0].shape
    tile = values.shape[-1]
    inside = pl.BlockSpec(memory_space=pltpu.VMEM)
    return pl.pallas_call(
        lambda *refs: forward_kernel(shards, at_source, at_place, *refs),
        out_shape=(jax.ShapeDtypeStruct((rows, width), jnp.bfloat16),) * parts,
        grid_spec=pltpu.PrefetchScalarGridSpec(
            num_scalar_prefetch=3,
            grid=(),
            in_specs=[inside] * (1 + shards),
            out_specs=(inside,) * parts,
            scratch_shapes=[
                pltpu.VMEM((parts * 2 + 1, tile, width), jnp.float32),
                pltpu.VMEM((shards, rows, width), jnp.bfloat16),
            ],
        ),
        compiler_params=pltpu.CompilerParams(vmem_limit_bytes=VMEM),
        cost_estimate=cost(8 << 30, 16 << 20),
        name="aggregate",
    )(index, targets, counts, pltpu.with_memory_space_constraint(values, pltpu.VMEM), *gathered)


def backward_kernel(shards, parts, at_source, at_turn, crossing, *refs):
    index_ref, target_ref, count_ref, v_ref = refs[:4]
    source_ref = Window(index_ref, at_source, shards)
    m_refs, refs = refs[4 : 4 + parts], refs[4 + parts :]
    if crossing:
        crossed_refs, refs = refs[:crossing], refs[crossing:]
        out_refs, refs = refs[:shards], refs[shards:]
    else:
        out_ref, refs = refs[0], refs[1:]
    table_ref = refs[0]
    tile = v_ref.shape[-1]
    rows = 2 * tile
    for i in range(parts):
        table_ref[pl.ds(i * rows, rows), :] = m_refs[i][pl.ds(0, rows), :]
    blank = table_ref.at[pl.ds(parts * rows, tile)]
    blank[...] = jnp.zeros_like(blank)
    if crossing:
        term_ref = refs[1]

    def group_step(k, carry):
        group = source_ref[k // 2] * 2 + k % 2
        i = k // 2
        at = pl.ds(pl.multiple_of(k % 2 * tile, tile), tile)

        def work(n):
            tiles = v_ref[group, pl.ds(0, n)].reshape(n * tile, tile)
            found = []
            for m in range(n):
                target = target_ref[m, group]
                held = index_ref[at_turn + target // 2] * 2 + target % 2
                held = jnp.where(m < count_ref[group], held, 2 * parts)
                found.append(table_ref[pl.ds(pl.multiple_of(held * tile, tile), tile), :])
            found = jnp.concatenate(found, axis=0) if n > 1 else found[0]
            product = lax.dot_general(tiles, found, (((0,), (0,)), ((), ())), preferred_element_type=jnp.float32)
            if crossing:
                term_ref[i, at, :] = (product + crossed_refs[0][i, at, :].astype(jnp.float32)).astype(jnp.bfloat16)
            else:
                out_ref[i, at, :] = product.astype(jnp.bfloat16)

        of_class(count_ref[group], work)
        return carry

    lax.fori_loop(0, 2 * shards, group_step, 0)
    if crossing:
        for i in range(shards):
            out_refs[i][...] = term_ref[i]


def share_kernel(*refs):
    m_refs, sum_ref = refs[:-1], refs[-1]
    share = sum_ref.shape[0] - 8
    more = share + EXTRA
    total = None
    for m_ref in m_refs:
        term = m_ref[pl.ds(m_ref.shape[0] - more, more), :].astype(jnp.float32)
        total = term if total is None else total + term
    sum_ref[pl.ds(0, share), :] = total[:share]
    bias = total[share : share + 1] + total[share + 1 : share + 2]
    sum_ref[pl.ds(share, 8), :] = jnp.broadcast_to(bias, (8, bias.shape[1]))


def add_shares(messages, share):
    width = messages[0].shape[1]
    return pl.pallas_call(
        share_kernel,
        out_shape=jax.ShapeDtypeStruct((share + 8, width), jnp.float32),
        in_specs=[pl.BlockSpec(memory_space=pltpu.VMEM)] * len(messages),
        out_specs=pl.BlockSpec(memory_space=pltpu.VMEM),
        compiler_params=pltpu.CompilerParams(vmem_limit_bytes=VMEM),
        cost_estimate=cost(1 << 20, 1 << 20),
        name="add_shares",
    )(*messages)


def split_rows(row):
    high = row.astype(jnp.bfloat16)
    low = (row - high.astype(jnp.float32)).astype(jnp.bfloat16)
    line = lax.broadcasted_iota(jnp.int32, (EXTRA, row.shape[1]), 0)
    spread_high = jnp.broadcast_to(high.astype(jnp.float32), line.shape)
    spread_low = jnp.broadcast_to(low.astype(jnp.float32), line.shape)
    return jnp.where(line == 0, spread_high, jnp.where(line == 1, spread_low, 0.0)).astype(jnp.bfloat16)


def spread(shards, at_source, at_turn, index, targets, counts, messages, values, crossed=()):
    parts = len(messages)
    width = messages[0].shape[1]
    tile = values.shape[-1]
    rows = 2 * tile
    inside = pl.BlockSpec(memory_space=pltpu.VMEM)
    scratch = [pltpu.VMEM((parts * rows + tile, width), jnp.bfloat16)]
    if crossed:
        out_shape = (jax.ShapeDtypeStruct((rows, width), jnp.bfloat16),) * shards
        scratch.append(pltpu.VMEM((shards, rows, width), jnp.bfloat16))
    else:
        out_shape = (jax.ShapeDtypeStruct((shards, rows, width), jnp.bfloat16),)
    return pl.pallas_call(
        lambda *refs: backward_kernel(
            shards, parts, at_source, at_turn, len(crossed), *refs
        ),
        out_shape=out_shape,
        grid_spec=pltpu.PrefetchScalarGridSpec(
            num_scalar_prefetch=3,
            grid=(),
            in_specs=[inside] * (1 + parts + len(crossed)),
            out_specs=(inside,) * len(out_shape),
            scratch_shapes=scratch,
        ),
        compiler_params=pltpu.CompilerParams(vmem_limit_bytes=VMEM),
        cost_estimate=cost(shards << 32, shards << 20),
        name="spread",
    )(index, targets, counts, pltpu.with_memory_space_constraint(values, pltpu.VMEM), *messages, *crossed)


def middle_kernel(parts, at_place, index_ref, *refs):
    place_ref = Window(index_ref, at_place, parts)
    part_refs, refs = refs[:parts], refs[parts:]
    weight_ref, bias_ref, cotangent_ref, out_ref = refs[:4]
    message_refs, part_ref = refs[4 : 4 + parts], refs[4 + parts]
    f32 = jnp.float32
    total = part_refs[0][...].astype(f32)
    for part in part_refs[1:]:
        total += part[...].astype(f32)
    rows = total.astype(jnp.bfloat16)
    shifted = jnp.dot(rows, weight_ref[...], preferred_element_type=f32) + bias_ref[...]
    logistic = jax.nn.sigmoid(shifted)
    out_ref[...] = (shifted * logistic).astype(jnp.bfloat16)
    derivative = logistic * (1.0 + shifted * (1.0 - logistic))
    grad = (cotangent_ref[...].astype(f32) * derivative).astype(jnp.bfloat16)
    back = lax.dot_general(
        grad, weight_ref[...], (((1,), (1,)), ((), ())), preferred_element_type=f32
    ).astype(jnp.bfloat16)
    part_ref[...] = lax.dot_general(rows, grad, (((0,), (0,)), ((), ())), preferred_element_type=f32)
    tail = split_rows(jnp.sum(grad.astype(f32), axis=0, keepdims=True))
    share = part_ref.shape[0] // parts
    high = back.shape[0]
    for i, message_ref in enumerate(message_refs):
        message_ref[pl.ds(0, high), :] = back
        at = pl.multiple_of(place_ref[i] * share, share)
        message_ref[pl.ds(high, share), :] = part_ref[pl.ds(at, share), :].astype(jnp.bfloat16)
        message_ref[pl.ds(high + share, EXTRA), :] = tail


def middle(at_place, index, sums, weight, layer_bias, cotangent):
    rows, width = cotangent.shape
    parts = len(sums)
    inside = pl.BlockSpec(memory_space=pltpu.VMEM)
    message = jax.ShapeDtypeStruct((rows + width // parts + EXTRA, width), jnp.bfloat16)
    return pl.pallas_call(
        lambda *refs: middle_kernel(parts, at_place, *refs),
        out_shape=(jax.ShapeDtypeStruct((rows, width), jnp.bfloat16),) + (message,) * parts,
        grid_spec=pltpu.PrefetchScalarGridSpec(
            num_scalar_prefetch=1,
            grid=(),
            in_specs=[inside] * (parts + 3),
            out_specs=(inside,) * (parts + 1),
            scratch_shapes=[pltpu.VMEM((width, width), jnp.float32)],
        ),
        compiler_params=pltpu.CompilerParams(vmem_limit_bytes=VMEM),
        cost_estimate=cost(1 << 30, 8 << 20),
        name="middle",
    )(index, *sums, weight, layer_bias[None, :], cotangent)


def place_kernel(scale, share, at_place, index_ref, *refs):
    place_ref = Window(index_ref, at_place, refs[-1].shape[0] // share)
    for i, piece in enumerate(refs[:-1]):
        for k in range(piece.shape[0] // share):
            at = pl.multiple_of(place_ref[2 * i + k] * share, share)
            refs[-1][pl.ds(at, share), :] = piece[pl.ds(k * share, share), :].astype(jnp.float32) * scale


def place(at_place, count, index, pieces, share, scale):
    width = pieces[0].shape[1]
    inside = pl.BlockSpec(memory_space=pltpu.VMEM)
    return pl.pallas_call(
        lambda *refs: place_kernel(scale, share, at_place, *refs),
        out_shape=jax.ShapeDtypeStruct((share * count, width), jnp.float32),
        grid_spec=pltpu.PrefetchScalarGridSpec(
            num_scalar_prefetch=1, grid=(), in_specs=[inside] * len(pieces), out_specs=inside
        ),
        compiler_params=pltpu.CompilerParams(vmem_limit_bytes=VMEM),
        name="place",
    )(index, *pieces)


PARTS = ((0, 0), (0, 1), (0, 3), (1, 0), (1, 2), (0, 2), (1, 1), (1, 3))
CHIP_HALVES = (((0, 0), (0, 1), (0, 3), (1, 0)), ((1, 2), (0, 2), (1, 1), (1, 3)))


def lists_of_numbers(halves, chips, parts):
    table, begin = [], {}
    for place in itertools.product(*[range(n) for n in SIZES.values()]):
        at = dict(zip(SIZES, place))

        def number(axes, offsets, sign):
            flat = 0
            for axis, offset in zip(axes, offsets):
                flat = flat * SIZES[axis] + (at[axis] + sign * offset) % SIZES[axis]
            return flat

        core = at["core"]
        come = [number(CHIP, o, -1) * 2 for o in chips]
        go = [number(CHIP, o, 1) * 2 for o in halves[0] + halves[1]]
        lists = {
            "come": [c + core for c in come] + [c + 1 - core for c in come],
            "to": [number(REP, o, 1) for o in parts],
            "cross": [c + 1 - core for c in go],
            "stay": [c + core for c in go],
            "turn": [
                parts.index(((at["xh"] - h) % SIZES["xh"], (at["y"] - y) % SIZES["y"])) for h, y in all_offsets(REP)
            ],
            "piece": [number(REP, (k, o), -1) for o in range(SIZES["y"]) for k in range(SIZES["xh"])],
        }
        row = []
        for name, numbers in lists.items():
            begin[name] = len(row)
            row += numbers
        table.append(row)
    return np.asarray(table, np.int32), begin


def body(features, weight, layer_bias, tile_values, tile_target, tile_counts, cotangent):
    local_rows, width = features.shape
    values = tile_values[0, 0]
    targets = tile_target[0, 0].T
    counts = tile_counts[0, 0]
    tile = values.shape[-1]
    slot_total = values.shape[1]
    assert local_rows == 2 * tile and slot_total == VARIANTS[-1]
    parts = list(PARTS)
    halves = CHIP_HALVES[::-1]
    chips = CHIP_HALVES[0] + CHIP_HALVES[1]
    y = SIZES["y"]
    table, begin = lists_of_numbers(halves, chips, parts)
    index = lax.dynamic_slice_in_dim(jnp.asarray(table), lax.axis_index(ALL), 1)[0]

    own = [send_by(features, CHIP, o) if any(o) else features for o in chips]
    values, index = fetch(values, index)
    index, own[3] = lax.optimization_barrier((index, own[3]))
    crossed = [send_by(x, ("core",), (1,)) for x in own]
    partial = aggregate(begin["come"], begin["to"], len(parts), index, targets, counts, own + crossed, values)

    received = [send_by(partial[i], REP, o) if any(o) else partial[i] for i, o in enumerate(parts)]
    output, *messages = middle(begin["to"], index, received, weight, layer_bias, cotangent)
    messages = [send_by(messages[i], REP, o) if any(o) else messages[i] for i, o in enumerate(parts)]

    share = width // len(parts)
    share_sum = add_shares(messages, share)
    each = len(halves[0])
    across, merged = [], []
    for i, step in enumerate((None, ("xl", 1), ("z", 1), ("z", 2))):
        if step:
            index, share_sum = lax.optimization_barrier((index, share_sum))
            arriving = exchange(share_sum, *step)
        k = i % 2
        if i < 2:
            found = spread(each, begin["cross"] + each * k, begin["turn"], index, targets, counts, messages, values)
            across.append(send_by(found[0], ("core",), (1,)))
        else:
            found = spread(
                each, begin["stay"] + each * k, begin["turn"], index, targets, counts, messages, values, across[k : k + 1]
            )
            merged += found
        if step:
            _, share_sum, arriving = lax.optimization_barrier((found, share_sum, arriving))
            share_sum = share_sum + arriving
    last = [send_by(piece, CHIP, o) if any(o) else piece for piece, o in zip(merged, halves[0] + halves[1])]
    _, share_sum = lax.optimization_barrier((found, share_sum))
    share_sum = share_sum + exchange(share_sum, "core", 1)
    arriving = exchange(share_sum, "xh", 1)
    arriving, last[5] = lax.optimization_barrier((arriving, last[5]))
    total = None
    for piece in last:
        piece = piece.astype(jnp.float32)
        total = piece if total is None else total + piece
    grad_features = total.astype(jnp.bfloat16)

    norm_scale = 1.0 / math.sqrt(local_rows * math.prod(SIZES.values()))
    grad_bias = share_sum[share] * norm_scale
    pair = jnp.concatenate([share_sum[:share], arriving[:share]]).astype(jnp.bfloat16)
    pieces = [send_by(pair, ("y",), (o,)) if o else pair for o in range(y)]
    grad_weight = place(begin["piece"], len(parts), index, pieces, share, norm_scale)
    return (output, grad_features, grad_weight, grad_bias)


def solution(mesh):
    fine = Mesh(np.asarray(mesh.devices).reshape(tuple(SIZES.values())), tuple(SIZES))
    placed = (
        P(ALL, None),
        P(),
        P(),
        P(BLK, REP, None, None, None, None),
        P(BLK, REP, None, None),
        P(BLK, REP, None),
        P(ALL, None),
    )
    return jax.shard_map(
        body,
        mesh=fine,
        in_specs=placed,
        out_specs=(P(ALL, None), P(ALL, None), P(), P()),
        check_vma=False,
    )
```

```python
import itertools
import math

import jax
import jax.numpy as jnp
import numpy as np
from jax import lax
from jax.experimental import pallas as pl
from jax.experimental.pallas import tpu as pltpu
from jax.sharding import Mesh, PartitionSpec as P

SIZES = {"xl": 2, "z": 4, "core": 2, "xh": 2, "y": 4}
BLK = ("xl", "z", "core")
REP = ("xh", "y")
CHIP = ("xl", "z")
ALL = BLK + REP
VMEM = 26 << 20


def send_by(value, axes, offsets):
    sizes = [SIZES[a] for a in axes]
    pairs = []
    for at in itertools.product(*[range(n) for n in sizes]):
        to = [(i + o) % n for i, o, n in zip(at, offsets, sizes)]
        pairs.append((int(np.ravel_multi_index(at, sizes)), int(np.ravel_multi_index(to, sizes))))
    return lax.ppermute(value, axes, pairs)


def exchange(value, axis, mask):
    return lax.ppermute(value, axis, [(i, i ^ mask) for i in range(SIZES[axis])])


def all_offsets(axes):
    return list(itertools.product(*[range(SIZES[a]) for a in axes]))


EXTRA = 8
VARIANTS = (1, 2, 3, 4, 6, 8)


def cost(flops, transferred):
    return pl.CostEstimate(flops=flops, transcendentals=0, bytes_accessed=transferred)


class Window:
    def __init__(self, ref, base, length):
        self.ref, self.base, self.shape = ref, base, (length,)

    def __getitem__(self, i):
        return self.ref[self.base + i]


def of_class(count, action):
    low = 0
    for n in VARIANTS:

        @pl.when((count > low) & (count <= n))
        def _():
            action(n)

        low = n


def fetch_kernel(index_ref, v_ref, out_ref, again_ref, sem):
    parts = sem.shape[0]
    each = v_ref.shape[0] // parts
    copies = [
        pltpu.make_async_copy(v_ref.at[pl.ds(i * each, each)], out_ref.at[pl.ds(i * each, each)], sem.at[i])
        for i in range(parts)
    ]
    for copy in copies:
        copy.start()
    for copy in copies:
        copy.wait()
    for i in range(index_ref.shape[0]):
        again_ref[i] = index_ref[i]


def fetch(values, index):
    return pl.pallas_call(
        fetch_kernel,
        out_shape=(pltpu.VMEM(values.shape, values.dtype), jax.ShapeDtypeStruct(index.shape, index.dtype)),
        in_specs=[pl.BlockSpec(memory_space=pltpu.SMEM), pl.BlockSpec(memory_space=pl.ANY)],
        out_specs=(pl.BlockSpec(memory_space=pltpu.VMEM), pl.BlockSpec(memory_space=pltpu.SMEM)),
        scratch_shapes=[pltpu.SemaphoreType.DMA((8,))],
        compiler_params=pltpu.CompilerParams(vmem_limit_bytes=VMEM),
        cost_estimate=cost(0, 16 << 20),
        name="fetch",
    )(index, pltpu.with_memory_space_constraint(values, pltpu.HBM))


def forward_kernel(shards, at_source, at_place, index_ref, target_ref, count_ref, v_ref, *refs):
    source_ref = Window(index_ref, at_source, shards)
    place_ref = Window(index_ref, at_place, len(refs) - 2 - shards)
    x_refs, refs = refs[:shards], refs[shards:]
    acc_ref, x_buf = refs[-2:]
    out_refs = refs[:-2]
    tile = v_ref.shape[-1]
    dummy = acc_ref.shape[0] - 1
    for i in range(shards):
        x_buf[i] = x_refs[i][...]
    acc_ref[...] = jnp.zeros_like(acc_ref)

    def group_step(k, carry):
        group = source_ref[k // 2] * 2 + k % 2

        def work(n):
            rows = x_buf[k // 2, pl.ds(pl.multiple_of(k % 2 * tile, tile), tile), :]
            tiles = v_ref[group, pl.ds(0, n)].reshape(n * tile, tile)
            product = jnp.dot(tiles, rows, preferred_element_type=jnp.float32)
            for m in range(n):
                to = jnp.where(m < count_ref[group], target_ref[m, group], dummy)
                acc_ref[to] += product[m * tile : (m + 1) * tile]

        of_class(count_ref[group], work)
        return carry

    lax.fori_loop(0, 2 * shards, group_step, 0)
    for i, out_ref in enumerate(out_refs):
        for t in range(2):
            out_ref[pl.ds(t * tile, tile), :] = acc_ref[place_ref[i] * 2 + t].astype(out_ref.dtype)


def aggregate(at_source, at_place, parts, index, targets, counts, gathered, values):
    shards = len(gathered)
    rows, width = gathered[0].shape
    tile = values.shape[-1]
    inside = pl.BlockSpec(memory_space=pltpu.VMEM)
    return pl.pallas_call(
        lambda *refs: forward_kernel(shards, at_source, at_place, *refs),
        out_shape=(jax.ShapeDtypeStruct((rows, width), jnp.bfloat16),) * parts,
        grid_spec=pltpu.PrefetchScalarGridSpec(
            num_scalar_prefetch=3,
            grid=(),
            in_specs=[inside] * (1 + shards),
            out_specs=(inside,) * parts,
            scratch_shapes=[
                pltpu.VMEM((parts * 2 + 1, tile, width), jnp.float32),
                pltpu.VMEM((shards, rows, width), jnp.bfloat16),
            ],
        ),
        compiler_params=pltpu.CompilerParams(vmem_limit_bytes=VMEM),
        cost_estimate=cost(8 << 30, 16 << 20),
        name="aggregate",
    )(index, targets, counts, pltpu.with_memory_space_constraint(values, pltpu.VMEM), *gathered)


def backward_kernel(shards, parts, at_source, at_turn, crossing, *refs):
    index_ref, target_ref, count_ref, v_ref = refs[:4]
    source_ref = Window(index_ref, at_source, shards)
    m_refs, refs = refs[4 : 4 + parts], refs[4 + parts :]
    if crossing:
        crossed_refs, refs = refs[:crossing], refs[crossing:]
        out_refs, refs = refs[:shards], refs[shards:]
    else:
        out_ref, refs = refs[0], refs[1:]
    table_ref = refs[0]
    tile = v_ref.shape[-1]
    rows = 2 * tile
    for i in range(parts):
        table_ref[pl.ds(i * rows, rows), :] = m_refs[i][pl.ds(0, rows), :]
    blank = table_ref.at[pl.ds(parts * rows, tile)]
    blank[...] = jnp.zeros_like(blank)
    if crossing:
        term_ref = refs[1]

    def group_step(k, carry):
        group = source_ref[k // 2] * 2 + k % 2
        i = k // 2
        at = pl.ds(pl.multiple_of(k % 2 * tile, tile), tile)

        def work(n):
            tiles = v_ref[group, pl.ds(0, n)].reshape(n * tile, tile)
            found = []
            for m in range(n):
                target = target_ref[m, group]
                held = index_ref[at_turn + target // 2] * 2 + target % 2
                held = jnp.where(m < count_ref[group], held, 2 * parts)
                found.append(table_ref[pl.ds(pl.multiple_of(held * tile, tile), tile), :])
            found = jnp.concatenate(found, axis=0) if n > 1 else found[0]
            product = lax.dot_general(tiles, found, (((0,), (0,)), ((), ())), preferred_element_type=jnp.float32)
            if crossing:
                term_ref[i, at, :] = (product + crossed_refs[0][i, at, :].astype(jnp.float32)).astype(jnp.bfloat16)
            else:
                out_ref[i, at, :] = product.astype(jnp.bfloat16)

        of_class(count_ref[group], work)
        return carry

    lax.fori_loop(0, 2 * shards, group_step, 0)
    if crossing:
        for i in range(shards):
            out_refs[i][...] = term_ref[i]


def share_kernel(*refs):
    m_refs, sum_ref = refs[:-1], refs[-1]
    share = sum_ref.shape[0] - 8
    more = share + EXTRA
    total = None
    for m_ref in m_refs:
        term = m_ref[pl.ds(m_ref.shape[0] - more, more), :].astype(jnp.float32)
        total = term if total is None else total + term
    sum_ref[pl.ds(0, share), :] = total[:share]
    bias = total[share : share + 1] + total[share + 1 : share + 2]
    sum_ref[pl.ds(share, 8), :] = jnp.broadcast_to(bias, (8, bias.shape[1]))


def add_shares(messages, share):
    width = messages[0].shape[1]
    return pl.pallas_call(
        share_kernel,
        out_shape=jax.ShapeDtypeStruct((share + 8, width), jnp.float32),
        in_specs=[pl.BlockSpec(memory_space=pltpu.VMEM)] * len(messages),
        out_specs=pl.BlockSpec(memory_space=pltpu.VMEM),
        compiler_params=pltpu.CompilerParams(vmem_limit_bytes=VMEM),
        cost_estimate=cost(1 << 20, 1 << 20),
        name="add_shares",
    )(*messages)


def split_rows(row):
    high = row.astype(jnp.bfloat16)
    low = (row - high.astype(jnp.float32)).astype(jnp.bfloat16)
    line = lax.broadcasted_iota(jnp.int32, (EXTRA, row.shape[1]), 0)
    spread_high = jnp.broadcast_to(high.astype(jnp.float32), line.shape)
    spread_low = jnp.broadcast_to(low.astype(jnp.float32), line.shape)
    return jnp.where(line == 0, spread_high, jnp.where(line == 1, spread_low, 0.0)).astype(jnp.bfloat16)


def spread(shards, at_source, at_turn, index, targets, counts, messages, values, crossed=()):
    parts = len(messages)
    width = messages[0].shape[1]
    tile = values.shape[-1]
    rows = 2 * tile
    inside = pl.BlockSpec(memory_space=pltpu.VMEM)
    scratch = [pltpu.VMEM((parts * rows + tile, width), jnp.bfloat16)]
    if crossed:
        out_shape = (jax.ShapeDtypeStruct((rows, width), jnp.bfloat16),) * shards
        scratch.append(pltpu.VMEM((shards, rows, width), jnp.bfloat16))
    else:
        out_shape = (jax.ShapeDtypeStruct((shards, rows, width), jnp.bfloat16),)
    return pl.pallas_call(
        lambda *refs: backward_kernel(
            shards, parts, at_source, at_turn, len(crossed), *refs
        ),
        out_shape=out_shape,
        grid_spec=pltpu.PrefetchScalarGridSpec(
            num_scalar_prefetch=3,
            grid=(),
            in_specs=[inside] * (1 + parts + len(crossed)),
            out_specs=(inside,) * len(out_shape),
            scratch_shapes=scratch,
        ),
        compiler_params=pltpu.CompilerParams(vmem_limit_bytes=VMEM),
        cost_estimate=cost(shards << 32, shards << 20),
        name="spread",
    )(index, targets, counts, pltpu.with_memory_space_constraint(values, pltpu.VMEM), *messages, *crossed)


def middle_kernel(parts, at_place, index_ref, *refs):
    place_ref = Window(index_ref, at_place, parts)
    part_refs, refs = refs[:parts], refs[parts:]
    weight_ref, bias_ref, cotangent_ref, out_ref = refs[:4]
    message_refs, part_ref = refs[4 : 4 + parts], refs[4 + parts]
    f32 = jnp.float32
    total = part_refs[0][...].astype(f32)
    for part in part_refs[1:]:
        total += part[...].astype(f32)
    rows = total.astype(jnp.bfloat16)
    shifted = jnp.dot(rows, weight_ref[...], preferred_element_type=f32) + bias_ref[...]
    logistic = jax.nn.sigmoid(shifted)
    out_ref[...] = (shifted * logistic).astype(jnp.bfloat16)
    derivative = logistic * (1.0 + shifted * (1.0 - logistic))
    grad = (cotangent_ref[...].astype(f32) * derivative).astype(jnp.bfloat16)
    back = lax.dot_general(
        grad, weight_ref[...], (((1,), (1,)), ((), ())), preferred_element_type=f32
    ).astype(jnp.bfloat16)
    part_ref[...] = lax.dot_general(rows, grad, (((0,), (0,)), ((), ())), preferred_element_type=f32)
    tail = split_rows(jnp.sum(grad.astype(f32), axis=0, keepdims=True))
    share = part_ref.shape[0] // parts
    high = back.shape[0]
    for i, message_ref in enumerate(message_refs):
        message_ref[pl.ds(0, high), :] = back
        at = pl.multiple_of(place_ref[i] * share, share)
        message_ref[pl.ds(high, share), :] = part_ref[pl.ds(at, share), :].astype(jnp.bfloat16)
        message_ref[pl.ds(high + share, EXTRA), :] = tail


def middle(at_place, index, sums, weight, layer_bias, cotangent):
    rows, width = cotangent.shape
    parts = len(sums)
    inside = pl.BlockSpec(memory_space=pltpu.VMEM)
    message = jax.ShapeDtypeStruct((rows + width // parts + EXTRA, width), jnp.bfloat16)
    return pl.pallas_call(
        lambda *refs: middle_kernel(parts, at_place, *refs),
        out_shape=(jax.ShapeDtypeStruct((rows, width), jnp.bfloat16),) + (message,) * parts,
        grid_spec=pltpu.PrefetchScalarGridSpec(
            num_scalar_prefetch=1,
            grid=(),
            in_specs=[inside] * (parts + 3),
            out_specs=(inside,) * (parts + 1),
            scratch_shapes=[pltpu.VMEM((width, width), jnp.float32)],
        ),
        compiler_params=pltpu.CompilerParams(vmem_limit_bytes=VMEM),
        cost_estimate=cost(1 << 30, 8 << 20),
        name="middle",
    )(index, *sums, weight, layer_bias[None, :], cotangent)


def place_kernel(scale, share, at_place, index_ref, *refs):
    place_ref = Window(index_ref, at_place, refs[-1].shape[0] // share)
    for i, piece in enumerate(refs[:-1]):
        for k in range(piece.shape[0] // share):
            at = pl.multiple_of(place_ref[2 * i + k] * share, share)
            refs[-1][pl.ds(at, share), :] = piece[pl.ds(k * share, share), :].astype(jnp.float32) * scale


def place(at_place, count, index, pieces, share, scale):
    width = pieces[0].shape[1]
    inside = pl.BlockSpec(memory_space=pltpu.VMEM)
    return pl.pallas_call(
        lambda *refs: place_kernel(scale, share, at_place, *refs),
        out_shape=jax.ShapeDtypeStruct((share * count, width), jnp.float32),
        grid_spec=pltpu.PrefetchScalarGridSpec(
            num_scalar_prefetch=1, grid=(), in_specs=[inside] * len(pieces), out_specs=inside
        ),
        compiler_params=pltpu.CompilerParams(vmem_limit_bytes=VMEM),
        name="place",
    )(index, *pieces)


PARTS = ((0, 0), (0, 1), (1, 0), (0, 3), (1, 2), (0, 2), (1, 1), (1, 3))
CHIP_HALVES = (((0, 0), (0, 1), (1, 0), (0, 3)), ((1, 2), (0, 2), (1, 1), (1, 3)))


def lists_of_numbers(halves, chips, parts):
    table, begin = [], {}
    for place in itertools.product(*[range(n) for n in SIZES.values()]):
        at = dict(zip(SIZES, place))

        def number(axes, offsets, sign):
            flat = 0
            for axis, offset in zip(axes, offsets):
                flat = flat * SIZES[axis] + (at[axis] + sign * offset) % SIZES[axis]
            return flat

        core = at["core"]
        come = [number(CHIP, o, -1) * 2 for o in chips]
        go = [number(CHIP, o, 1) * 2 for o in halves[0] + halves[1]]
        lists = {
            "come": [c + core for c in come] + [c + 1 - core for c in come],
            "to": [number(REP, o, 1) for o in parts],
            "cross": [c + 1 - core for c in go],
            "stay": [c + core for c in go],
            "turn": [
                parts.index(((at["xh"] - h) % SIZES["xh"], (at["y"] - y) % SIZES["y"])) for h, y in all_offsets(REP)
            ],
            "piece": [number(REP, (k, o), -1) for o in range(SIZES["y"]) for k in range(SIZES["xh"])],
        }
        row = []
        for name, numbers in lists.items():
            begin[name] = len(row)
            row += numbers
        table.append(row)
    return np.asarray(table, np.int32), begin


def body(features, weight, layer_bias, tile_values, tile_target, tile_counts, cotangent):
    local_rows, width = features.shape
    values = tile_values[0, 0]
    targets = tile_target[0, 0].T
    counts = tile_counts[0, 0]
    tile = values.shape[-1]
    slot_total = values.shape[1]
    assert local_rows == 2 * tile and slot_total == VARIANTS[-1]
    parts = list(PARTS)
    halves = CHIP_HALVES[::-1]
    chips = CHIP_HALVES[0] + CHIP_HALVES[1]
    y = SIZES["y"]
    table, begin = lists_of_numbers(halves, chips, parts)
    index = lax.dynamic_slice_in_dim(jnp.asarray(table), lax.axis_index(ALL), 1)[0]

    own = [send_by(features, CHIP, o) if any(o) else features for o in chips]
    values, index = fetch(values, index)
    index, own[1] = lax.optimization_barrier((index, own[1]))
    crossed = [send_by(x, ("core",), (1,)) for x in own]
    partial = aggregate(begin["come"], begin["to"], len(parts), index, targets, counts, own + crossed, values)

    received = [send_by(partial[i], REP, o) if any(o) else partial[i] for i, o in enumerate(parts)]
    output, *messages = middle(begin["to"], index, received, weight, layer_bias, cotangent)
    messages = [send_by(messages[i], REP, o) if any(o) else messages[i] for i, o in enumerate(parts)]

    share = width // len(parts)
    share_sum = add_shares(messages, share)
    each = len(halves[0])
    across, merged = [], []
    for i, step in enumerate((None, ("xl", 1), ("z", 1), ("z", 2))):
        if step:
            index, share_sum = lax.optimization_barrier((index, share_sum))
            arriving = exchange(share_sum, *step)
        k = i % 2
        if i < 2:
            found = spread(each, begin["cross"] + each * k, begin["turn"], index, targets, counts, messages, values)
            across.append(send_by(found[0], ("core",), (1,)))
        else:
            found = spread(
                each, begin["stay"] + each * k, begin["turn"], index, targets, counts, messages, values, across[k : k + 1]
            )
            merged += found
        if step:
            _, share_sum, arriving = lax.optimization_barrier((found, share_sum, arriving))
            share_sum = share_sum + arriving
    last = [send_by(piece, CHIP, o) if any(o) else piece for piece, o in zip(merged, halves[0] + halves[1])]
    _, share_sum = lax.optimization_barrier((found, share_sum))
    share_sum = share_sum + exchange(share_sum, "core", 1)
    arriving = exchange(share_sum, "xh", 1)
    arriving, last[5] = lax.optimization_barrier((arriving, last[5]))
    total = None
    for piece in last:
        piece = piece.astype(jnp.float32)
        total = piece if total is None else total + piece
    grad_features = total.astype(jnp.bfloat16)

    norm_scale = 1.0 / math.sqrt(local_rows * math.prod(SIZES.values()))
    grad_bias = share_sum[share] * norm_scale
    pair = jnp.concatenate([share_sum[:share], arriving[:share]]).astype(jnp.bfloat16)
    pieces = [send_by(pair, ("y",), (o,)) if o else pair for o in range(y)]
    grad_weight = place(begin["piece"], len(parts), index, pieces, share, norm_scale)
    return (output, grad_features, grad_weight, grad_bias)


def solution(mesh):
    fine = Mesh(np.asarray(mesh.devices).reshape(tuple(SIZES.values())), tuple(SIZES))
    placed = (
        P(ALL, None),
        P(),
        P(),
        P(BLK, REP, None, None, None, None),
        P(BLK, REP, None, None),
        P(BLK, REP, None),
        P(ALL, None),
    )
    return jax.shard_map(
        body,
        mesh=fine,
        in_specs=placed,
        out_specs=(P(ALL, None), P(ALL, None), P(), P()),
        check_vma=False,
    )
```

```python
import itertools
import math

import jax
import jax.numpy as jnp
import numpy as np
from jax import lax
from jax.experimental import pallas as pl
from jax.experimental.pallas import tpu as pltpu
from jax.sharding import Mesh, PartitionSpec as P

SIZES = {"xl": 2, "z": 4, "core": 2, "xh": 2, "y": 4}
BLK = ("xl", "z", "core")
REP = ("xh", "y")
CHIP = ("xl", "z")
ALL = BLK + REP
VMEM = 26 << 20


def send_by(value, axes, offsets):
    sizes = [SIZES[a] for a in axes]
    pairs = []
    for at in itertools.product(*[range(n) for n in sizes]):
        to = [(i + o) % n for i, o, n in zip(at, offsets, sizes)]
        pairs.append((int(np.ravel_multi_index(at, sizes)), int(np.ravel_multi_index(to, sizes))))
    return lax.ppermute(value, axes, pairs)


def exchange(value, axis, mask):
    return lax.ppermute(value, axis, [(i, i ^ mask) for i in range(SIZES[axis])])


def all_offsets(axes):
    return list(itertools.product(*[range(SIZES[a]) for a in axes]))


EXTRA = 8
VARIANTS = (1, 2, 3, 4, 6, 8)


def cost(flops, transferred):
    return pl.CostEstimate(flops=flops, transcendentals=0, bytes_accessed=transferred)


class Window:
    def __init__(self, ref, base, length):
        self.ref, self.base, self.shape = ref, base, (length,)

    def __getitem__(self, i):
        return self.ref[self.base + i]


def of_class(count, action):
    low = 0
    for n in VARIANTS:

        @pl.when((count > low) & (count <= n))
        def _():
            action(n)

        low = n


def fetch_kernel(index_ref, v_ref, out_ref, again_ref, sem):
    parts = sem.shape[0]
    each = v_ref.shape[0] // parts
    copies = [
        pltpu.make_async_copy(v_ref.at[pl.ds(i * each, each)], out_ref.at[pl.ds(i * each, each)], sem.at[i])
        for i in range(parts)
    ]
    for copy in copies:
        copy.start()
    for copy in copies:
        copy.wait()
    for i in range(index_ref.shape[0]):
        again_ref[i] = index_ref[i]


def fetch(values, index):
    return pl.pallas_call(
        fetch_kernel,
        out_shape=(pltpu.VMEM(values.shape, values.dtype), jax.ShapeDtypeStruct(index.shape, index.dtype)),
        in_specs=[pl.BlockSpec(memory_space=pltpu.SMEM), pl.BlockSpec(memory_space=pl.ANY)],
        out_specs=(pl.BlockSpec(memory_space=pltpu.VMEM), pl.BlockSpec(memory_space=pltpu.SMEM)),
        scratch_shapes=[pltpu.SemaphoreType.DMA((8,))],
        compiler_params=pltpu.CompilerParams(vmem_limit_bytes=VMEM),
        cost_estimate=cost(0, 16 << 20),
        name="fetch",
    )(index, pltpu.with_memory_space_constraint(values, pltpu.HBM))


def forward_kernel(shards, at_source, at_place, index_ref, target_ref, count_ref, v_ref, *refs):
    source_ref = Window(index_ref, at_source, shards)
    place_ref = Window(index_ref, at_place, len(refs) - 2 - shards)
    x_refs, refs = refs[:shards], refs[shards:]
    acc_ref, x_buf = refs[-2:]
    out_refs = refs[:-2]
    tile = v_ref.shape[-1]
    dummy = acc_ref.shape[0] - 1
    for i in range(shards):
        x_buf[i] = x_refs[i][...]
    acc_ref[...] = jnp.zeros_like(acc_ref)

    def group_step(k, carry):
        group = source_ref[k // 2] * 2 + k % 2

        def work(n):
            rows = x_buf[k // 2, pl.ds(pl.multiple_of(k % 2 * tile, tile), tile), :]
            tiles = v_ref[group, pl.ds(0, n)].reshape(n * tile, tile)
            product = jnp.dot(tiles, rows, preferred_element_type=jnp.float32)
            for m in range(n):
                to = jnp.where(m < count_ref[group], target_ref[m, group], dummy)
                acc_ref[to] += product[m * tile : (m + 1) * tile]

        of_class(count_ref[group], work)
        return carry

    lax.fori_loop(0, 2 * shards, group_step, 0)
    for i, out_ref in enumerate(out_refs):
        for t in range(2):
            out_ref[pl.ds(t * tile, tile), :] = acc_ref[place_ref[i] * 2 + t].astype(out_ref.dtype)


def aggregate(at_source, at_place, parts, index, targets, counts, gathered, values):
    shards = len(gathered)
    rows, width = gathered[0].shape
    tile = values.shape[-1]
    inside = pl.BlockSpec(memory_space=pltpu.VMEM)
    return pl.pallas_call(
        lambda *refs: forward_kernel(shards, at_source, at_place, *refs),
        out_shape=(jax.ShapeDtypeStruct((rows, width), jnp.bfloat16),) * parts,
        grid_spec=pltpu.PrefetchScalarGridSpec(
            num_scalar_prefetch=3,
            grid=(),
            in_specs=[inside] * (1 + shards),
            out_specs=(inside,) * parts,
            scratch_shapes=[
                pltpu.VMEM((parts * 2 + 1, tile, width), jnp.float32),
                pltpu.VMEM((shards, rows, width), jnp.bfloat16),
            ],
        ),
        compiler_params=pltpu.CompilerParams(vmem_limit_bytes=VMEM),
        cost_estimate=cost(8 << 30, 16 << 20),
        name="aggregate",
    )(index, targets, counts, pltpu.with_memory_space_constraint(values, pltpu.VMEM), *gathered)


def backward_kernel(shards, parts, at_source, at_turn, crossing, *refs):
    index_ref, target_ref, count_ref, v_ref = refs[:4]
    source_ref = Window(index_ref, at_source, shards)
    m_refs, refs = refs[4 : 4 + parts], refs[4 + parts :]
    if crossing:
        crossed_refs, refs = refs[:crossing], refs[crossing:]
        out_refs, refs = refs[:shards], refs[shards:]
    else:
        out_ref, refs = refs[0], refs[1:]
    table_ref = refs[0]
    tile = v_ref.shape[-1]
    rows = 2 * tile
    for i in range(parts):
        table_ref[pl.ds(i * rows, rows), :] = m_refs[i][pl.ds(0, rows), :]
    blank = table_ref.at[pl.ds(parts * rows, tile)]
    blank[...] = jnp.zeros_like(blank)
    if crossing:
        term_ref = refs[1]

    def group_step(k, carry):
        group = source_ref[k // 2] * 2 + k % 2
        i = k // 2
        at = pl.ds(pl.multiple_of(k % 2 * tile, tile), tile)

        def work(n):
            tiles = v_ref[group, pl.ds(0, n)].reshape(n * tile, tile)
            found = []
            for m in range(n):
                target = target_ref[m, group]
                held = index_ref[at_turn + target // 2] * 2 + target % 2
                held = jnp.where(m < count_ref[group], held, 2 * parts)
                found.append(table_ref[pl.ds(pl.multiple_of(held * tile, tile), tile), :])
            found = jnp.concatenate(found, axis=0) if n > 1 else found[0]
            product = lax.dot_general(tiles, found, (((0,), (0,)), ((), ())), preferred_element_type=jnp.float32)
            if crossing:
                term_ref[i, at, :] = (product + crossed_refs[0][i, at, :].astype(jnp.float32)).astype(jnp.bfloat16)
            else:
                out_ref[i, at, :] = product.astype(jnp.bfloat16)

        of_class(count_ref[group], work)
        return carry

    lax.fori_loop(0, 2 * shards, group_step, 0)
    if crossing:
        for i in range(shards):
            out_refs[i][...] = term_ref[i]


def share_kernel(*refs):
    m_refs, sum_ref = refs[:-1], refs[-1]
    share = sum_ref.shape[0] - 8
    more = share + EXTRA
    total = None
    for m_ref in m_refs:
        term = m_ref[pl.ds(m_ref.shape[0] - more, more), :].astype(jnp.float32)
        total = term if total is None else total + term
    sum_ref[pl.ds(0, share), :] = total[:share]
    bias = total[share : share + 1] + total[share + 1 : share + 2]
    sum_ref[pl.ds(share, 8), :] = jnp.broadcast_to(bias, (8, bias.shape[1]))


def add_shares(messages, share):
    width = messages[0].shape[1]
    return pl.pallas_call(
        share_kernel,
        out_shape=jax.ShapeDtypeStruct((share + 8, width), jnp.float32),
        in_specs=[pl.BlockSpec(memory_space=pltpu.VMEM)] * len(messages),
        out_specs=pl.BlockSpec(memory_space=pltpu.VMEM),
        compiler_params=pltpu.CompilerParams(vmem_limit_bytes=VMEM),
        cost_estimate=cost(1 << 20, 1 << 20),
        name="add_shares",
    )(*messages)


def split_rows(row):
    high = row.astype(jnp.bfloat16)
    low = (row - high.astype(jnp.float32)).astype(jnp.bfloat16)
    line = lax.broadcasted_iota(jnp.int32, (EXTRA, row.shape[1]), 0)
    spread_high = jnp.broadcast_to(high.astype(jnp.float32), line.shape)
    spread_low = jnp.broadcast_to(low.astype(jnp.float32), line.shape)
    return jnp.where(line == 0, spread_high, jnp.where(line == 1, spread_low, 0.0)).astype(jnp.bfloat16)


def spread(shards, at_source, at_turn, index, targets, counts, messages, values, crossed=()):
    parts = len(messages)
    width = messages[0].shape[1]
    tile = values.shape[-1]
    rows = 2 * tile
    inside = pl.BlockSpec(memory_space=pltpu.VMEM)
    scratch = [pltpu.VMEM((parts * rows + tile, width), jnp.bfloat16)]
    if crossed:
        out_shape = (jax.ShapeDtypeStruct((rows, width), jnp.bfloat16),) * shards
        scratch.append(pltpu.VMEM((shards, rows, width), jnp.bfloat16))
    else:
        out_shape = (jax.ShapeDtypeStruct((shards, rows, width), jnp.bfloat16),)
    return pl.pallas_call(
        lambda *refs: backward_kernel(
            shards, parts, at_source, at_turn, len(crossed), *refs
        ),
        out_shape=out_shape,
        grid_spec=pltpu.PrefetchScalarGridSpec(
            num_scalar_prefetch=3,
            grid=(),
            in_specs=[inside] * (1 + parts + len(crossed)),
            out_specs=(inside,) * len(out_shape),
            scratch_shapes=scratch,
        ),
        compiler_params=pltpu.CompilerParams(vmem_limit_bytes=VMEM),
        cost_estimate=cost(shards << 32, shards << 20),
        name="spread",
    )(index, targets, counts, pltpu.with_memory_space_constraint(values, pltpu.VMEM), *messages, *crossed)


def middle_kernel(parts, at_place, index_ref, *refs):
    place_ref = Window(index_ref, at_place, parts)
    part_refs, refs = refs[:parts], refs[parts:]
    weight_ref, bias_ref, cotangent_ref, out_ref = refs[:4]
    message_refs, part_ref = refs[4 : 4 + parts], refs[4 + parts]
    f32 = jnp.float32
    total = part_refs[0][...].astype(f32)
    for part in part_refs[1:]:
        total += part[...].astype(f32)
    rows = total.astype(jnp.bfloat16)
    shifted = jnp.dot(rows, weight_ref[...], preferred_element_type=f32) + bias_ref[...]
    logistic = jax.nn.sigmoid(shifted)
    out_ref[...] = (shifted * logistic).astype(jnp.bfloat16)
    derivative = logistic * (1.0 + shifted * (1.0 - logistic))
    grad = (cotangent_ref[...].astype(f32) * derivative).astype(jnp.bfloat16)
    back = lax.dot_general(
        grad, weight_ref[...], (((1,), (1,)), ((), ())), preferred_element_type=f32
    ).astype(jnp.bfloat16)
    part_ref[...] = lax.dot_general(rows, grad, (((0,), (0,)), ((), ())), preferred_element_type=f32)
    tail = split_rows(jnp.sum(grad.astype(f32), axis=0, keepdims=True))
    share = part_ref.shape[0] // parts
    high = back.shape[0]
    for i, message_ref in enumerate(message_refs):
        message_ref[pl.ds(0, high), :] = back
        at = pl.multiple_of(place_ref[i] * share, share)
        message_ref[pl.ds(high, share), :] = part_ref[pl.ds(at, share), :].astype(jnp.bfloat16)
        message_ref[pl.ds(high + share, EXTRA), :] = tail


def middle(at_place, index, sums, weight, layer_bias, cotangent):
    rows, width = cotangent.shape
    parts = len(sums)
    inside = pl.BlockSpec(memory_space=pltpu.VMEM)
    message = jax.ShapeDtypeStruct((rows + width // parts + EXTRA, width), jnp.bfloat16)
    return pl.pallas_call(
        lambda *refs: middle_kernel(parts, at_place, *refs),
        out_shape=(jax.ShapeDtypeStruct((rows, width), jnp.bfloat16),) + (message,) * parts,
        grid_spec=pltpu.PrefetchScalarGridSpec(
            num_scalar_prefetch=1,
            grid=(),
            in_specs=[inside] * (parts + 3),
            out_specs=(inside,) * (parts + 1),
            scratch_shapes=[pltpu.VMEM((width, width), jnp.float32)],
        ),
        compiler_params=pltpu.CompilerParams(vmem_limit_bytes=VMEM),
        cost_estimate=cost(1 << 30, 8 << 20),
        name="middle",
    )(index, *sums, weight, layer_bias[None, :], cotangent)


def place_kernel(scale, share, at_place, index_ref, *refs):
    place_ref = Window(index_ref, at_place, refs[-1].shape[0] // share)
    for i, piece in enumerate(refs[:-1]):
        for k in range(piece.shape[0] // share):
            at = pl.multiple_of(place_ref[2 * i + k] * share, share)
            refs[-1][pl.ds(at, share), :] = piece[pl.ds(k * share, share), :].astype(jnp.float32) * scale


def place(at_place, count, index, pieces, share, scale):
    width = pieces[0].shape[1]
    inside = pl.BlockSpec(memory_space=pltpu.VMEM)
    return pl.pallas_call(
        lambda *refs: place_kernel(scale, share, at_place, *refs),
        out_shape=jax.ShapeDtypeStruct((share * count, width), jnp.float32),
        grid_spec=pltpu.PrefetchScalarGridSpec(
            num_scalar_prefetch=1, grid=(), in_specs=[inside] * len(pieces), out_specs=inside
        ),
        compiler_params=pltpu.CompilerParams(vmem_limit_bytes=VMEM),
        name="place",
    )(index, *pieces)


PARTS = ((0, 0), (1, 0), (0, 1), (0, 3), (1, 2), (0, 2), (1, 1), (1, 3))
CHIP_HALVES = (((0, 0), (0, 1), (1, 0), (0, 3)), ((1, 2), (0, 2), (1, 1), (1, 3)))


def lists_of_numbers(halves, chips, parts):
    table, begin = [], {}
    for place in itertools.product(*[range(n) for n in SIZES.values()]):
        at = dict(zip(SIZES, place))

        def number(axes, offsets, sign):
            flat = 0
            for axis, offset in zip(axes, offsets):
                flat = flat * SIZES[axis] + (at[axis] + sign * offset) % SIZES[axis]
            return flat

        core = at["core"]
        come = [number(CHIP, o, -1) * 2 for o in chips]
        go = [number(CHIP, o, 1) * 2 for o in halves[0] + halves[1]]
        lists = {
            "come": [c + core for c in come] + [c + 1 - core for c in come],
            "to": [number(REP, o, 1) for o in parts],
            "cross": [c + 1 - core for c in go],
            "stay": [c + core for c in go],
            "turn": [
                parts.index(((at["xh"] - h) % SIZES["xh"], (at["y"] - y) % SIZES["y"])) for h, y in all_offsets(REP)
            ],
            "piece": [number(REP, (k, o), -1) for o in range(SIZES["y"]) for k in range(SIZES["xh"])],
        }
        row = []
        for name, numbers in lists.items():
            begin[name] = len(row)
            row += numbers
        table.append(row)
    return np.asarray(table, np.int32), begin


def body(features, weight, layer_bias, tile_values, tile_target, tile_counts, cotangent):
    local_rows, width = features.shape
    values = tile_values[0, 0]
    targets = tile_target[0, 0].T
    counts = tile_counts[0, 0]
    tile = values.shape[-1]
    slot_total = values.shape[1]
    assert local_rows == 2 * tile and slot_total == VARIANTS[-1]
    parts = list(PARTS)
    halves = CHIP_HALVES[::-1]
    chips = CHIP_HALVES[0] + CHIP_HALVES[1]
    y = SIZES["y"]
    table, begin = lists_of_numbers(halves, chips, parts)
    index = lax.dynamic_slice_in_dim(jnp.asarray(table), lax.axis_index(ALL), 1)[0]

    own = [send_by(features, CHIP, o) if any(o) else features for o in chips]
    values, index = fetch(values, index)
    index, own[1] = lax.optimization_barrier((index, own[1]))
    crossed = [send_by(x, ("core",), (1,)) for x in own]
    partial = aggregate(begin["come"], begin["to"], len(parts), index, targets, counts, own + crossed, values)

    received = [send_by(partial[i], REP, o) if any(o) else partial[i] for i, o in enumerate(parts)]
    output, *messages = middle(begin["to"], index, received, weight, layer_bias, cotangent)
    messages = [send_by(messages[i], REP, o) if any(o) else messages[i] for i, o in enumerate(parts)]

    share = width // len(parts)
    share_sum = add_shares(messages, share)
    each = len(halves[0])
    across, merged = [], []
    for i, step in enumerate((None, ("xl", 1), ("z", 1), ("z", 2))):
        if step:
            index, share_sum = lax.optimization_barrier((index, share_sum))
            arriving = exchange(share_sum, *step)
        k = i % 2
        if i < 2:
            found = spread(each, begin["cross"] + each * k, begin["turn"], index, targets, counts, messages, values)
            across.append(send_by(found[0], ("core",), (1,)))
        else:
            found = spread(
                each, begin["stay"] + each * k, begin["turn"], index, targets, counts, messages, values, across[k : k + 1]
            )
            merged += found
        if step:
            _, share_sum, arriving = lax.optimization_barrier((found, share_sum, arriving))
            share_sum = share_sum + arriving
    last = [send_by(piece, CHIP, o) if any(o) else piece for piece, o in zip(merged, halves[0] + halves[1])]
    _, share_sum = lax.optimization_barrier((found, share_sum))
    share_sum = share_sum + exchange(share_sum, "core", 1)
    arriving = exchange(share_sum, "xh", 1)
    arriving, last[5] = lax.optimization_barrier((arriving, last[5]))
    total = None
    for piece in last:
        piece = piece.astype(jnp.float32)
        total = piece if total is None else total + piece
    grad_features = total.astype(jnp.bfloat16)

    norm_scale = 1.0 / math.sqrt(local_rows * math.prod(SIZES.values()))
    grad_bias = share_sum[share] * norm_scale
    pair = jnp.concatenate([share_sum[:share], arriving[:share]]).astype(jnp.bfloat16)
    pieces = [send_by(pair, ("y",), (o,)) if o else pair for o in range(y)]
    grad_weight = place(begin["piece"], len(parts), index, pieces, share, norm_scale)
    return (output, grad_features, grad_weight, grad_bias)


def solution(mesh):
    fine = Mesh(np.asarray(mesh.devices).reshape(tuple(SIZES.values())), tuple(SIZES))
    placed = (
        P(ALL, None),
        P(),
        P(),
        P(BLK, REP, None, None, None, None),
        P(BLK, REP, None, None),
        P(BLK, REP, None),
        P(ALL, None),
    )
    return jax.shard_map(
        body,
        mesh=fine,
        in_specs=placed,
        out_specs=(P(ALL, None), P(ALL, None), P(), P()),
        check_vma=False,
    )
```
